512 devices in a mesh: dp: 4 (over x), ctx: 64 (over y, z), tensor: 2 (over core).
Axes of the slice: x: 4, y: 4, z: 16, core: 2. Of those that a mesh axis runs over, the one named last changes fastest.
Arguments:
- layer_in: bfloat16 [4, 8192, 2048], P('dp', 'ctx'), may hold values from -16 to 16
- out_grad: bfloat16 [4, 8192, 2048], P('dp', 'ctx'), may hold values from -6 to 6
- w_in: bfloat16 [2048, 2048], P('dp', 'tensor'), as said below
- w_out: bfloat16 [2048, 2048], P('dp', 'tensor'), as said below
- w_bc: bfloat16 [2048, 256], P('dp', 'tensor'), may hold values from -0.015625 to 0.015625
- w_dt: bfloat16 [2048, 32], P('dp', 'tensor'), may hold values from -0.125 to 0.125
- dt_bias: float32 [32], P('tensor'), may hold values from -3 to -2
- a_log: float32 [32], P('tensor')
- d_skip: float32 [32], P('tensor'), may hold values from 0.5 to 1.5
- norm_gain: float32 [2048], P('tensor'), may hold values from 0.5 to 1.5
Outputs:
- grad_in: bfloat16 [4, 8192, 2048], P('dp', 'ctx', 'tensor')
- grad_bc: float32 [2048, 256], P(('dp', 'ctx'), 'tensor')
- grad_dt: float32 [2048, 32], P(('dp', 'ctx'), 'tensor')
The draws below stay inside these ranges and needn't reach their ends.
Inputs may be any that keep to these rules, and one draw needn't show every extreme that they name: `w_in`: latent weights of order one over the square root of 2048. `w_out`: latent weights of order one over the square root of 2048.
All inputs are finite; a program needn't handle non-finite values.
Results may differ from the reference program's by a relative error of at most 0.018.
Values may be sent and summed in bfloat16 or wider, within the bound.
A program may use at most 128 MiB of HBM per device.

```python
import math
import jax
import jax.numpy as jnp
from jax import lax

D = 2048
H = 32
P_SIZE = 64
N = 128
GROUP = 256
Q = 128
BATCH = 4
SEQ = 8192
N_CTX = 64


def banded(key, row_count, col_count):
    subkeys = jax.random.split(key, 4)
    row_frac = (jnp.arange(row_count, dtype=jnp.float32) / row_count)[:, None]
    col_frac = (jnp.arange(col_count, dtype=jnp.float32) / col_count)[None, :]
    mixture = 0.8 * row_frac + 0.2 * col_frac
    base_scale = 1.7
    small_top = 0.2
    large_low = 0.7
    large_top = 1.3
    zero_share = 0.95 - 0.94 * mixture
    small_mag = jax.random.uniform(subkeys[0], (row_count, col_count), jnp.float32) * small_top
    large_mag = large_low + jax.random.uniform(subkeys[1], (row_count, col_count), jnp.float32) * (large_top - large_low)
    zero_pick = jax.random.uniform(subkeys[2], (row_count, col_count), jnp.float32) < zero_share
    sign_flip = jax.random.uniform(subkeys[3], (row_count, col_count), jnp.float32) < 0.5
    magnitude = jnp.where(zero_pick, small_mag, large_mag) * base_scale * D ** (-0.5)
    return jnp.where(sign_flip, -magnitude, magnitude).astype(jnp.float32)


def draw_w_in(key, part):
    return banded(jax.random.fold_in(key, 11), D, H * P_SIZE).astype(jnp.bfloat16)


def draw_w_out(key, part):
    return banded(jax.random.fold_in(key, 23), D, H * P_SIZE).astype(jnp.bfloat16)


def draw_a_log(key, part):
    subkeys = jax.random.split(jax.random.fold_in(key, 37), 3)
    slow_share = 0.5
    slow_pick = jax.random.uniform(subkeys[0], (H,), jnp.float32) < slow_share
    fast_rate = jnp.exp(jax.random.uniform(subkeys[1], (H,), jnp.float32, math.log(0.15), math.log(0.5)))
    slow_rate = jax.random.uniform(subkeys[2], (H,), jnp.float32, 0.2, 1.0) * 12.5 / SEQ
    return jnp.log(jnp.where(slow_pick, slow_rate, fast_rate)).astype(jnp.float32)


def strengthened(drawn, rng, source, target, parts, factor):
    owner, partner = [(jnp.arange(drawn.shape[dim]) // (drawn.shape[dim] // parts)).reshape([-1 if axis == dim else 1 for axis in range(drawn.ndim)]) for dim in (source, target)]
    chosen = jax.random.permutation(rng, parts)[partner]
    strong = (owner == chosen) | (owner == (partner + parts // 2) % parts)
    return jnp.where(strong, factor * drawn, drawn)


def shard_levels(rng, extent, cuts, low, top_value):
    factor_of, own = 1.0, jax.random.fold_in(rng, 6)
    for dim, shards_of in cuts:
        draws = jnp.exp(jax.random.uniform(jax.random.fold_in(own, dim), (shards_of,), jnp.float32, low / len(cuts), top_value / len(cuts)))
        factor_of = factor_of * jnp.repeat(draws, extent[dim] // shards_of).reshape([-1 if axis == dim else 1 for axis in range(len(extent))])
    return factor_of


def normal_values(rng, shape, width, most, shards=(), kind=jnp.bfloat16):
    factor_of = shard_levels(rng, shape, shards, -0.22, 0.18) if shards else 1.0
    values = jax.random.normal(rng, shape, jnp.float32) * width * factor_of
    return jnp.minimum(jnp.maximum(values, -most), most).astype(kind)


def gaussian_with(key, shape, scale, most, cuts, heavy, kind=jnp.bfloat16):
    values = scale * jax.random.normal(key, shape, jnp.float32)
    if cuts:
        values = values * shard_levels(key, shape, cuts, -0.22, 0.18)
    return jnp.clip(strengthened(values, jax.random.fold_in(key, 3), *heavy), -most, most).astype(kind)


def setup_inputs(seed: int = 0) -> dict:
    splits = jax.random.split(jax.random.key(seed), 11)
    layer_in = gaussian_with(splits[0], (BATCH, SEQ, D), 1.0, 16.0, ((0, 4), (1, 64)), (1, 2, 64, 4.0))
    out_grad = normal_values(splits[1], (BATCH, SEQ, D), 1.0, 6.0, ((0, 4), (1, 64)))
    w_in = draw_w_in(jax.random.fold_in(splits[10], 71), 0)
    w_out = draw_w_out(jax.random.fold_in(splits[10], 71), 0)
    w_bc = normal_values(splits[4], (D, 2 * N), (70 * D) ** -0.5, 0.015625, ((0, 4), (1, 2)))
    w_dt = normal_values(splits[5], (D, H), D ** -0.5, 0.125, ((0, 4), (1, 2)))
    dt_bias = jnp.clip(-3.0 + 1.0 * jax.random.uniform(splits[6], (H,), jnp.float32) ** shard_levels(splits[6], (H,), ((0, 2),), -0.2, 0.2), -3.0, -2.0)
    a_log = draw_a_log(jax.random.fold_in(splits[10], 71), 0)
    d_skip = jnp.clip(0.5 + 1.0 * jax.random.uniform(splits[8], (H,), jnp.float32) ** shard_levels(splits[8], (H,), ((0, 2),), -0.2, 0.2), 0.5, 1.5)
    norm_gain = jnp.clip(1.0 + 0.1 * jax.random.normal(splits[9], (H * P_SIZE,), jnp.float32), 0.5, 1.5)
    return {"layer_in": layer_in, "out_grad": out_grad, "w_in": w_in, "w_out": w_out, "w_bc": w_bc, "w_dt": w_dt, "dt_bias": dt_bias, "a_log": a_log, "d_skip": d_skip, "norm_gain": norm_gain}


def product_of(spec, left, right):
    return jnp.einsum(spec, left.astype(jnp.float32), right.astype(jnp.float32), precision=lax.Precision.HIGHEST)

def ternary(weights, scale):
    magnitude = jnp.abs(weights.astype(jnp.float32))
    sign_of = jnp.sign(weights.astype(jnp.float32))
    return jnp.where(magnitude > 0.5 * scale, sign_of, 0.0).astype(jnp.bfloat16)

def local_block(values, b_proj, step_size, decay_rate):
    cumulative = jnp.cumsum(step_size * decay_rate[None, None, :], axis=1)
    block_log = cumulative[:, -1, :]
    weight = jnp.exp(block_log[:, None, :] - cumulative) * step_size
    weighted = (values.astype(jnp.float32) * weight[..., None]).astype(jnp.bfloat16)
    local_state = product_of('bjhp,bjn->bhpn', weighted, b_proj)
    return (cumulative, block_log, weight, weighted, local_state)

def block_output(values, b_proj, c_proj, step_size, cumulative, entering, skip_gain):
    length = cumulative.shape[1]
    gram_matrix = product_of('bin,bjn->bij', c_proj, b_proj)
    row_index = lax.broadcasted_iota(jnp.int32, (length, length), 0)
    col_index = lax.broadcasted_iota(jnp.int32, (length, length), 1)
    causal = row_index >= col_index
    cum_heads = jnp.transpose(cumulative, (0, 2, 1))
    decay_mask = jnp.exp(jnp.where(causal, cum_heads[:, :, :, None] - cum_heads[:, :, None, :], -jnp.inf))
    step_heads = jnp.transpose(step_size, (0, 2, 1))
    full_kernel = gram_matrix[:, None, :, :] * decay_mask * step_heads[:, :, None, :]
    kernel_bf = full_kernel.astype(jnp.bfloat16)
    intra_out = product_of('bhij,bjhp->bihp', kernel_bf, values)
    held_state = entering.astype(jnp.bfloat16)
    growth = jnp.exp(cumulative)
    inter_out = growth[..., None] * product_of('bin,bhpn->bihp', c_proj, held_state)
    output = intra_out + inter_out + skip_gain[None, None, :, None] * values.astype(jnp.float32)
    return (output, (decay_mask, full_kernel, kernel_bf, held_state, growth, inter_out))

def norm_grad(output, grad_normed, norm_gain):
    batch_rows, length = (output.shape[0], output.shape[1])
    grouped = output.reshape(batch_rows, length, -1, GROUP)
    inverse = lax.rsqrt(lax.optimization_barrier(jnp.mean(grouped * grouped, axis=-1, keepdims=True)) + 1e-05)
    scaled = (grad_normed * norm_gain).reshape(grouped.shape)
    result = inverse * (scaled - grouped * inverse * inverse * lax.optimization_barrier(jnp.mean(scaled * grouped, axis=-1, keepdims=True)))
    return result.reshape(output.shape)

def chain_term(grad_y, c_proj, growth):
    grad_grown = (grad_y * growth[..., None]).astype(jnp.bfloat16)
    return (grad_grown, product_of('bihp,bin->bhpn', grad_grown, c_proj))

def block_grads(values, b_proj, c_proj, step_size, decay_rate, cumulative, block_log, weight, weighted, saved, entering, skip_gain, grad_y, grad_grown, leaving):
    decay_mask, full_kernel, kernel_bf, held_state, growth, inter_out = saved
    grad_bf = grad_y.astype(jnp.bfloat16)
    leaving_bf = leaving.astype(jnp.bfloat16)
    grad_kernel = product_of('bihp,bjhp->bhij', grad_bf, values)
    from_intra = product_of('bhij,bihp->bjhp', kernel_bf, grad_bf)
    grad_weighted = product_of('bjn,bhpn->bjhp', b_proj, leaving_bf)
    grad_values = from_intra + grad_weighted * weight[..., None] + skip_gain[None, None, :, None] * grad_y
    grad_weight = lax.optimization_barrier(jnp.sum(grad_weighted * values.astype(jnp.float32), axis=-1))
    step_heads = jnp.transpose(step_size, (0, 2, 1))
    z_bf = (grad_kernel * decay_mask * step_heads[:, :, None, :]).astype(jnp.bfloat16)
    grad_c = product_of('bhij,bjn->bin', z_bf, b_proj) + product_of('bihp,bhpn->bin', grad_grown, held_state)
    grad_b = product_of('bhij,bin->bjn', z_bf, c_proj) + product_of('bjhp,bhpn->bjn', weighted, leaving_bf)
    product = grad_kernel * full_kernel
    row_sums = lax.optimization_barrier(jnp.sum(product, axis=3))
    col_sums = lax.optimization_barrier(jnp.sum(product, axis=2))
    grad_cum = lax.optimization_barrier(jnp.sum(grad_y * inter_out, axis=-1)) + jnp.transpose(row_sums - col_sums, (0, 2, 1)) - grad_weight * weight
    grad_step = jnp.transpose(col_sums, (0, 2, 1)) / step_size + grad_weight * jnp.exp(block_log[:, None, :] - cumulative)
    grad_log = lax.optimization_barrier(jnp.sum(grad_weight * weight, axis=1)) + jnp.exp(block_log) * lax.optimization_barrier(jnp.sum(leaving * entering, axis=(2, 3)))
    length = cumulative.shape[1]
    final_row = lax.broadcasted_iota(jnp.int32, (1, length, 1), 1) == length - 1
    grad_cum = grad_cum + jnp.where(final_row, grad_log[:, None, :], 0.0)
    grad_rate = lax.cumsum(grad_cum, axis=1, reverse=True)
    grad_step = grad_step + grad_rate * decay_rate[None, None, :]
    return (grad_values, jnp.concatenate([grad_b, grad_c], axis=-1), grad_step)

def reference(layer_in, out_grad, w_in, w_out, w_bc, w_dt, dt_bias, a_log, d_skip, norm_gain):
    entries = w_in.shape[0] * w_in.shape[1]
    scale_in = jnp.sum(jnp.abs(w_in.astype(jnp.float32))) / entries
    scale_out = jnp.sum(jnp.abs(w_out.astype(jnp.float32))) / entries
    codes_in = ternary(w_in, scale_in)
    codes_out = ternary(w_out, scale_out)
    decay_rate = -jnp.exp(a_log)
    heads = a_log.shape[0]
    head_size = w_in.shape[1] // heads
    state_size = w_bc.shape[1] // 2
    norm_rows = (BATCH * SEQ) ** (-0.5)

    def block_inputs(index):
        start = (index * Q).astype(jnp.int32)
        piece = lax.dynamic_slice_in_dim(layer_in, start, Q, 1)
        grad_piece = lax.dynamic_slice_in_dim(out_grad, start, Q, 1)
        pre_act = scale_in * product_of('bld,de->ble', piece, codes_in)
        values = jax.nn.silu(pre_act).astype(jnp.bfloat16).reshape(BATCH, Q, heads, head_size)
        both_bc = product_of('bld,dn->bln', piece, w_bc).astype(jnp.bfloat16)
        raw_step = product_of('bld,dh->blh', piece, w_dt) + dt_bias
        step_size = jax.nn.softplus(raw_step)
        return (piece, grad_piece, pre_act, values, both_bc[:, :, :state_size], both_bc[:, :, state_size:], raw_step, step_size)

    def forward_step(carry, index):
        piece, grad_piece, pre_act, values, b_proj, c_proj, raw_step, step_size = block_inputs(index)
        cumulative, block_log, weight, weighted, local_state = local_block(values, b_proj, step_size, decay_rate)
        return (jnp.exp(block_log)[:, :, None, None] * carry + local_state, carry)
    zero_state = jnp.zeros((BATCH, heads, head_size, state_size), jnp.float32)
    block_ids = jnp.arange(N_CTX, dtype=jnp.int32)
    last_state, entering_all = lax.scan(forward_step, zero_state, block_ids)

    def backward_step(carry, inputs):
        index, entering = inputs
        leaving, sum_bc, sum_dt = carry
        piece, grad_piece, pre_act, values, b_proj, c_proj, raw_step, step_size = block_inputs(index)
        cumulative, block_log, weight, weighted, local_state = local_block(values, b_proj, step_size, decay_rate)
        output, saved = block_output(values, b_proj, c_proj, step_size, cumulative, entering, d_skip)
        normed_grad = scale_out * product_of('bld,de->ble', grad_piece, codes_out)
        grad_y = norm_grad(output, normed_grad, norm_gain)
        grad_grown, term = chain_term(grad_y, c_proj, saved[4])
        grad_values, grad_bcx, grad_step = block_grads(values, b_proj, c_proj, step_size, decay_rate, cumulative, block_log, weight, weighted, saved, entering, d_skip, grad_y, grad_grown, leaving)
        grad_raw = grad_step * jax.nn.sigmoid(raw_step)
        sigmoid_pre = jax.nn.sigmoid(pre_act)
        grad_pre = grad_values.reshape(pre_act.shape) * sigmoid_pre * (1.0 + pre_act * (1.0 - sigmoid_pre))
        send_in = (scale_in * grad_pre).astype(jnp.bfloat16)
        send_bc = grad_bcx.astype(jnp.bfloat16)
        send_dt = grad_raw.astype(jnp.bfloat16)
        grad_piece_in = product_of('ble,de->bld', send_in, codes_in) + product_of('bln,dn->bld', send_bc, w_bc) + product_of('blh,dh->bld', send_dt, w_dt)
        term_bc = product_of('bld,bln->dn', piece, send_bc) * norm_rows
        term_dt = product_of('bld,blh->dh', piece, send_dt) * norm_rows
        new_leaving = jnp.exp(block_log)[:, :, None, None] * leaving + term
        return ((new_leaving, sum_bc + term_bc, sum_dt + term_dt), grad_piece_in.astype(jnp.bfloat16))
    start_carry = (zero_state, jnp.zeros(w_bc.shape, jnp.float32), jnp.zeros(w_dt.shape, jnp.float32))
    final_carry, pieces = lax.scan(backward_step, start_carry, (block_ids, entering_all), reverse=True)
    grad_in = jnp.transpose(pieces, (1, 0, 2, 3)).reshape(BATCH, SEQ, -1)
    return (grad_in, final_carry[1], final_carry[2])
```

```python
import functools

import jax
import jax.numpy as jnp
from jax import lax
from jax.experimental import pallas as pl
from jax.experimental.pallas import tpu as pltpu
from jax.sharding import PartitionSpec as P

GROUP = 256
MESH = pl.DeviceIdType.MESH
F32 = jnp.float32
BF16 = jnp.bfloat16
EXACT = lax.Precision.HIGHEST


def dot(a, b, ca=1, cb=0, precision=None):
    return lax.dot_general(
        a, b, (((ca,), (cb,)), ((), ())), precision=precision, preferred_element_type=F32
    )


def layer_kernel(
    nx,
    ny,
    nz,
    x_ref,
    g_ref,
    win_ref,
    wout_ref,
    wsm_ref,
    vec_ref,
    gin_out,
    gbc_out,
    gdt_out,
    win_all,
    wout_all,
    wsm_all,
    codes_in,
    sums_own,
    sums_all,
    bc_own,
    bc,
    log_own,
    logs,
    loc_own,
    loc_all,
    ent_own,
    held,
    term_own,
    term_all,
    lea_own,
    leav,
    fwd_own,
    fwd_all,
    bwd_own,
    bwd_all,
    x_all,
    send_own,
    send_all,
    yg_own,
    yg_all,
    zg_own,
    zg_all,
    half_own,
    half_in,
    part_own,
    part_in,
    pre,
    values,
    weighted,
    cumt,
    stept,
    kern,
    zmask,
    intra,
    ngrad,
    gbf,
    ggrown,
    rowsum,
    colt,
    fromintra,
    dec,
    ring_s,
    ring_r,
    grp_s,
    grp_r,
    core_s,
    core_r,
    z_s,
    z_r,
    y_s,
    y_r,
    x_s,
    x_r,
    loc_s,
):
    q, depth = x_ref.shape
    rows, units = win_ref.shape
    heads = nz
    width = units // heads
    nstate = bc.shape[2]
    ix = lax.axis_index("dp")
    ic = lax.axis_index("ctx")
    it = lax.axis_index("tensor")
    iz = lax.rem(ic, nz)
    iy = ic // nz
    other = 1 - it

    def dev(x=ix, y=iy, z=iz, t=it):
        return (x, y * nz + z, t)

    def remote(src, dst, ssem, rsem, device):
        return pltpu.make_async_remote_copy(
            src_ref=src,
            dst_ref=dst,
            send_sem=ssem,
            recv_sem=rsem,
            device_id=device,
            device_id_type=MESH,
        )

    def xoff(d):
        return lax.rem(ix + d, nx)

    def yoff(d):
        return lax.rem(iy + d, ny)

    def zoff(d):
        return lax.rem(iz + d, nz)

    barrier = pltpu.get_barrier_semaphore()
    count = 0
    for d in range(nx):
        for t in (it, other):
            if d == 0 and t is it:
                continue
            pl.semaphore_signal(barrier, inc=1, device_id=dev(x=xoff(d), t=t), device_id_type=MESH)
            count += 1
    for d in range(1, ny):
        pl.semaphore_signal(barrier, inc=1, device_id=dev(y=yoff(d)), device_id_type=MESH)
        count += 1

    def greet(d, carry):
        pl.semaphore_signal(barrier, inc=1, device_id=dev(z=zoff(d)), device_id_type=MESH)
        return carry

    lax.fori_loop(1, nz, greet, 0)
    count += nz - 1

    def magnitude(ref):
        def one(i, acc):
            piece = jnp.abs(ref[pl.ds(pl.multiple_of(i * 16, 16), 16), :].astype(F32))
            return acc + piece

        total = lax.fori_loop(0, rows // 16, one, jnp.zeros((16, units), F32))
        out = total[:8, :128] + total[8:, :128]
        for c in range(1, units // 128):
            out = out + total[:8, c * 128 : (c + 1) * 128] + total[8:, c * 128 : (c + 1) * 128]
        return out

    sums_own[0:8, :] = magnitude(win_ref)
    sums_own[8:16, :] = magnitude(wout_ref)
    pl.semaphore_wait(barrier, count)

    half = rows // 2
    top, low = pl.ds(0, half), pl.ds(half, half)

    class Ring:
        def __init__(self, src, dst, base):
            right, left = dev(x=xoff(1)), dev(x=xoff(nx - 1))
            own, before, after = ix, xoff(nx - 1), xoff(1)
            sems = lambda k: (ring_s.at[base + k], ring_r.at[base + k])
            self.local = pltpu.make_async_copy(src, dst.at[own], loc_s.at[base // 6])
            self.first = [
                remote(src.at[top], dst.at[own, top], *sems(0), right),
                remote(src.at[low], dst.at[own, low], *sems(1), left),
                remote(src.at[low], dst.at[own, low], *sems(2), right),
                remote(src.at[top], dst.at[own, top], *sems(3), left),
            ]
            self.relay = [
                remote(dst.at[before, top], dst.at[before, top], *sems(4), right),
                remote(dst.at[after, low], dst.at[after, low], *sems(5), left),
            ]

        def start(self):
            self.local.start()
            for c in self.first:
                c.start()

        def forward(self):
            self.first[0].wait_recv()
            self.relay[0].start()
            self.first[1].wait_recv()
            self.relay[1].start()

        def finish(self):
            self.local.wait()
            self.first[2].wait_recv()
            self.first[3].wait_recv()
            self.relay[0].wait_recv()
            self.relay[1].wait_recv()

        def drain(self):
            for c in self.first + self.relay:
                c.wait_send()

    ring_sm = Ring(wsm_ref, wsm_all, 0)
    ring_in = Ring(win_ref, win_all, 6)
    ring_out = Ring(wout_ref, wout_all, 12)

    group = []
    for d in range(nx):
        for k, t in enumerate((it, other)):
            if d == 0 and k == 0:
                continue
            group.append(
                remote(
                    sums_own,
                    sums_all.at[2 * ix + it],
                    grp_s.at[2 * d + k],
                    grp_r.at[2 * d + k],
                    dev(x=xoff(d), t=t),
                )
            )
    for c in group:
        c.start()
    sums_all[2 * ix + it] = sums_own[...]
    ring_sm.start()
    ring_in.start()
    ring_sm.forward()
    ring_in.forward()
    ring_out.start()

    ring_sm.finish()
    raw_bc = jnp.zeros((q, 2 * nstate), F32)
    for k in range(nx):
        raw_bc = raw_bc + dot(x_ref[:, k * rows : (k + 1) * rows], wsm_all[k])
    bc_own[...] = raw_bc[:, :nstate].astype(BF16)
    share_bc = remote(bc_own, bc.at[it], core_s.at[0], core_r.at[0], dev(t=other))
    share_bc.start()
    bc[it] = bc_own[...]
    raw_step = raw_bc[:, nstate:] + vec_ref[2:3, :128]
    rate = -jnp.exp(vec_ref[3:4, :128])
    step = jnp.maximum(raw_step, 0.0) + jnp.log1p(jnp.exp(-jnp.abs(raw_step)))
    ri = lax.broadcasted_iota(jnp.int32, (q, q), 0)
    ci = lax.broadcasted_iota(jnp.int32, (q, q), 1)
    causal = ri >= ci
    lower = jnp.where(causal, 1.0, 0.0).astype(F32)
    upper = jnp.where(ci >= ri, 1.0, 0.0).astype(F32)
    cum = dot(lower, step * rate, precision=EXACT)
    block_log = cum[q - 1 : q, :]
    fade = jnp.exp(block_log - cum)
    weight = fade * step
    growth = jnp.exp(cum)
    cumt[...] = cum.T
    stept[...] = step.T
    log_own[...] = block_log
    eh = lax.broadcasted_iota(jnp.int32, (128, units), 0)
    eu = lax.broadcasted_iota(jnp.int32, (128, units), 1)
    expand = jnp.where(eu // width == eh, 1.0, 0.0).astype(F32)
    weight_u = dot(weight, expand, precision=EXACT)
    growth_u = dot(growth, expand, precision=EXACT)
    skip_u = vec_ref[1:2, :]
    gain_u = vec_ref[0:1, :]

    for c in group:
        c.wait_recv()
    total = sums_all[0]
    for k in range(1, 2 * nx):
        total = total + sums_all[k]
    entries = 2.0 * nx * rows * units
    scale_in = jnp.sum(total[0:8, :]) / entries
    scale_out = jnp.sum(total[8:16, :]) / entries

    def ternary(w, scale):
        w = w.astype(F32)
        sign = jnp.where(w > 0.0, 1.0, -1.0)
        return jnp.where(jnp.abs(w) > 0.5 * scale, sign, 0.0).astype(BF16)

    ring_in.finish()
    tile = min(256, units)

    def project_in(j, carry):
        cols = pl.ds(pl.multiple_of(j * tile, tile), tile)
        acc = jnp.zeros((q, tile), F32)
        for k in range(nx):
            code = ternary(win_all[k, :, cols], scale_in)
            codes_in[k, :, cols] = code
            acc = acc + dot(x_ref[:, k * rows : (k + 1) * rows], code)
        v = scale_in * acc
        pre[:, cols] = v
        values[:, cols] = (v * lax.logistic(v)).astype(BF16)
        return carry

    lax.fori_loop(0, units // tile, project_in, 0)
    weighted[...] = (values[...].astype(F32) * weight_u).astype(BF16)
    share_bc.wait_recv()
    b_proj, c_proj = bc[0], bc[1]
    local_state = dot(weighted[...], b_proj, 0, 0)
    loc_own[...] = local_state.astype(BF16).reshape(nz, width, nstate)

    def z_exchange(own, all_, base):
        def copy(d):
            to = zoff(d)
            return remote(
                own.at[to], all_.at[iz], z_s.at[base + d], z_r.at[base + d], dev(z=to)
            )

        def start():
            def one(d, carry):
                copy(d).start()
                return carry

            lax.fori_loop(1, nz, one, 0)
            all_[iz] = own[iz]

        def wait():
            def one(d, carry):
                copy(d).wait_recv()
                return carry

            lax.fori_loop(1, nz, one, 0)

        def drain():
            def one(d, carry):
                copy(d).wait_send()
                return carry

            lax.fori_loop(1, nz, one, 0)

        return start, wait, drain

    def log_copy(d):
        return remote(
            log_own, logs.at[iz], z_s.at[5 * nz + d], z_r.at[5 * nz + d], dev(z=zoff(d))
        )

    def log_start(d, carry):
        log_copy(d).start()
        return carry

    def log_wait(d, carry):
        log_copy(d).wait_recv()
        return carry

    def log_drain(d, carry):
        log_copy(d).wait_send()
        return carry

    def y_exchange(own, all_, base):
        copies = [
            remote(own, all_.at[iy], y_s.at[base + d], y_r.at[base + d], dev(y=yoff(d)))
            for d in range(1, ny)
        ]
        for c in copies:
            c.start()
        all_[iy] = own[...]
        return copies

    drains = []
    lax.fori_loop(1, nz, log_start, 0)
    logs[iz] = log_own[...]
    start, wait_loc, drain = z_exchange(loc_own, loc_all, 0)
    drains.append(drain)
    start()

    gram = dot(c_proj, b_proj, 1, 1)
    lane = ci
    left_half = lax.broadcasted_iota(jnp.int32, (q, 2 * width), 1) < width
    zero_pair = jnp.zeros((q, 2 * width), BF16)

    def head_mask(h):
        col = jnp.sum(jnp.where(lane == h, cum, 0.0), axis=1, keepdims=True)
        row = cumt[pl.ds(h, 1), :]
        return jnp.exp(jnp.where(causal, col - row, -jnp.inf)) * stept[pl.ds(h, 1), :]

    def inside(p, carry):
        cols = pl.ds(pl.multiple_of(p * 2 * width, 2 * width), 2 * width)
        pair = values[:, cols]
        acc = jnp.zeros((q, 2 * width), F32)
        for s in range(2):
            h = 2 * p + s
            mask = head_mask(h)
            zmask[h] = mask
            kb = (gram * mask).astype(BF16)
            kern[h] = kb
            picked = jnp.where(left_half, pair, zero_pair) if s == 0 else jnp.where(left_half, zero_pair, pair)
            acc = acc + dot(kb, picked)
        intra[:, cols] = acc
        return carry

    lax.fori_loop(0, heads // 2, inside, 0)
    ring_out.forward()

    x_copies = [
        remote(
            x_ref.at[:, pl.ds(pl.multiple_of(xoff(d) * rows, rows), rows)],
            x_all.at[ix],
            x_s.at[d],
            x_r.at[d],
            dev(x=xoff(d)),
        )
        for d in range(1, nx)
    ]
    for c in x_copies:
        c.start()
    x_all[ix] = x_ref[:, pl.ds(pl.multiple_of(ix * rows, rows), rows)]

    lax.fori_loop(1, nz, log_wait, 0)
    log_rows = logs[...].reshape(nz, 128)
    lane_z = lax.broadcasted_iota(jnp.int32, (nz, 128), 1)
    log_col = jnp.sum(jnp.where(lane_z == iz, log_rows, 0.0), axis=1, keepdims=True)
    dec[...] = jnp.broadcast_to(jnp.exp(log_col), (nz, 128))
    row_decay = jnp.exp(jnp.sum(log_col))
    wait_loc()

    def fwd_total(k, s):
        return dec[pl.ds(k, 1), :] * s + loc_all[k].astype(F32)

    zero_state = jnp.zeros((width, nstate), F32)
    fwd_own[0:width, :] = lax.fori_loop(0, nz, fwd_total, zero_state)
    fwd_own[width : width + 8, :] = jnp.broadcast_to(row_decay, (8, nstate))
    y_fwd = y_exchange(fwd_own, fwd_all, 0)
    for c in y_fwd:
        c.wait_recv()
    state = zero_state
    for k in range(ny):
        grown = fwd_all[k, width : width + 1, :] * state + fwd_all[k, 0:width, :]
        state = jnp.where(k < iy, grown, state)

    def fwd_emit(k, s):
        ent_own[k] = s.astype(BF16)
        return fwd_total(k, s)

    lax.fori_loop(0, nz, fwd_emit, state)
    start, wait_ent, drain = z_exchange(ent_own, held, nz)
    drains.append(drain)
    start()

    ring_out.finish()

    def project_out(j, carry):
        cols = pl.ds(pl.multiple_of(j * tile, tile), tile)
        acc = jnp.zeros((q, tile), F32)
        for k in range(nx):
            acc = acc + dot(
                g_ref[:, k * rows : (k + 1) * rows], ternary(wout_all[k, :, cols], scale_out)
            )
        ngrad[:, cols] = scale_out * acc
        return carry

    lax.fori_loop(0, units // tile, project_out, 0)

    wait_ent()
    held_flat = held[...].reshape(units, nstate)
    inter = growth_u * dot(c_proj, held_flat, 1, 1)
    values_f = values[...].astype(F32)
    output = intra[...] + inter + skip_u * values_f
    scaled = ngrad[...] * gain_u
    pieces = []
    for g in range(units // GROUP):
        sl = slice(g * GROUP, (g + 1) * GROUP)
        o, s = output[:, sl], scaled[:, sl]
        inverse = lax.rsqrt(jnp.mean(o * o, axis=1, keepdims=True) + 1e-05)
        mixed = jnp.mean(s * o, axis=1, keepdims=True)
        pieces.append(inverse * (s - o * (inverse * inverse) * mixed))
    grad_y = jnp.concatenate(pieces, axis=1) if len(pieces) > 1 else pieces[0]
    gbf[...] = grad_y.astype(BF16)
    ggrown[...] = (grad_y * growth_u).astype(BF16)
    ngrad[...] = grad_y
    term_own[...] = dot(ggrown[...], c_proj, 0, 0).astype(BF16).reshape(nz, width, nstate)
    start, wait_term, drain = z_exchange(term_own, term_all, 2 * nz)
    drains.append(drain)
    start()

    def head_sum(v):
        return dot(v, expand, 1, 1, precision=EXACT)

    inter_sum = head_sum(grad_y * inter)

    colt[...] = jnp.zeros((128, q), F32)

    def inside_back(p, carry):
        zsum, rsum = carry
        cols = pl.ds(pl.multiple_of(p * 2 * width, 2 * width), 2 * width)
        pair = values[:, cols]
        gpair = gbf[:, cols]
        acc = jnp.zeros((q, 2 * width), F32)
        for s in range(2):
            h = 2 * p + s
            picked = jnp.where(left_half, gpair, zero_pair) if s == 0 else jnp.where(left_half, zero_pair, gpair)
            gk = dot(picked, pair, 1, 1)
            z = gk * zmask[h]
            zsum = zsum + z
            product = z * gram
            rs = jnp.sum(product, axis=1, keepdims=True)
            rsum = jnp.where(lane == h, rs, rsum)
            colt[pl.ds(h, 1), :] = jnp.sum(product, axis=0, keepdims=True)
            acc = acc + dot(kern[h], picked, 0, 0)
        fromintra[:, cols] = acc
        return (zsum, rsum)

    zero_q = jnp.zeros((q, q), F32)
    zsum, row_sums = lax.fori_loop(0, heads // 2, inside_back, (zero_q, zero_q))
    col_sums = colt[...].T
    zsum = zsum.astype(BF16)
    grad_c = dot(zsum, b_proj) + dot(ggrown[...], held_flat)
    grad_b0 = dot(zsum, c_proj, 0, 0)

    wait_term()

    def bwd_total(i, s):
        k = nz - 1 - i
        return dec[pl.ds(k, 1), :] * s + term_all[k].astype(F32)

    bwd_own[0:width, :] = lax.fori_loop(0, nz, bwd_total, zero_state)
    bwd_own[width : width + 8, :] = jnp.broadcast_to(row_decay, (8, nstate))
    y_bwd = y_exchange(bwd_own, bwd_all, ny)
    for c in y_bwd:
        c.wait_recv()
    state = zero_state
    for k in range(ny - 1, -1, -1):
        grown = bwd_all[k, width : width + 1, :] * state + bwd_all[k, 0:width, :]
        state = jnp.where(k > iy, grown, state)

    def bwd_emit(i, s):
        k = nz - 1 - i
        lea_own[k] = s.astype(BF16)
        return bwd_total(i, s)

    lax.fori_loop(0, nz, bwd_emit, state)
    start, wait_lea, drain = z_exchange(lea_own, leav, 3 * nz)
    drains.append(drain)
    start()
    wait_lea()
    leav_flat = leav[...].reshape(units, nstate)

    grad_b = grad_b0 + dot(weighted[...], leav_flat)
    mine = jnp.where(it == 0, grad_b, grad_c)
    half_own[...] = jnp.where(it == 0, grad_c, grad_b).astype(BF16)
    share_half = remote(half_own, half_in, core_s.at[1], core_r.at[1], dev(t=other))
    share_half.start()

    grad_weighted = dot(b_proj, leav_flat, 1, 1)
    grad_weight = head_sum(grad_weighted * values_f)
    both = leav_flat.astype(F32) * held_flat.astype(F32)
    state_rows = dot(jnp.ones((8, nstate), F32), both, 1, 1, precision=EXACT)
    state_dot = head_sum(state_rows)[0:1, :]
    gw_w = grad_weight * weight
    grad_log = jnp.sum(gw_w, axis=0, keepdims=True) + jnp.exp(block_log) * state_dot
    grad_cum = inter_sum + row_sums - col_sums - gw_w
    grad_cum = grad_cum + jnp.where(ri == q - 1, grad_log, 0.0)
    grad_rate = dot(upper, grad_cum, precision=EXACT)
    grad_step = col_sums / step + grad_weight * fade + rate * grad_rate
    send_dt = (grad_step * lax.logistic(raw_step)).astype(BF16)

    share_half.wait_recv()
    send_bc = (mine + half_in[...].astype(F32)).astype(BF16)
    send_own[:, :nstate] = send_bc
    send_own[:, nstate:] = jnp.where(lane < heads, send_dt.astype(F32), 0.0).astype(BF16)
    s_copies = [
        remote(send_own, send_all.at[ix], x_s.at[nx + d], x_r.at[nx + d], dev(x=xoff(d)))
        for d in range(1, nx)
    ]
    for c in s_copies:
        c.start()
    send_all[ix] = send_own[...]

    grad_values = fromintra[...] + grad_weighted * weight_u + skip_u * ngrad[...]
    v = pre[...]
    sg = lax.logistic(v)
    send_in = (scale_in * (grad_values * sg * (1.0 + v * (1.0 - sg)))).astype(BF16)
    gbf[...] = send_in

    for c in x_copies + s_copies:
        c.wait_recv()
    grad_w = jnp.zeros((rows, 2 * nstate), F32)
    for k in range(nx):
        grad_w = grad_w + dot(x_all[k], send_all[k], 0, 0)
    yrows = rows // ny
    yg_own[...] = grad_w.astype(BF16).reshape(ny, yrows, 2 * nstate)
    yg_copies = [
        remote(
            yg_own.at[yoff(d)], yg_all.at[iy], y_s.at[2 * ny + d], y_r.at[2 * ny + d], dev(y=yoff(d))
        )
        for d in range(1, ny)
    ]
    for c in yg_copies:
        c.start()
    yg_all[iy] = yg_own[iy]

    def partial_in(k):
        rowsum = dot(gbf[...], codes_in[k], 1, 1)
        return rowsum + dot(send_own[...], wsm_all[k], 1, 1)

    per = nx // 2 if nx > 1 else 1
    wide = rows if nx > 1 else rows // 2

    def piece_of(side, j):
        if nx > 1:
            return partial_in(side * per + j)
        w = pl.ds(pl.multiple_of(side * wide, wide), wide)
        return dot(gbf[...], codes_in[0, w, :], 1, 1) + dot(send_own[...], wsm_all[0, w, :], 1, 1)

    for j in range(per):
        part_own[:, j * wide : (j + 1) * wide] = piece_of(other, j).astype(BF16)
    share_part = remote(part_own, part_in, core_s.at[2], core_r.at[2], dev(t=other))
    share_part.start()

    for c in yg_copies:
        c.wait_recv()
    ysum = yg_all[0].astype(F32)
    for k in range(1, ny):
        ysum = ysum + yg_all[k].astype(F32)
    few = yrows // nz
    for k in range(nz):
        block = ysum[k * few : (k + 1) * few, :]
        zg_own[k] = jnp.concatenate([block[:, :nstate], block[:, nstate:]], axis=0).astype(BF16)
    start, wait_zg, drain = z_exchange(zg_own, zg_all, 4 * nz)
    drains.append(drain)
    start()

    share_part.wait_recv()
    for j in range(per):
        sl = slice(j * wide, (j + 1) * wide)
        gin_out[:, sl] = (piece_of(it, j) + part_in[:, sl].astype(F32)).astype(BF16)

    wait_zg()
    zsum_all = zg_all[0].astype(F32)
    for k in range(1, nz):
        zsum_all = zsum_all + zg_all[k].astype(F32)
    norm = (q * nx * ny * nz) ** -0.5
    gbc_out[...] = zsum_all[:few, :] * norm
    gdt_out[...] = zsum_all[few:, :heads] * norm

    for ring in (ring_sm, ring_in, ring_out):
        ring.drain()
    for c in group + [share_bc, share_half, share_part]:
        c.wait_send()
    for c in y_fwd + y_bwd + yg_copies + x_copies + s_copies:
        c.wait_send()
    for drain in drains:
        drain()
    lax.fori_loop(1, nz, log_drain, 0)


def shards(mesh_shape, layer_in, out_grad, w_in, w_out, w_bc, w_dt, dt_bias, a_log, d_skip, norm_gain):
    nx, nc = mesh_shape
    heads = a_log.shape[0]
    nz = heads
    ny = nc // nz
    q, depth = layer_in.shape[1:]
    rows, units = w_in.shape
    nstate = w_bc.shape[1]
    width = units // heads
    yrows = rows // ny
    few = yrows // nz
    w_small = jnp.concatenate(
        [w_bc, w_dt, jnp.zeros((rows, 128 - heads), BF16)], axis=1
    )
    flat = lambda v: jnp.pad(v, (0, units - v.shape[0]))[None, :]
    vec = jnp.concatenate(
        [
            norm_gain[None, :],
            jnp.repeat(d_skip, width)[None, :],
            flat(dt_bias),
            flat(a_log),
            jnp.zeros((4, units), F32),
        ],
        axis=0,
    )
    V = pltpu.VMEM
    dma = pltpu.SemaphoreType.DMA
    state = (nz, width, nstate)
    scratch = [
        V((nx, rows, units), BF16),
        V((nx, rows, units), BF16),
        V((nx, rows, 2 * nstate), BF16),
        V((nx, rows, units), BF16),
        V((16, 128), F32),
        V((2 * nx, 16, 128), F32),
        V((q, nstate), BF16),
        V((2, q, nstate), BF16),
        V((1, 128), F32),
        V((nz, 1, 128), F32),
        V(state, BF16),
        V(state, BF16),
        V(state, BF16),
        V(state, BF16),
        V(state, BF16),
        V(state, BF16),
        V(state, BF16),
        V(state, BF16),
        V((width + 8, nstate), F32),
        V((ny, width + 8, nstate), F32),
        V((width + 8, nstate), F32),
        V((ny, width + 8, nstate), F32),
        V((nx, q, rows), BF16),
        V((q, 2 * nstate), BF16),
        V((nx, q, 2 * nstate), BF16),
        V((ny, yrows, 2 * nstate), BF16),
        V((ny, yrows, 2 * nstate), BF16),
        V((nz, 2 * few, nstate), BF16),
        V((nz, 2 * few, nstate), BF16),
        V((q, nstate), BF16),
        V((q, nstate), BF16),
        V((q, depth // 2), BF16),
        V((q, depth // 2), BF16),
        V((q, units), F32),
        V((q, units), BF16),
        V((q, units), BF16),
        V((128, q), F32),
        V((128, q), F32),
        V((heads, q, q), BF16),
        V((heads, q, q), F32),
        V((q, units), F32),
        V((q, units), F32),
        V((q, units), BF16),
        V((q, units), BF16),
        V((q, 128), F32),
        V((128, q), F32),
        V((q, units), F32),
        V((nz, 128), F32),
        dma((18,)),
        dma((18,)),
        dma((2 * nx,)),
        dma((2 * nx,)),
        dma((3,)),
        dma((3,)),
        dma((6 * nz,)),
        dma((6 * nz,)),
        dma((3 * ny,)),
        dma((3 * ny,)),
        dma((2 * nx,)),
        dma((2 * nx,)),
        dma((3,)),
    ]
    vm = pl.BlockSpec(memory_space=pltpu.VMEM)
    grad_in, grad_bc, grad_dt = pl.pallas_call(
        functools.partial(layer_kernel, nx, ny, nz),
        out_shape=(
            jax.ShapeDtypeStruct((q, depth // 2), BF16),
            jax.ShapeDtypeStruct((few, nstate), F32),
            jax.ShapeDtypeStruct((few, heads), F32),
        ),
        in_specs=[vm] * 6,
        out_specs=(vm, vm, vm),
        scratch_shapes=scratch,
        compiler_params=pltpu.CompilerParams(
            collective_id=0, has_side_effects=True, vmem_limit_bytes=60 * 1024 * 1024
        ),
        name="ternary_layer",
    )(layer_in[0], out_grad[0], w_in, w_out, w_small, vec)
    return (grad_in[None], grad_bc, grad_dt)


def solution(mesh):
    in_specs = (
        P("dp", "ctx", None),
        P("dp", "ctx", None),
        P("dp", "tensor"),
        P("dp", "tensor"),
        P("dp", "tensor"),
        P("dp", "tensor"),
        P("tensor"),
        P("tensor"),
        P("tensor"),
        P("tensor"),
    )
    out_specs = (P("dp", "ctx", "tensor"), P(("dp", "ctx"), "tensor"), P(("dp", "ctx"), "tensor"))
    body = functools.partial(shards, (mesh.shape["dp"], mesh.shape["ctx"]))
    return jax.shard_map(body, mesh=mesh, in_specs=in_specs, out_specs=out_specs, check_vma=False)
```

```python
import functools
import types

import jax
import jax.numpy as jnp
from jax import lax
from jax.experimental import pallas as pl
from jax.experimental.pallas import tpu as pltpu
from jax.sharding import PartitionSpec as P

GROUP = 256
MESH = pl.DeviceIdType.MESH
F32 = jnp.float32
BF16 = jnp.bfloat16
EXACT = lax.Precision.HIGHEST


def dot(a, b, ca=1, cb=0, precision=None):
    return lax.dot_general(
        a, b, (((ca,), (cb,)), ((), ())), precision=precision, preferred_element_type=F32
    )


NAMES = [
    "x", "g", "win", "wout", "wbc", "wdt", "vec", "gin",
    "gbc", "gdt", "win_all", "wout_all", "wbc_all", "wdt_all", "codes", "sums_own",
    "sums_all", "bc_own", "bc", "log_own", "logs", "loc_own", "loc_all", "ent_own",
    "held", "term_own", "term_all", "lea_own", "leav", "fwd_own", "fwd_all", "bwd_own",
    "bwd_all", "x_all", "sbc_own", "sbc_all", "sdt_own", "sdt_all", "ybc_own", "ybc_all",
    "ydt_own", "ydt_all", "zg_own", "zg_all", "half_own", "half_in", "part_own", "part_in",
    "part_own_f", "pre", "values", "weighted", "weight_u", "growth_u", "cumt", "stept",
    "kern", "zmask", "intra", "grad", "gbf", "ggrown", "iprod", "colt",
    "fromintra", "dec", "w_s", "w_r", "grp_s", "grp_r", "core_s", "core_r",
    "z_s", "z_r", "y_s", "y_r", "x_s", "x_r", "loc_s",
]


def far_first(n):
    return sorted(range(1, n), key=lambda d: -min(d, n - d))


def layer_kernel(nx, ny, nz, straight, *refs):
    R = types.SimpleNamespace(**dict(zip(NAMES, refs, strict=True)))
    q, depth = R.x.shape
    rows, units = R.win.shape
    heads = nz
    width = units // heads
    nstate = R.wbc.shape[1]
    tile = min(256, units)
    ntile = units // tile
    hpt = tile // width
    ix = lax.axis_index("dp")
    ic = lax.axis_index("ctx")
    it = lax.axis_index("tensor")
    iz = lax.rem(ic, nz)
    iy = ic // nz
    other = 1 - it

    def dev(x=ix, y=iy, z=iz, t=it):
        return (x, y * nz + z, t)

    def remote(src, dst, ssem, rsem, device):
        return pltpu.make_async_remote_copy(
            src_ref=src,
            dst_ref=dst,
            send_sem=ssem,
            recv_sem=rsem,
            device_id=device,
            device_id_type=MESH,
        )

    def xoff(d):
        return lax.rem(ix + d, nx)

    def yoff(d):
        return lax.rem(iy + d, ny)

    def zoff(d):
        return lax.rem(iz + d, nz)

    barrier = pltpu.get_barrier_semaphore()
    count = 0

    def greet(d, carry):
        pl.semaphore_signal(barrier, inc=1, device_id=dev(z=zoff(d)), device_id_type=MESH)
        return carry

    lax.fori_loop(1, nz, greet, 0)
    count += nz - 1
    for d in range(nx):
        for t in (it, other):
            if d == 0 and t is it:
                continue
            pl.semaphore_signal(barrier, inc=1, device_id=dev(x=xoff(d), t=t), device_id_type=MESH)
            count += 1
    for d in range(1, ny):
        pl.semaphore_signal(barrier, inc=1, device_id=dev(y=yoff(d)), device_id_type=MESH)
        count += 1

    def magnitude(ref):
        def one(i, acc):
            piece = jnp.abs(ref[pl.ds(pl.multiple_of(i * 16, 16), 16), :].astype(F32))
            return acc + piece

        total = lax.fori_loop(0, rows // 16, one, jnp.zeros((16, units), F32))
        out = total[:8, :128] + total[8:, :128]
        for c in range(1, units // 128):
            out = out + total[:8, c * 128 : (c + 1) * 128] + total[8:, c * 128 : (c + 1) * 128]
        return out

    R.sums_own[0:8, :] = magnitude(R.win)
    R.sums_own[8:16, :] = magnitude(R.wout)
    for k in range(nx):
        R.wdt_all[k, heads:, :] = jnp.zeros((128 - heads, rows), BF16)
    pl.semaphore_wait(barrier, count)

    links = [0]
    every = []

    def link(src, dst, device):
        k = links[0]
        links[0] += 1
        c = remote(src, dst, R.w_s.at[k], R.w_r.at[k], device)
        every.append(c)
        return c

    class Ring:
        def __init__(self, n, own, place, before, after, right, left):
            self.relay = []
            if n == 2:
                self.first = [link(own(c), place(c), right) for c in range(2)]
                return
            self.first = [
                link(own(0), place(0), right),
                link(own(1), place(1), left),
                link(own(1), place(1), right),
                link(own(0), place(0), left),
            ]
            self.relay = [
                link(before(0), before(0), right),
                link(after(1), after(1), left),
            ]

        def start(self):
            for c in self.first:
                c.start()

        def forward(self):
            for k, c in enumerate(self.relay):
                self.first[k].wait_recv()
                c.start()

        def neighbours(self):
            for c in self.first[2:] if self.relay else self.first:
                c.wait_recv()

        def opposite(self):
            for c in self.relay:
                c.wait_recv()

    def x_ring(view, dst):
        return Ring(
            nx,
            lambda c: view(None, c),
            lambda c: view(dst.at[ix], c),
            lambda c: view(dst.at[xoff(nx - 1)], c),
            lambda c: view(dst.at[xoff(1)], c),
            dev(x=xoff(1)),
            dev(x=xoff(nx - 1)),
        )

    half_units = units // 2

    class Gather:
        def __init__(self, src, dst, k):
            share = (rows - straight) // ny

            def part(first, count):
                def view(ref, c):
                    ref = src if ref is None else ref
                    return ref.at[pl.ds(first, count), pl.ds(c * half_units, half_units)]

                return view

            def quarter(y):
                return part(pl.multiple_of(straight + y * share, 8), share)

            self.xb = x_ring(quarter(iy), dst)
            self.xa = x_ring(part(0, straight), dst)
            self.y = []
            for slot in (xoff(nx - 1), xoff(1), xoff(2)):
                at = dst.at[slot]
                mine = quarter(iy)
                self.y.append(
                    Ring(
                        ny,
                        lambda c, at=at: mine(at, c),
                        lambda c, at=at: mine(at, c),
                        lambda c, at=at: quarter(yoff(ny - 1))(at, c),
                        lambda c, at=at: quarter(yoff(1))(at, c),
                        dev(y=yoff(1)),
                        dev(y=yoff(ny - 1)),
                    )
                )
            self.local = pltpu.make_async_copy(src, dst.at[ix], R.loc_s.at[k])

        def finish(self):
            self.xa.neighbours()
            self.xa.opposite()
            for ring in self.y:
                ring.neighbours()
                ring.opposite()
            self.local.wait()

    by_rows = rows // 2
    ring_bc = x_ring(
        lambda ref, c: (R.wbc if ref is None else ref).at[pl.ds(c * by_rows, by_rows), :], R.wbc_all
    )
    ring_dt = x_ring(
        lambda ref, c: (
            R.wdt.at[:, pl.ds(c * by_rows, by_rows)]
            if ref is None
            else ref.at[pl.ds(0, heads), pl.ds(c * by_rows, by_rows)]
        ),
        R.wdt_all,
    )
    into = Gather(R.win, R.win_all, 0)
    outof = Gather(R.wout, R.wout_all, 1)

    group = []
    for d in range(nx):
        for k, t in enumerate((it, other)):
            if d == 0 and k == 0:
                continue
            group.append(
                remote(
                    R.sums_own,
                    R.sums_all.at[2 * ix + it],
                    R.grp_s.at[2 * d + k],
                    R.grp_r.at[2 * d + k],
                    dev(x=xoff(d), t=t),
                )
            )

    into.xb.start()
    ring_bc.start()
    ring_dt.start()
    for c in group:
        c.start()
    into.local.start()
    outof.local.start()
    R.sums_all[2 * ix + it] = R.sums_own[...]
    R.wbc_all[ix] = R.wbc[...]
    R.wdt_all[ix, 0:heads, :] = R.wdt[...]
    into.xb.forward()
    into.xa.start()
    into.xb.neighbours()
    into.y[0].start()
    into.y[1].start()
    ring_bc.forward()
    ring_dt.forward()
    into.xb.opposite()
    into.y[2].start()
    into.y[0].forward()
    into.xa.forward()
    into.y[1].forward()

    for ring in (ring_bc, ring_dt):
        ring.neighbours()
        ring.opposite()
    half_bc = jnp.zeros((q, nstate), F32)
    raw_step = jnp.zeros((q, 128), F32)
    for k in range(nx):
        piece = R.x[:, k * rows : (k + 1) * rows]
        half_bc = half_bc + dot(piece, R.wbc_all[k])
        raw_step = raw_step + dot(piece, R.wdt_all[k], 1, 1)
    R.bc_own[...] = half_bc.astype(BF16)
    share_bc = remote(R.bc_own, R.bc.at[it], R.core_s.at[0], R.core_r.at[0], dev(t=other))
    share_bc.start()
    R.bc[it] = R.bc_own[...]
    raw_step = raw_step + R.vec[2:3, :128]
    rate = -jnp.exp(R.vec[3:4, :128])
    step = jnp.maximum(raw_step, 0.0) + jnp.log1p(jnp.exp(-jnp.abs(raw_step)))
    ri = lax.broadcasted_iota(jnp.int32, (q, q), 0)
    ci = lax.broadcasted_iota(jnp.int32, (q, q), 1)
    causal = ri >= ci
    lower = jnp.where(causal, 1.0, 0.0).astype(F32)
    upper = jnp.where(ci >= ri, 1.0, 0.0).astype(F32)
    cum = dot(lower, step * rate, precision=EXACT)
    block_log = cum[q - 1 : q, :]
    R.log_own[...] = block_log

    def log_copy(d):
        return remote(
            R.log_own,
            R.logs.at[iz],
            R.z_s.at[5 * nz + d],
            R.z_r.at[5 * nz + d],
            dev(z=zoff(d)),
        )

    def log_start(d, carry):
        log_copy(d).start()
        return carry

    def log_wait(d, carry):
        log_copy(d).wait_recv()
        return carry

    def log_drain(d, carry):
        log_copy(d).wait_send()
        return carry

    lax.fori_loop(1, nz, log_start, 0)
    R.logs[iz] = R.log_own[...]
    into.y[2].forward()
    outof.xb.start()
    outof.xa.start()
    fade = jnp.exp(block_log - cum)
    weight = fade * step
    growth = jnp.exp(cum)
    R.cumt[...] = cum.T
    R.stept[...] = step.T
    eh = lax.broadcasted_iota(jnp.int32, (128, units), 0)
    eu = lax.broadcasted_iota(jnp.int32, (128, units), 1)
    expand = jnp.where(eu // width == eh, 1.0, 0.0).astype(BF16)

    def split(v):
        high = v.astype(BF16)
        return high, (v - high.astype(F32)).astype(BF16)

    def widen(v):
        high, rest = split(v)
        return dot(high, expand) + dot(rest, expand)

    R.weight_u[...] = widen(weight)
    R.growth_u[...] = widen(growth)

    for c in group:
        c.wait_recv()
    total = R.sums_all[0]
    for k in range(1, 2 * nx):
        total = total + R.sums_all[k]
    entries = 2.0 * nx * rows * units
    scale_in = jnp.sum(total[0:8, :]) / entries
    scale_out = jnp.sum(total[8:16, :]) / entries

    def ternary(w, scale):
        w = w.astype(F32)
        sign = jnp.where(w > 0.0, 1.0, -1.0)
        return jnp.where(jnp.abs(w) > 0.5 * scale, sign, 0.0).astype(BF16)

    share_bc.wait_recv()
    b_proj, c_proj = R.bc[0], R.bc[1]

    def z_copy(own, all_, base, to):
        d = lax.rem(to - iz + nz, nz)
        return remote(
            own.at[to], all_.at[iz], R.z_s.at[base + d], R.z_r.at[base + d], dev(z=to)
        )

    def z_send(own, all_, base, to, near):
        if not near:
            z_copy(own, all_, base, to).start()
            return

        @pl.when(to != iz)
        def _():
            z_copy(own, all_, base, to).start()

        @pl.when(to == iz)
        def _():
            all_[iz] = own[iz]

    def z_wait_from(own, all_, base, source, near):
        d = lax.rem(iz - source + nz, nz)
        copy = remote(
            own.at[source],
            all_.at[source],
            R.z_s.at[base + d],
            R.z_r.at[base + d],
            dev(z=source),
        )
        if not near:
            copy.wait_recv()
            return

        @pl.when(source != iz)
        def _():
            copy.wait_recv()

    def z_wait(own, all_, base):
        def one(d, carry):
            z_copy(own, all_, base, zoff(d)).wait_recv()
            return carry

        lax.fori_loop(1, nz, one, 0)

    def z_drain(own, all_, base):
        def one(d, carry):
            z_copy(own, all_, base, zoff(d)).wait_send()
            return carry

        lax.fori_loop(1, nz, one, 0)

    offs = sorted(range(ntile), key=lambda d: -min(d, ntile - d))
    own_tile = iz // hpt

    def tiles():
        for off in offs:
            t = lax.rem(own_tile + off, ntile)
            yield t, pl.ds(pl.multiple_of(t * tile, tile), tile), off == 0

    def y_exchange(own, all_, base):
        copies = [
            remote(own, all_.at[iy], R.y_s.at[base + d], R.y_r.at[base + d], dev(y=yoff(d)))
            for d in far_first(ny)
        ]
        for c in copies:
            c.start()
        all_[iy] = own[...]
        return copies

    into.finish()
    for t, cols, near in tiles():
        acc = jnp.zeros((q, tile), F32)
        for k in range(nx):
            code = ternary(R.win_all[k, :, cols], scale_in)
            R.codes[k, :, cols] = code
            acc = acc + dot(R.x[:, k * rows : (k + 1) * rows], code)
        v = scale_in * acc
        R.pre[:, cols] = v
        val = (v * lax.logistic(v)).astype(BF16)
        R.values[:, cols] = val
        wv = (val.astype(F32) * R.weight_u[:, cols]).astype(BF16)
        R.weighted[:, cols] = wv
        R.loc_own[pl.ds(t * hpt, hpt)] = (
            dot(wv, b_proj, 0, 0).astype(BF16).reshape(hpt, width, nstate)
        )
        for i in range(hpt):
            z_send(R.loc_own, R.loc_all, 0, t * hpt + i, near)

    gram = dot(c_proj, b_proj, 1, 1)
    lane = ci
    left_half = lax.broadcasted_iota(jnp.int32, (q, 2 * width), 1) < width
    zero_pair = jnp.zeros((q, 2 * width), BF16)

    def pick(s, pair):
        return jnp.where(left_half, pair, zero_pair) if s == 0 else jnp.where(left_half, zero_pair, pair)

    def inside(p, carry):
        cols = pl.ds(pl.multiple_of(p * 2 * width, 2 * width), 2 * width)
        pair = R.values[:, cols]
        acc = jnp.zeros((q, 2 * width), F32)
        for s in range(2):
            h = 2 * p + s
            col = jnp.sum(jnp.where(lane == h, cum, 0.0), axis=1, keepdims=True)
            row = R.cumt[pl.ds(h, 1), :]
            mask = jnp.exp(jnp.where(causal, col - row, -jnp.inf)) * R.stept[pl.ds(h, 1), :]
            R.zmask[h] = mask
            kb = (gram * mask).astype(BF16)
            R.kern[h] = kb
            acc = acc + dot(kb, pick(s, pair))
        R.intra[:, cols] = acc
        return carry

    lax.fori_loop(0, heads // 2, inside, 0)
    outof.xb.forward()
    outof.xb.neighbours()
    outof.y[0].start()
    outof.y[1].start()
    outof.xa.forward()
    outof.xb.opposite()
    outof.y[2].start()

    lax.fori_loop(1, nz, log_wait, 0)
    log_rows = R.logs[...].reshape(nz, 128)
    lane_z = lax.broadcasted_iota(jnp.int32, (nz, 128), 1)
    log_col = jnp.sum(jnp.where(lane_z == iz, log_rows, 0.0), axis=1, keepdims=True)
    R.dec[...] = jnp.broadcast_to(jnp.exp(log_col), (nz, 128))
    row_decay = jnp.exp(jnp.sum(log_col))
    z_wait(R.loc_own, R.loc_all, 0)

    def fwd_total(k, s):
        return R.dec[pl.ds(k, 1), :] * s + R.loc_all[k].astype(F32)

    zero_state = jnp.zeros((width, nstate), F32)
    R.fwd_own[0:width, :] = lax.fori_loop(0, nz, fwd_total, zero_state)
    R.fwd_own[width : width + 8, :] = jnp.broadcast_to(row_decay, (8, nstate))
    y_fwd = y_exchange(R.fwd_own, R.fwd_all, 0)
    for ring in outof.y:
        ring.forward()
    for c in y_fwd:
        c.wait_recv()
    state = zero_state
    for k in range(ny):
        grown = R.fwd_all[k, width : width + 1, :] * state + R.fwd_all[k, 0:width, :]
        state = jnp.where(k < iy, grown, state)

    def fwd_emit(k, s):
        R.ent_own[k] = s.astype(BF16)
        return fwd_total(k, s)

    lax.fori_loop(0, nz, fwd_emit, state)
    for off in offs:
        t = lax.rem(own_tile - off + ntile, ntile)
        for i in range(hpt):
            z_send(R.ent_own, R.held, nz, t * hpt + i, off == 0)

    x_copies = [
        remote(
            R.x.at[:, pl.ds(pl.multiple_of(xoff(d) * rows, rows), rows)],
            R.x_all.at[ix],
            R.x_s.at[d],
            R.x_r.at[d],
            dev(x=xoff(d)),
        )
        for d in range(1, nx)
    ]
    for c in x_copies:
        c.start()
    R.x_all[ix] = R.x[:, pl.ds(pl.multiple_of(ix * rows, rows), rows)]
    outof.finish()

    def project_out(j, carry):
        cols = pl.ds(pl.multiple_of(j * tile, tile), tile)
        acc = jnp.zeros((q, tile), F32)
        for k in range(nx):
            acc = acc + dot(
                R.g[:, k * rows : (k + 1) * rows], ternary(R.wout_all[k, :, cols], scale_out)
            )
        R.grad[:, cols] = scale_out * acc * R.vec[0:1, cols]
        return carry

    lax.fori_loop(0, ntile, project_out, 0)

    for t, cols, near in tiles():
        for i in range(hpt):
            z_wait_from(R.ent_own, R.held, nz, t * hpt + i, near)
        hb = R.held[pl.ds(t * hpt, hpt)].reshape(tile, nstate)
        grow = R.growth_u[:, cols]
        inter = grow * dot(c_proj, hb, 1, 1)
        output = R.intra[:, cols] + inter + R.vec[1:2, cols] * R.values[:, cols].astype(F32)
        scaled = R.grad[:, cols]
        pieces = []
        for g in range(tile // GROUP):
            sl = slice(g * GROUP, (g + 1) * GROUP)
            o, s = output[:, sl], scaled[:, sl]
            inverse = lax.rsqrt(jnp.mean(o * o, axis=1, keepdims=True) + 1e-05)
            mixed = jnp.mean(s * o, axis=1, keepdims=True)
            pieces.append(inverse * (s - o * (inverse * inverse) * mixed))
        grad_y = jnp.concatenate(pieces, axis=1) if len(pieces) > 1 else pieces[0]
        grown = (grad_y * grow).astype(BF16)
        R.term_own[pl.ds(t * hpt, hpt)] = (
            dot(grown, c_proj, 0, 0).astype(BF16).reshape(hpt, width, nstate)
        )
        for i in range(hpt):
            z_send(R.term_own, R.term_all, 2 * nz, t * hpt + i, near)
        R.grad[:, cols] = grad_y
        R.gbf[:, cols] = grad_y.astype(BF16)
        R.ggrown[:, cols] = grown
        R.iprod[:, cols] = grad_y * inter

    def head_sum(v, e=expand):
        high, rest = split(v)
        return dot(high, e, 1, 1) + dot(rest, e, 1, 1)

    R.colt[...] = jnp.zeros((128, q), F32)

    def inside_back(p, carry):
        zsum, rsum = carry
        cols = pl.ds(pl.multiple_of(p * 2 * width, 2 * width), 2 * width)
        pair = R.values[:, cols]
        gpair = R.gbf[:, cols]
        acc = jnp.zeros((q, 2 * width), F32)
        for s in range(2):
            h = 2 * p + s
            picked = pick(s, gpair)
            z = dot(picked, pair, 1, 1) * R.zmask[h]
            zsum = zsum + z
            product = z * gram
            rs = jnp.sum(product, axis=1, keepdims=True)
            rsum = jnp.where(lane == h, rs, rsum)
            R.colt[pl.ds(h, 1), :] = jnp.sum(product, axis=0, keepdims=True)
            acc = acc + dot(R.kern[h], picked, 0, 0)
        R.fromintra[:, cols] = acc + R.vec[1:2, cols] * R.grad[:, cols]
        return (zsum, rsum)

    zero_q = jnp.zeros((q, q), F32)
    zsum, row_sums = lax.fori_loop(0, heads // 2, inside_back, (zero_q, zero_q))
    inter_sum = head_sum(R.iprod[...])
    col_sums = R.colt[...].T
    zsum = zsum.astype(BF16)
    grad_c = dot(zsum, b_proj) + dot(R.ggrown[...], R.held[...].reshape(units, nstate))
    grad_b = dot(zsum, c_proj, 0, 0)

    z_wait(R.term_own, R.term_all, 2 * nz)

    def bwd_total(i, s):
        k = nz - 1 - i
        return R.dec[pl.ds(k, 1), :] * s + R.term_all[k].astype(F32)

    R.bwd_own[0:width, :] = lax.fori_loop(0, nz, bwd_total, zero_state)
    R.bwd_own[width : width + 8, :] = jnp.broadcast_to(row_decay, (8, nstate))
    y_bwd = y_exchange(R.bwd_own, R.bwd_all, ny)
    for c in y_bwd:
        c.wait_recv()
    state = zero_state
    for k in range(ny - 1, -1, -1):
        grown = R.bwd_all[k, width : width + 1, :] * state + R.bwd_all[k, 0:width, :]
        state = jnp.where(k > iy, grown, state)

    def bwd_emit(i, s):
        R.lea_own[nz - 1 - i] = s.astype(BF16)
        return bwd_total(i, s)

    lax.fori_loop(0, nz, bwd_emit, state)
    for off in offs:
        t = lax.rem(own_tile - off + ntile, ntile)
        for i in range(hpt):
            z_send(R.lea_own, R.leav, 3 * nz, t * hpt + i, off == 0)

    grad_weight = jnp.zeros((q, 128), F32)
    state_dot = jnp.zeros((8, 128), F32)
    ones = jnp.ones((8, nstate), BF16)
    tile_head = lax.broadcasted_iota(jnp.int32, (128, tile), 0)
    tile_unit = lax.broadcasted_iota(jnp.int32, (128, tile), 1)
    for t, cols, near in tiles():
        for i in range(hpt):
            z_wait_from(R.lea_own, R.leav, 3 * nz, t * hpt + i, near)
        lb = R.leav[pl.ds(t * hpt, hpt)].reshape(tile, nstate)
        hb = R.held[pl.ds(t * hpt, hpt)].reshape(tile, nstate)
        e = jnp.where(tile_unit // width + t * hpt == tile_head, 1.0, 0.0).astype(BF16)
        grad_b = grad_b + dot(R.weighted[:, cols], lb)
        gw = dot(b_proj, lb, 1, 1)
        grad_weight = grad_weight + head_sum(gw * R.values[:, cols].astype(F32), e)
        high, rest = split(lb.astype(F32) * hb.astype(F32))
        state_dot = state_dot + head_sum(dot(ones, high, 1, 1) + dot(ones, rest, 1, 1), e)
        grad_values = R.fromintra[:, cols] + gw * R.weight_u[:, cols]
        v = R.pre[:, cols]
        sg = lax.logistic(v)
        R.gbf[:, cols] = (scale_in * (grad_values * sg * (1.0 + v * (1.0 - sg)))).astype(BF16)

    R.half_own[...] = jnp.where(it == 0, grad_c, grad_b).astype(BF16)
    share_half = remote(R.half_own, R.half_in, R.core_s.at[1], R.core_r.at[1], dev(t=other))
    share_half.start()
    mine = jnp.where(it == 0, grad_b, grad_c)

    gw_w = grad_weight * weight
    grad_log = jnp.sum(gw_w, axis=0, keepdims=True) + jnp.exp(block_log) * state_dot[0:1, :]
    grad_cum = inter_sum + row_sums - col_sums - gw_w
    grad_cum = grad_cum + jnp.where(ri == q - 1, grad_log, 0.0)
    grad_rate = dot(upper, grad_cum, precision=EXACT)
    grad_step = col_sums / step + grad_weight * fade + rate * grad_rate
    grad_raw = jnp.where(lane < heads, grad_step * lax.logistic(raw_step), 0.0)
    R.sdt_own[...] = grad_raw.T[0:heads, :].astype(BF16)
    send_dt = grad_raw.astype(BF16)

    share_half.wait_recv()
    R.sbc_own[...] = (mine + R.half_in[...].astype(F32)).astype(BF16)
    s_copies = []
    for d in far_first(nx):
        for k, (own, all_) in enumerate(((R.sbc_own, R.sbc_all), (R.sdt_own, R.sdt_all))):
            at = nx * (k + 1) + d
            s_copies.append(
                remote(own, all_.at[ix], R.x_s.at[at], R.x_r.at[at], dev(x=xoff(d)))
            )
    for c in s_copies:
        c.start()
    R.sbc_all[ix] = R.sbc_own[...]
    R.sdt_all[ix] = R.sdt_own[...]

    per = nx // 2

    def partial_in(side, j):
        k = side * per + j
        return (
            dot(R.gbf[...], R.codes[k], 1, 1)
            + dot(R.sbc_own[...], R.wbc_all[k], 1, 1)
            + dot(send_dt, R.wdt_all[k])
        )

    for j in range(per):
        R.part_own[:, j * rows : (j + 1) * rows] = partial_in(other, j).astype(BF16)
    share_part = remote(R.part_own, R.part_in, R.core_s.at[2], R.core_r.at[2], dev(t=other))
    share_part.start()

    for c in x_copies + s_copies:
        c.wait_recv()
    grad_w = jnp.zeros((rows, nstate), F32)
    grad_t = jnp.zeros((heads, rows), F32)
    for k in range(nx):
        grad_w = grad_w + dot(R.x_all[k], R.sbc_all[k], 0, 0)
        grad_t = grad_t + dot(R.sdt_all[k], R.x_all[k])
    yrows = rows // ny
    R.ybc_own[...] = grad_w.astype(BF16).reshape(ny, yrows, nstate)
    for k in range(ny):
        R.ydt_own[k] = grad_t[:, k * yrows : (k + 1) * yrows].astype(BF16)
    yg_copies = []
    for d in far_first(ny):
        for k, (own, all_) in enumerate(((R.ybc_own, R.ybc_all), (R.ydt_own, R.ydt_all))):
            at = ny * (k + 2) + d
            yg_copies.append(
                remote(own.at[yoff(d)], all_.at[iy], R.y_s.at[at], R.y_r.at[at], dev(y=yoff(d)))
            )
    for c in yg_copies:
        c.start()
    R.ybc_all[iy] = R.ybc_own[iy]
    R.ydt_all[iy] = R.ydt_own[iy]

    for j in range(per):
        R.part_own_f[:, j * rows : (j + 1) * rows] = partial_in(it, j)

    for c in yg_copies:
        c.wait_recv()
    ysum = R.ybc_all[0].astype(F32)
    tsum = R.ydt_all[0].astype(F32)
    for k in range(1, ny):
        ysum = ysum + R.ybc_all[k].astype(F32)
        tsum = tsum + R.ydt_all[k].astype(F32)
    tsum = jnp.concatenate([tsum, jnp.zeros((128 - heads, yrows), F32)], axis=0).T
    few = yrows // nz
    for k in range(nz):
        sl = slice(k * few, (k + 1) * few)
        R.zg_own[k] = jnp.concatenate([ysum[sl], tsum[sl]], axis=0).astype(BF16)
    for d in far_first(nz):
        z_copy(R.zg_own, R.zg_all, 4 * nz, zoff(d)).start()
    R.zg_all[iz] = R.zg_own[iz]

    share_part.wait_recv()
    R.gin[...] = (R.part_own_f[...] + R.part_in[...].astype(F32)).astype(BF16)

    z_wait(R.zg_own, R.zg_all, 4 * nz)
    gsum = R.zg_all[0].astype(F32)
    for k in range(1, nz):
        gsum = gsum + R.zg_all[k].astype(F32)
    norm = (q * nx * ny * nz) ** -0.5
    R.gbc[...] = gsum[:few, :] * norm
    R.gdt[...] = gsum[few:, :heads] * norm

    for c in every + group + [share_bc, share_half, share_part]:
        c.wait_send()
    for c in y_fwd + y_bwd + yg_copies + x_copies + s_copies:
        c.wait_send()
    z_drain(R.loc_own, R.loc_all, 0)
    z_drain(R.ent_own, R.held, nz)
    z_drain(R.term_own, R.term_all, 2 * nz)
    z_drain(R.lea_own, R.leav, 3 * nz)
    z_drain(R.zg_own, R.zg_all, 4 * nz)
    lax.fori_loop(1, nz, log_drain, 0)


def shards(mesh_shape, layer_in, out_grad, w_in, w_out, w_bc, w_dt, dt_bias, a_log, d_skip, norm_gain):
    nx, nc = mesh_shape
    heads = a_log.shape[0]
    nz = heads
    ny = nc // nz
    q, depth = layer_in.shape[1:]
    rows, units = w_in.shape
    nstate = w_bc.shape[1]
    width = units // heads
    yrows = rows // ny
    few = yrows // nz
    straight = 3 * rows // 8 // (8 * ny) * 8 * ny
    flat = lambda v: jnp.pad(v, (0, units - v.shape[0]))[None, :]
    vec = jnp.concatenate(
        [
            norm_gain[None, :],
            jnp.repeat(d_skip, width)[None, :],
            flat(dt_bias),
            flat(a_log),
            jnp.zeros((4, units), F32),
        ],
        axis=0,
    )
    V = pltpu.VMEM
    dma = pltpu.SemaphoreType.DMA
    state = V((nz, width, nstate), BF16)
    full = V((q, units), F32)
    half = V((q, units), BF16)
    total = V((width + 8, nstate), F32)
    totals = V((ny, width + 8, nstate), F32)
    scratch = dict(
        win_all=V((nx, rows, units), BF16),
        wout_all=V((nx, rows, units), BF16),
        wbc_all=V((nx, rows, nstate), BF16),
        wdt_all=V((nx, 128, rows), BF16),
        codes=V((nx, rows, units), BF16),
        sums_own=V((16, 128), F32),
        sums_all=V((2 * nx, 16, 128), F32),
        bc_own=V((q, nstate), BF16),
        bc=V((2, q, nstate), BF16),
        log_own=V((1, 128), F32),
        logs=V((nz, 1, 128), F32),
        loc_own=state,
        loc_all=state,
        ent_own=state,
        held=state,
        term_own=state,
        term_all=state,
        lea_own=state,
        leav=state,
        fwd_own=total,
        fwd_all=totals,
        bwd_own=total,
        bwd_all=totals,
        x_all=V((nx, q, rows), BF16),
        sbc_own=V((q, nstate), BF16),
        sbc_all=V((nx, q, nstate), BF16),
        sdt_own=V((heads, q), BF16),
        sdt_all=V((nx, heads, q), BF16),
        ybc_own=V((ny, yrows, nstate), BF16),
        ybc_all=V((ny, yrows, nstate), BF16),
        ydt_own=V((ny, heads, yrows), BF16),
        ydt_all=V((ny, heads, yrows), BF16),
        zg_own=V((nz, 2 * few, nstate), BF16),
        zg_all=V((nz, 2 * few, nstate), BF16),
        half_own=V((q, nstate), BF16),
        half_in=V((q, nstate), BF16),
        part_own=V((q, depth // 2), BF16),
        part_in=V((q, depth // 2), BF16),
        part_own_f=V((q, depth // 2), F32),
        pre=full,
        values=half,
        weighted=half,
        weight_u=full,
        growth_u=full,
        cumt=V((128, q), F32),
        stept=V((128, q), F32),
        kern=V((heads, q, q), BF16),
        zmask=V((heads, q, q), F32),
        intra=full,
        grad=full,
        gbf=half,
        ggrown=half,
        iprod=full,
        colt=V((128, q), F32),
        fromintra=full,
        dec=V((nz, 128), F32),
        w_s=dma((72,)),
        w_r=dma((72,)),
        grp_s=dma((2 * nx,)),
        grp_r=dma((2 * nx,)),
        core_s=dma((3,)),
        core_r=dma((3,)),
        z_s=dma((6 * nz,)),
        z_r=dma((6 * nz,)),
        y_s=dma((4 * ny,)),
        y_r=dma((4 * ny,)),
        x_s=dma((3 * nx,)),
        x_r=dma((3 * nx,)),
        loc_s=dma((2,)),
    )
    names = NAMES[10:]
    vm = pl.BlockSpec(memory_space=pltpu.VMEM)
    grad_in, grad_bc, grad_dt = pl.pallas_call(
        functools.partial(layer_kernel, nx, ny, nz, straight),
        out_shape=(
            jax.ShapeDtypeStruct((q, depth // 2), BF16),
            jax.ShapeDtypeStruct((few, nstate), F32),
            jax.ShapeDtypeStruct((few, heads), F32),
        ),
        in_specs=[vm] * 7,
        out_specs=(vm, vm, vm),
        scratch_shapes=[scratch[n] for n in names],
        compiler_params=pltpu.CompilerParams(
            collective_id=0, has_side_effects=True, vmem_limit_bytes=60 * 1024 * 1024
        ),
        name="ternary_layer",
    )(layer_in[0], out_grad[0], w_in, w_out, w_bc, w_dt.T, vec)
    return (grad_in[None], grad_bc, grad_dt)


def solution(mesh):
    in_specs = (
        P("dp", "ctx", None),
        P("dp", "ctx", None),
        P("dp", "tensor"),
        P("dp", "tensor"),
        P("dp", "tensor"),
        P("dp", "tensor"),
        P("tensor"),
        P("tensor"),
        P("tensor"),
        P("tensor"),
    )
    out_specs = (P("dp", "ctx", "tensor"), P(("dp", "ctx"), "tensor"), P(("dp", "ctx"), "tensor"))
    body = functools.partial(shards, (mesh.shape["dp"], mesh.shape["ctx"]))
    return jax.shard_map(body, mesh=mesh, in_specs=in_specs, out_specs=out_specs, check_vma=False)
```

```python
import functools
import types

import jax
import jax.numpy as jnp
from jax import lax
from jax.experimental import pallas as pl
from jax.experimental.pallas import tpu as pltpu
from jax.sharding import PartitionSpec as P

GROUP = 256
MESH = pl.DeviceIdType.MESH
F32 = jnp.float32
BF16 = jnp.bfloat16
EXACT = lax.Precision.HIGHEST


def dot(a, b, ca=1, cb=0, precision=None):
    return lax.dot_general(
        a, b, (((ca,), (cb,)), ((), ())), precision=precision, preferred_element_type=F32
    )


NAMES = [
    "x_in", "g_in", "win", "wout", "wbc_in", "wdt_in", "gain_in", "skip_in",
    "bias_in", "rate_in", "gin", "gbc", "gdt", "x", "g", "wbc",
    "wdt", "gain", "skip", "bias", "rate", "skip_u", "win_all", "wout_all",
    "wbc_all", "wdt_all", "codes", "sums_own", "sums_all", "bc_own", "bc", "log_own",
    "logs", "loc_own", "loc_all", "ent_own", "held", "term_own", "term_all", "lea_own",
    "leav", "fwd_own", "fwd_all", "bwd_own", "bwd_all", "x_all", "sbc_own", "sbc_all",
    "sdt_own", "sdt_all", "ybc_own", "ybc_all", "ydt_own", "ydt_all", "zg_own", "zg_all",
    "half_own", "half_in", "part_own", "part_in", "part_own_f", "pre", "values", "weighted",
    "weight_u", "growth_u", "cumt", "stept", "kern", "zmask", "intra", "grad",
    "gbf", "ggrown", "iprod", "colt", "fromintra", "dec", "w_s", "w_r",
    "grp_s", "grp_r", "core_s", "core_r", "z_s", "z_r", "y_s", "y_r",
    "x_s", "x_r", "loc_s", "far",
]


def far_first(n):
    return sorted(range(1, n), key=lambda d: -min(d, n - d))


def layer_kernel(nx, ny, nz, straight, *refs):
    R = types.SimpleNamespace(**dict(zip(NAMES, refs, strict=True)))
    q, depth = R.x_in.shape
    rows, units = R.win.shape
    heads = nz
    width = units // heads
    nstate = R.wbc_in.shape[1]
    tile = min(256, units)
    ntile = units // tile
    hpt = tile // width
    ix = lax.axis_index("dp")
    ic = lax.axis_index("ctx")
    it = lax.axis_index("tensor")
    iz = lax.rem(ic, nz)
    iy = ic // nz
    other = 1 - it

    def dev(x=ix, y=iy, z=iz, t=it):
        return (x, y * nz + z, t)

    def remote(src, dst, ssem, rsem, device):
        return pltpu.make_async_remote_copy(
            src_ref=src,
            dst_ref=dst,
            send_sem=ssem,
            recv_sem=rsem,
            device_id=device,
            device_id_type=MESH,
        )

    def xoff(d):
        return lax.rem(ix + d, nx)

    def yoff(d):
        return lax.rem(iy + d, ny)

    def zoff(d):
        return lax.rem(iz + d, nz)

    barrier = pltpu.get_barrier_semaphore()
    count = 0

    for d in (1, nz - 1):
        pl.semaphore_signal(barrier, inc=1, device_id=dev(z=zoff(d)), device_id_type=MESH)
        count += 1
    for d in range(nx):
        for t in (it, other):
            if d == 0 and t is it:
                continue
            pl.semaphore_signal(barrier, inc=1, device_id=dev(x=xoff(d), t=t), device_id_type=MESH)
            count += 1
    for d in range(1, ny):
        pl.semaphore_signal(barrier, inc=1, device_id=dev(y=yoff(d)), device_id_type=MESH)
        count += 1

    loads = [
        pltpu.make_async_copy(src, dst, R.loc_s.at[k])
        for k, (src, dst) in enumerate(
            (
                (R.win, R.win_all.at[ix]),
                (R.wout, R.wout_all.at[ix]),
                (R.wbc_in, R.wbc),
                (R.wdt_in, R.wdt),
                (R.x_in, R.x),
                (R.bias_in, R.bias),
                (R.rate_in, R.rate),
                (R.gain_in, R.gain),
                (R.skip_in, R.skip),
                (R.g_in, R.g),
            )
        )
    ]
    for c in loads:
        c.start()

    def magnitude(ref):
        def one(i, acc):
            piece = jnp.abs(ref[ix, pl.ds(pl.multiple_of(i * 16, 16), 16), :].astype(F32))
            return acc + piece

        total = lax.fori_loop(0, rows // 16, one, jnp.zeros((16, units), F32))
        out = total[:8, :128] + total[8:, :128]
        for c in range(1, units // 128):
            out = out + total[:8, c * 128 : (c + 1) * 128] + total[8:, c * 128 : (c + 1) * 128]
        return out

    for k in range(nx):
        R.wdt_all[k, heads:, :] = jnp.zeros((128 - heads, rows), BF16)
    for c in loads:
        c.wait()
    pl.semaphore_wait(barrier, count)

    links = [0]
    every = []

    def link(src, dst, device):
        k = links[0]
        links[0] += 1
        c = remote(src, dst, R.w_s.at[k], R.w_r.at[k], device)
        every.append(c)
        return c

    class Ring:
        def __init__(self, n, own, place, before, after, right, left):
            self.relay = []
            if n == 2:
                self.first = [link(own(c), place(c), right) for c in range(2)]
                return
            self.first = [
                link(own(0), place(0), right),
                link(own(1), place(1), left),
                link(own(1), place(1), right),
                link(own(0), place(0), left),
            ]
            self.relay = [
                link(before(0), before(0), right),
                link(after(1), after(1), left),
            ]

        def start(self):
            for c in self.first:
                c.start()

        def forward(self):
            for k, c in enumerate(self.relay):
                self.first[k].wait_recv()
                c.start()

        def neighbours(self):
            for c in self.first[2:] if self.relay else self.first:
                c.wait_recv()

        def opposite(self):
            for c in self.relay:
                c.wait_recv()

    def x_ring(view, dst):
        return Ring(
            nx,
            lambda c: view(None, c),
            lambda c: view(dst.at[ix], c),
            lambda c: view(dst.at[xoff(nx - 1)], c),
            lambda c: view(dst.at[xoff(1)], c),
            dev(x=xoff(1)),
            dev(x=xoff(nx - 1)),
        )

    half_units = units // 2

    class Gather:
        def __init__(self, dst):
            share = (rows - straight) // ny

            def part(first, count):
                def view(ref, c):
                    ref = dst.at[ix] if ref is None else ref
                    return ref.at[pl.ds(first, count), pl.ds(c * half_units, half_units)]

                return view

            def quarter(y):
                return part(pl.multiple_of(straight + y * share, 8), share)

            self.xb = x_ring(quarter(iy), dst)
            self.xa = x_ring(part(0, straight), dst)
            self.y = []
            for slot in (xoff(nx - 1), xoff(1), xoff(2)):
                at = dst.at[slot]
                mine = quarter(iy)
                self.y.append(
                    Ring(
                        ny,
                        lambda c, at=at: mine(at, c),
                        lambda c, at=at: mine(at, c),
                        lambda c, at=at: quarter(yoff(ny - 1))(at, c),
                        lambda c, at=at: quarter(yoff(1))(at, c),
                        dev(y=yoff(1)),
                        dev(y=yoff(ny - 1)),
                    )
                )

        def finish(self):
            self.xa.neighbours()
            self.xa.opposite()
            for ring in self.y:
                ring.neighbours()
                ring.opposite()

    by_rows = rows // 2
    ring_bc = x_ring(
        lambda ref, c: (R.wbc if ref is None else ref).at[pl.ds(c * by_rows, by_rows), :], R.wbc_all
    )
    ring_dt = x_ring(
        lambda ref, c: (
            R.wdt.at[:, pl.ds(c * by_rows, by_rows)]
            if ref is None
            else ref.at[pl.ds(0, heads), pl.ds(c * by_rows, by_rows)]
        ),
        R.wdt_all,
    )
    into = Gather(R.win_all)
    outof = Gather(R.wout_all)

    group = []
    for d in range(nx):
        for k, t in enumerate((it, other)):
            if d == 0 and k == 0:
                continue
            group.append(
                remote(
                    R.sums_own,
                    R.sums_all.at[2 * ix + it],
                    R.grp_s.at[2 * d + k],
                    R.grp_r.at[2 * d + k],
                    dev(x=xoff(d), t=t),
                )
            )

    into.xb.start()
    ring_bc.start()
    ring_dt.start()
    def farther(r, carry):
        for k, d in enumerate((1, nz - 1)):
            pl.semaphore_signal(R.far.at[k], inc=1, device_id=dev(z=zoff(d)), device_id_type=MESH)
        for k in range(2):
            pl.semaphore_wait(R.far.at[k], 1)
        return carry

    lax.fori_loop(1, nz // 2, farther, 0)
    R.sums_own[0:8, :] = magnitude(R.win_all)
    R.sums_own[8:16, :] = magnitude(R.wout_all)
    for c in group:
        c.start()
    R.sums_all[2 * ix + it] = R.sums_own[...]
    R.wbc_all[ix] = R.wbc[...]
    R.wdt_all[ix, 0:heads, :] = R.wdt[...]
    into.xb.forward()
    into.xa.start()
    into.xb.neighbours()
    into.y[0].start()
    into.y[1].start()
    ring_bc.forward()
    ring_dt.forward()
    into.xb.opposite()
    into.y[2].start()
    into.y[0].forward()
    into.xa.forward()
    into.y[1].forward()

    for ring in (ring_bc, ring_dt):
        ring.neighbours()
        ring.opposite()
    half_bc = jnp.zeros((q, nstate), F32)
    raw_step = jnp.zeros((q, 128), F32)
    for k in range(nx):
        piece = R.x[:, k * rows : (k + 1) * rows]
        half_bc = half_bc + dot(piece, R.wbc_all[k])
        raw_step = raw_step + dot(piece, R.wdt_all[k], 1, 1)
    R.bc_own[...] = half_bc.astype(BF16)
    share_bc = remote(R.bc_own, R.bc.at[it], R.core_s.at[0], R.core_r.at[0], dev(t=other))
    share_bc.start()
    R.bc[it] = R.bc_own[...]

    def lane_pad(v):
        return jnp.concatenate([v, jnp.zeros((1, 128 - heads), F32)], axis=1)

    raw_step = raw_step + lane_pad(R.bias[...])
    rate = -jnp.exp(lane_pad(R.rate[...]))
    step = jnp.maximum(raw_step, 0.0) + jnp.log1p(jnp.exp(-jnp.abs(raw_step)))
    ri = lax.broadcasted_iota(jnp.int32, (q, q), 0)
    ci = lax.broadcasted_iota(jnp.int32, (q, q), 1)
    causal = ri >= ci
    lower = jnp.where(causal, 1.0, 0.0).astype(F32)
    upper = jnp.where(ci >= ri, 1.0, 0.0).astype(F32)
    cum = dot(lower, step * rate, precision=EXACT)
    block_log = cum[q - 1 : q, :]
    R.log_own[...] = block_log

    def log_copy(d):
        return remote(
            R.log_own,
            R.logs.at[iz],
            R.z_s.at[5 * nz + d],
            R.z_r.at[5 * nz + d],
            dev(z=zoff(d)),
        )

    def log_start(d, carry):
        log_copy(d).start()
        return carry

    def log_wait(d, carry):
        log_copy(d).wait_recv()
        return carry

    def log_drain(d, carry):
        log_copy(d).wait_send()
        return carry

    lax.fori_loop(1, nz, log_start, 0)
    R.logs[iz] = R.log_own[...]
    into.y[2].forward()
    outof.xb.start()
    outof.xa.start()
    fade = jnp.exp(block_log - cum)
    weight = fade * step
    growth = jnp.exp(cum)
    R.cumt[...] = cum.T
    R.stept[...] = step.T
    eh = lax.broadcasted_iota(jnp.int32, (128, units), 0)
    eu = lax.broadcasted_iota(jnp.int32, (128, units), 1)
    expand = jnp.where(eu // width == eh, 1.0, 0.0).astype(BF16)

    def split(v):
        high = v.astype(BF16)
        return high, (v - high.astype(F32)).astype(BF16)

    def widen(v):
        high, rest = split(v)
        return dot(high, expand) + dot(rest, expand)

    R.weight_u[...] = widen(weight)
    R.growth_u[...] = widen(growth)
    R.skip_u[...] = dot(
        jnp.broadcast_to(lane_pad(R.skip[...]), (8, 128)), expand.astype(F32), precision=EXACT
    )

    for c in group:
        c.wait_recv()
    total = R.sums_all[0]
    for k in range(1, 2 * nx):
        total = total + R.sums_all[k]
    entries = 2.0 * nx * rows * units
    scale_in = jnp.sum(total[0:8, :]) / entries
    scale_out = jnp.sum(total[8:16, :]) / entries

    def ternary(w, scale):
        w = w.astype(F32)
        sign = jnp.where(w > 0.0, 1.0, -1.0)
        return jnp.where(jnp.abs(w) > 0.5 * scale, sign, 0.0).astype(BF16)

    share_bc.wait_recv()
    b_proj, c_proj = R.bc[0], R.bc[1]

    def z_copy(own, all_, base, to):
        d = lax.rem(to - iz + nz, nz)
        return remote(
            own.at[to], all_.at[iz], R.z_s.at[base + d], R.z_r.at[base + d], dev(z=to)
        )

    def z_send(own, all_, base, to, near):
        if not near:
            z_copy(own, all_, base, to).start()
            return

        @pl.when(to != iz)
        def _():
            z_copy(own, all_, base, to).start()

        @pl.when(to == iz)
        def _():
            all_[iz] = own[iz]

    def z_wait_from(own, all_, base, source, near):
        d = lax.rem(iz - source + nz, nz)
        copy = remote(
            own.at[source],
            all_.at[source],
            R.z_s.at[base + d],
            R.z_r.at[base + d],
            dev(z=source),
        )
        if not near:
            copy.wait_recv()
            return

        @pl.when(source != iz)
        def _():
            copy.wait_recv()

    def z_wait(own, all_, base):
        def one(d, carry):
            z_copy(own, all_, base, zoff(d)).wait_recv()
            return carry

        lax.fori_loop(1, nz, one, 0)

    def z_drain(own, all_, base):
        def one(d, carry):
            z_copy(own, all_, base, zoff(d)).wait_send()
            return carry

        lax.fori_loop(1, nz, one, 0)

    offs = sorted(range(ntile), key=lambda d: -min(d, ntile - d))
    own_tile = iz // hpt

    def tiles():
        for off in offs:
            t = lax.rem(own_tile + off, ntile)
            yield t, pl.ds(pl.multiple_of(t * tile, tile), tile), off == 0

    def y_exchange(own, all_, base):
        copies = [
            remote(own, all_.at[iy], R.y_s.at[base + d], R.y_r.at[base + d], dev(y=yoff(d)))
            for d in far_first(ny)
        ]
        for c in copies:
            c.start()
        all_[iy] = own[...]
        return copies

    into.finish()
    for t, cols, near in tiles():
        acc = jnp.zeros((q, tile), F32)
        for k in range(nx):
            code = ternary(R.win_all[k, :, cols], scale_in)
            R.codes[k, :, cols] = code
            acc = acc + dot(R.x[:, k * rows : (k + 1) * rows], code)
        v = scale_in * acc
        R.pre[:, cols] = v
        val = (v * lax.logistic(v)).astype(BF16)
        R.values[:, cols] = val
        wv = (val.astype(F32) * R.weight_u[:, cols]).astype(BF16)
        R.weighted[:, cols] = wv
        R.loc_own[pl.ds(t * hpt, hpt)] = (
            dot(wv, b_proj, 0, 0).astype(BF16).reshape(hpt, width, nstate)
        )
        for i in range(hpt):
            z_send(R.loc_own, R.loc_all, 0, t * hpt + i, near)

    gram = dot(c_proj, b_proj, 1, 1)
    lane = ci
    left_half = lax.broadcasted_iota(jnp.int32, (q, 2 * width), 1) < width
    zero_pair = jnp.zeros((q, 2 * width), BF16)

    def pick(s, pair):
        return jnp.where(left_half, pair, zero_pair) if s == 0 else jnp.where(left_half, zero_pair, pair)

    def inside(p, carry):
        cols = pl.ds(pl.multiple_of(p * 2 * width, 2 * width), 2 * width)
        pair = R.values[:, cols]
        acc = jnp.zeros((q, 2 * width), F32)
        for s in range(2):
            h = 2 * p + s
            col = jnp.sum(jnp.where(lane == h, cum, 0.0), axis=1, keepdims=True)
            row = R.cumt[pl.ds(h, 1), :]
            mask = jnp.exp(jnp.where(causal, col - row, -jnp.inf)) * R.stept[pl.ds(h, 1), :]
            R.zmask[h] = mask
            kb = (gram * mask).astype(BF16)
            R.kern[h] = kb
            acc = acc + dot(kb, pick(s, pair))
        R.intra[:, cols] = acc
        return carry

    lax.fori_loop(0, heads // 2, inside, 0)
    outof.xb.forward()
    outof.xb.neighbours()
    outof.y[0].start()
    outof.y[1].start()
    outof.xa.forward()
    outof.xb.opposite()
    outof.y[2].start()

    lax.fori_loop(1, nz, log_wait, 0)
    log_rows = R.logs[...].reshape(nz, 128)
    lane_z = lax.broadcasted_iota(jnp.int32, (nz, 128), 1)
    log_col = jnp.sum(jnp.where(lane_z == iz, log_rows, 0.0), axis=1, keepdims=True)
    R.dec[...] = jnp.broadcast_to(jnp.exp(log_col), (nz, 128))
    row_decay = jnp.broadcast_to(jnp.exp(jnp.sum(log_col)), (16, nstate))
    high, rest = split(row_decay)
    decay_rows = jnp.where(
        lax.broadcasted_iota(jnp.int32, (16, nstate), 0) < 8, high.astype(F32), rest.astype(F32)
    ).astype(BF16)

    def row_total(ref, k):
        tail = ref[k, width:, :].astype(F32)
        return tail[0:1, :] + tail[8:9, :], ref[k, 0:width, :].astype(F32)

    z_wait(R.loc_own, R.loc_all, 0)

    def fwd_total(k, s):
        return R.dec[pl.ds(k, 1), :] * s + R.loc_all[k].astype(F32)

    zero_state = jnp.zeros((width, nstate), F32)
    R.fwd_own[0:width, :] = lax.fori_loop(0, nz, fwd_total, zero_state).astype(BF16)
    R.fwd_own[width:, :] = decay_rows
    y_fwd = y_exchange(R.fwd_own, R.fwd_all, 0)
    for ring in outof.y:
        ring.forward()
    for c in y_fwd:
        c.wait_recv()
    state = zero_state
    for k in range(ny):
        factor, added = row_total(R.fwd_all, k)
        grown = factor * state + added
        state = jnp.where(k < iy, grown, state)

    def fwd_emit(k, s):
        R.ent_own[k] = s.astype(BF16)
        return fwd_total(k, s)

    lax.fori_loop(0, nz, fwd_emit, state)
    for off in offs:
        t = lax.rem(own_tile - off + ntile, ntile)
        for i in range(hpt):
            z_send(R.ent_own, R.held, nz, t * hpt + i, off == 0)

    x_copies = [
        remote(
            R.x.at[:, pl.ds(pl.multiple_of(xoff(d) * rows, rows), rows)],
            R.x_all.at[ix],
            R.x_s.at[d],
            R.x_r.at[d],
            dev(x=xoff(d)),
        )
        for d in range(1, nx)
    ]
    for c in x_copies:
        c.start()
    R.x_all[ix] = R.x[:, pl.ds(pl.multiple_of(ix * rows, rows), rows)]
    outof.finish()

    def project_out(j, carry):
        cols = pl.ds(pl.multiple_of(j * tile, tile), tile)
        acc = jnp.zeros((q, tile), F32)
        for k in range(nx):
            acc = acc + dot(
                R.g[:, k * rows : (k + 1) * rows], ternary(R.wout_all[k, :, cols], scale_out)
            )
        R.grad[:, cols] = scale_out * acc * R.gain[:, cols]
        return carry

    lax.fori_loop(0, ntile, project_out, 0)

    for t, cols, near in tiles():
        for i in range(hpt):
            z_wait_from(R.ent_own, R.held, nz, t * hpt + i, near)
        hb = R.held[pl.ds(t * hpt, hpt)].reshape(tile, nstate)
        grow = R.growth_u[:, cols]
        inter = grow * dot(c_proj, hb, 1, 1)
        output = R.intra[:, cols] + inter + R.skip_u[0:1, cols] * R.values[:, cols].astype(F32)
        scaled = R.grad[:, cols]
        pieces = []
        for g in range(tile // GROUP):
            sl = slice(g * GROUP, (g + 1) * GROUP)
            o, s = output[:, sl], scaled[:, sl]
            inverse = lax.rsqrt(jnp.mean(o * o, axis=1, keepdims=True) + 1e-05)
            mixed = jnp.mean(s * o, axis=1, keepdims=True)
            pieces.append(inverse * (s - o * (inverse * inverse) * mixed))
        grad_y = jnp.concatenate(pieces, axis=1) if len(pieces) > 1 else pieces[0]
        grown = (grad_y * grow).astype(BF16)
        R.term_own[pl.ds(t * hpt, hpt)] = (
            dot(grown, c_proj, 0, 0).astype(BF16).reshape(hpt, width, nstate)
        )
        for i in range(hpt):
            z_send(R.term_own, R.term_all, 2 * nz, t * hpt + i, near)
        R.grad[:, cols] = grad_y
        R.gbf[:, cols] = grad_y.astype(BF16)
        R.ggrown[:, cols] = grown
        R.iprod[:, cols] = grad_y * inter

    def head_sum(v, e=expand):
        high, rest = split(v)
        return dot(high, e, 1, 1) + dot(rest, e, 1, 1)

    R.colt[...] = jnp.zeros((128, q), F32)

    def inside_back(p, carry):
        zsum, rsum = carry
        cols = pl.ds(pl.multiple_of(p * 2 * width, 2 * width), 2 * width)
        pair = R.values[:, cols]
        gpair = R.gbf[:, cols]
        acc = jnp.zeros((q, 2 * width), F32)
        for s in range(2):
            h = 2 * p + s
            picked = pick(s, gpair)
            z = dot(picked, pair, 1, 1) * R.zmask[h]
            zsum = zsum + z
            product = z * gram
            rs = jnp.sum(product, axis=1, keepdims=True)
            rsum = jnp.where(lane == h, rs, rsum)
            R.colt[pl.ds(h, 1), :] = jnp.sum(product, axis=0, keepdims=True)
            acc = acc + dot(R.kern[h], picked, 0, 0)
        R.fromintra[:, cols] = acc + R.skip_u[0:1, cols] * R.grad[:, cols]
        return (zsum, rsum)

    zero_q = jnp.zeros((q, q), F32)
    zsum, row_sums = lax.fori_loop(0, heads // 2, inside_back, (zero_q, zero_q))
    inter_sum = head_sum(R.iprod[...])
    col_sums = R.colt[...].T
    zsum = zsum.astype(BF16)
    grad_c = dot(zsum, b_proj) + dot(R.ggrown[...], R.held[...].reshape(units, nstate))
    grad_b = dot(zsum, c_proj, 0, 0)

    z_wait(R.term_own, R.term_all, 2 * nz)

    def bwd_total(i, s):
        k = nz - 1 - i
        return R.dec[pl.ds(k, 1), :] * s + R.term_all[k].astype(F32)

    R.bwd_own[0:width, :] = lax.fori_loop(0, nz, bwd_total, zero_state).astype(BF16)
    R.bwd_own[width:, :] = decay_rows
    y_bwd = y_exchange(R.bwd_own, R.bwd_all, ny)
    for c in y_bwd:
        c.wait_recv()
    state = zero_state
    for k in range(ny - 1, -1, -1):
        factor, added = row_total(R.bwd_all, k)
        grown = factor * state + added
        state = jnp.where(k > iy, grown, state)

    def bwd_emit(i, s):
        R.lea_own[nz - 1 - i] = s.astype(BF16)
        return bwd_total(i, s)

    lax.fori_loop(0, nz, bwd_emit, state)
    for off in offs:
        t = lax.rem(own_tile - off + ntile, ntile)
        for i in range(hpt):
            z_send(R.lea_own, R.leav, 3 * nz, t * hpt + i, off == 0)

    grad_weight = jnp.zeros((q, 128), F32)
    state_dot = jnp.zeros((8, 128), F32)
    ones = jnp.ones((8, nstate), BF16)
    tile_head = lax.broadcasted_iota(jnp.int32, (128, tile), 0)
    tile_unit = lax.broadcasted_iota(jnp.int32, (128, tile), 1)
    for t, cols, near in tiles():
        for i in range(hpt):
            z_wait_from(R.lea_own, R.leav, 3 * nz, t * hpt + i, near)
        lb = R.leav[pl.ds(t * hpt, hpt)].reshape(tile, nstate)
        hb = R.held[pl.ds(t * hpt, hpt)].reshape(tile, nstate)
        e = jnp.where(tile_unit // width + t * hpt == tile_head, 1.0, 0.0).astype(BF16)
        grad_b = grad_b + dot(R.weighted[:, cols], lb)
        gw = dot(b_proj, lb, 1, 1)
        grad_weight = grad_weight + head_sum(gw * R.values[:, cols].astype(F32), e)
        high, rest = split(lb.astype(F32) * hb.astype(F32))
        state_dot = state_dot + head_sum(dot(ones, high, 1, 1) + dot(ones, rest, 1, 1), e)
        grad_values = R.fromintra[:, cols] + gw * R.weight_u[:, cols]
        v = R.pre[:, cols]
        sg = lax.logistic(v)
        R.gbf[:, cols] = (scale_in * (grad_values * sg * (1.0 + v * (1.0 - sg)))).astype(BF16)

    R.half_own[...] = jnp.where(it == 0, grad_c, grad_b).astype(BF16)
    share_half = remote(R.half_own, R.half_in, R.core_s.at[1], R.core_r.at[1], dev(t=other))
    share_half.start()
    mine = jnp.where(it == 0, grad_b, grad_c)

    gw_w = grad_weight * weight
    grad_log = jnp.sum(gw_w, axis=0, keepdims=True) + jnp.exp(block_log) * state_dot[0:1, :]
    grad_cum = inter_sum + row_sums - col_sums - gw_w
    grad_cum = grad_cum + jnp.where(ri == q - 1, grad_log, 0.0)
    grad_rate = dot(upper, grad_cum, precision=EXACT)
    grad_step = col_sums / step + grad_weight * fade + rate * grad_rate
    grad_raw = jnp.where(lane < heads, grad_step * lax.logistic(raw_step), 0.0)
    R.sdt_own[...] = grad_raw.T[0:heads, :].astype(BF16)
    send_dt = grad_raw.astype(BF16)

    share_half.wait_recv()
    R.sbc_own[...] = (mine + R.half_in[...].astype(F32)).astype(BF16)
    s_copies = []
    for d in far_first(nx):
        for k, (own, all_) in enumerate(((R.sbc_own, R.sbc_all), (R.sdt_own, R.sdt_all))):
            at = nx * (k + 1) + d
            s_copies.append(
                remote(own, all_.at[ix], R.x_s.at[at], R.x_r.at[at], dev(x=xoff(d)))
            )
    for c in s_copies:
        c.start()
    R.sbc_all[ix] = R.sbc_own[...]
    R.sdt_all[ix] = R.sdt_own[...]

    per = nx // 2

    def partial_in(side, j):
        k = side * per + j
        return (
            dot(R.gbf[...], R.codes[k], 1, 1)
            + dot(R.sbc_own[...], R.wbc_all[k], 1, 1)
            + dot(send_dt, R.wdt_all[k])
        )

    for j in range(per):
        R.part_own[:, j * rows : (j + 1) * rows] = partial_in(other, j).astype(BF16)
    share_part = remote(R.part_own, R.part_in, R.core_s.at[2], R.core_r.at[2], dev(t=other))
    share_part.start()

    for c in x_copies + s_copies:
        c.wait_recv()
    grad_w = jnp.zeros((rows, nstate), F32)
    grad_t = jnp.zeros((heads, rows), F32)
    for k in range(nx):
        grad_w = grad_w + dot(R.x_all[k], R.sbc_all[k], 0, 0)
        grad_t = grad_t + dot(R.sdt_all[k], R.x_all[k])
    yrows = rows // ny
    R.ybc_own[...] = grad_w.astype(BF16).reshape(ny, yrows, nstate)
    for k in range(ny):
        R.ydt_own[k] = grad_t[:, k * yrows : (k + 1) * yrows].astype(BF16)
    yg_copies = []
    for d in far_first(ny):
        for k, (own, all_) in enumerate(((R.ybc_own, R.ybc_all), (R.ydt_own, R.ydt_all))):
            at = ny * (k + 2) + d
            yg_copies.append(
                remote(own.at[yoff(d)], all_.at[iy], R.y_s.at[at], R.y_r.at[at], dev(y=yoff(d)))
            )
    for c in yg_copies:
        c.start()
    R.ybc_all[iy] = R.ybc_own[iy]
    R.ydt_all[iy] = R.ydt_own[iy]

    for j in range(per):
        R.part_own_f[:, j * rows : (j + 1) * rows] = partial_in(it, j)

    for c in yg_copies:
        c.wait_recv()
    ysum = R.ybc_all[0].astype(F32)
    tsum = R.ydt_all[0].astype(F32)
    for k in range(1, ny):
        ysum = ysum + R.ybc_all[k].astype(F32)
        tsum = tsum + R.ydt_all[k].astype(F32)
    tsum = jnp.concatenate([tsum, jnp.zeros((128 - heads, yrows), F32)], axis=0).T
    few = yrows // nz
    for k in range(nz):
        sl = slice(k * few, (k + 1) * few)
        R.zg_own[k] = jnp.concatenate([ysum[sl], tsum[sl]], axis=0).astype(BF16)
    for d in far_first(nz):
        z_copy(R.zg_own, R.zg_all, 4 * nz, zoff(d)).start()
    R.zg_all[iz] = R.zg_own[iz]

    share_part.wait_recv()
    R.gin[...] = (R.part_own_f[...] + R.part_in[...].astype(F32)).astype(BF16)

    z_wait(R.zg_own, R.zg_all, 4 * nz)
    gsum = R.zg_all[0].astype(F32)
    for k in range(1, nz):
        gsum = gsum + R.zg_all[k].astype(F32)
    norm = (q * nx * ny * nz) ** -0.5
    R.gbc[...] = gsum[:few, :] * norm
    R.gdt[...] = gsum[few:, :heads] * norm

    for c in every + group + [share_bc, share_half, share_part]:
        c.wait_send()
    for c in y_fwd + y_bwd + yg_copies + x_copies + s_copies:
        c.wait_send()
    z_drain(R.loc_own, R.loc_all, 0)
    z_drain(R.ent_own, R.held, nz)
    z_drain(R.term_own, R.term_all, 2 * nz)
    z_drain(R.lea_own, R.leav, 3 * nz)
    z_drain(R.zg_own, R.zg_all, 4 * nz)
    lax.fori_loop(1, nz, log_drain, 0)


def shards(mesh_shape, layer_in, out_grad, w_in, w_out, w_bc, w_dt, dt_bias, a_log, d_skip, norm_gain):
    nx, nc = mesh_shape
    heads = a_log.shape[0]
    nz = heads
    ny = nc // nz
    q, depth = layer_in.shape[1:]
    rows, units = w_in.shape
    nstate = w_bc.shape[1]
    width = units // heads
    yrows = rows // ny
    few = yrows // nz
    straight = 3 * rows // 8 // (8 * ny) * 8 * ny
    V = pltpu.VMEM
    dma = pltpu.SemaphoreType.DMA
    state = V((nz, width, nstate), BF16)
    full = V((q, units), F32)
    half = V((q, units), BF16)
    total = V((width + 16, nstate), BF16)
    totals = V((ny, width + 16, nstate), BF16)
    scratch = dict(
        x=V((q, depth), BF16),
        g=V((q, depth), BF16),
        wbc=V((rows, nstate), BF16),
        wdt=V((heads, rows), BF16),
        gain=V((1, units), F32),
        skip=V((1, heads), F32),
        bias=V((1, heads), F32),
        rate=V((1, heads), F32),
        skip_u=V((8, units), F32),
        win_all=V((nx, rows, units), BF16),
        wout_all=V((nx, rows, units), BF16),
        wbc_all=V((nx, rows, nstate), BF16),
        wdt_all=V((nx, 128, rows), BF16),
        codes=V((nx, rows, units), BF16),
        sums_own=V((16, 128), F32),
        sums_all=V((2 * nx, 16, 128), F32),
        bc_own=V((q, nstate), BF16),
        bc=V((2, q, nstate), BF16),
        log_own=V((1, 128), F32),
        logs=V((nz, 1, 128), F32),
        loc_own=state,
        loc_all=state,
        ent_own=state,
        held=state,
        term_own=state,
        term_all=state,
        lea_own=state,
        leav=state,
        fwd_own=total,
        fwd_all=totals,
        bwd_own=total,
        bwd_all=totals,
        x_all=V((nx, q, rows), BF16),
        sbc_own=V((q, nstate), BF16),
        sbc_all=V((nx, q, nstate), BF16),
        sdt_own=V((heads, q), BF16),
        sdt_all=V((nx, heads, q), BF16),
        ybc_own=V((ny, yrows, nstate), BF16),
        ybc_all=V((ny, yrows, nstate), BF16),
        ydt_own=V((ny, heads, yrows), BF16),
        ydt_all=V((ny, heads, yrows), BF16),
        zg_own=V((nz, 2 * few, nstate), BF16),
        zg_all=V((nz, 2 * few, nstate), BF16),
        half_own=V((q, nstate), BF16),
        half_in=V((q, nstate), BF16),
        part_own=V((q, depth // 2), BF16),
        part_in=V((q, depth // 2), BF16),
        part_own_f=V((q, depth // 2), F32),
        pre=full,
        values=half,
        weighted=half,
        weight_u=full,
        growth_u=full,
        cumt=V((128, q), F32),
        stept=V((128, q), F32),
        kern=V((heads, q, q), BF16),
        zmask=V((heads, q, q), F32),
        intra=full,
        grad=full,
        gbf=half,
        ggrown=half,
        iprod=full,
        colt=V((128, q), F32),
        fromintra=full,
        dec=V((nz, 128), F32),
        w_s=dma((72,)),
        w_r=dma((72,)),
        grp_s=dma((2 * nx,)),
        grp_r=dma((2 * nx,)),
        core_s=dma((3,)),
        core_r=dma((3,)),
        z_s=dma((6 * nz,)),
        z_r=dma((6 * nz,)),
        y_s=dma((4 * ny,)),
        y_r=dma((4 * ny,)),
        x_s=dma((3 * nx,)),
        x_r=dma((3 * nx,)),
        loc_s=dma((10,)),
        far=pltpu.SemaphoreType.REGULAR((2,)),
    )
    names = NAMES[13:]
    vm = pl.BlockSpec(memory_space=pltpu.VMEM)
    grad_in, grad_bc, grad_dt = pl.pallas_call(
        functools.partial(layer_kernel, nx, ny, nz, straight),
        out_shape=(
            jax.ShapeDtypeStruct((q, depth // 2), BF16),
            jax.ShapeDtypeStruct((few, nstate), F32),
            jax.ShapeDtypeStruct((few, heads), F32),
        ),
        in_specs=[pl.BlockSpec(memory_space=pltpu.HBM)] * 10,
        out_specs=(vm, vm, vm),
        scratch_shapes=[scratch[n] for n in names],
        compiler_params=pltpu.CompilerParams(
            collective_id=0, has_side_effects=True, vmem_limit_bytes=60 * 1024 * 1024
        ),
        name="ternary_layer",
    )(
        layer_in[0],
        out_grad[0],
        w_in,
        w_out,
        w_bc,
        w_dt.T,
        norm_gain[None],
        d_skip[None],
        dt_bias[None],
        a_log[None],
    )
    return (grad_in[None], grad_bc, grad_dt)


def solution(mesh):
    in_specs = (
        P("dp", "ctx", None),
        P("dp", "ctx", None),
        P("dp", "tensor"),
        P("dp", "tensor"),
        P("dp", "tensor"),
        P("dp", "tensor"),
        P("tensor"),
        P("tensor"),
        P("tensor"),
        P("tensor"),
    )
    out_specs = (P("dp", "ctx", "tensor"), P(("dp", "ctx"), "tensor"), P(("dp", "ctx"), "tensor"))
    body = functools.partial(shards, (mesh.shape["dp"], mesh.shape["ctx"]))
    return jax.shard_map(body, mesh=mesh, in_specs=in_specs, out_specs=out_specs, check_vma=False)
```

```python
import functools
import types

import jax
import jax.numpy as jnp
from jax import lax
from jax.experimental import pallas as pl
from jax.experimental.pallas import tpu as pltpu
from jax.sharding import PartitionSpec as P

GROUP = 256
CHUNKS = 2
MESH = pl.DeviceIdType.MESH
F32 = jnp.float32
BF16 = jnp.bfloat16
EXACT = lax.Precision.HIGHEST


def dot(a, b, ca=1, cb=0, precision=None):
    return lax.dot_general(
        a, b, (((ca,), (cb,)), ((), ())), precision=precision, preferred_element_type=F32
    )


NAMES = [
    "x_in", "g_in", "win", "wout", "wbc_in", "wdt_in", "gain_in", "skip_in",
    "bias_in", "rate_in", "gin", "gbc", "gdt", "x", "g", "wbc",
    "wdt", "gain", "skip", "bias", "rate", "skip_u", "win_all", "wout_all",
    "wbc_all", "wdt_all", "codes", "sums_own", "sums_all", "bc_own", "bc", "log_own",
    "logs", "loc_own", "loc_all", "ent_own", "held", "term_own", "term_all", "lea_own",
    "leav", "fwd_own", "fwd_all", "bwd_own", "bwd_all", "x_all", "sbc_own", "sbc_all",
    "sdt_own", "sdt_all", "ybc_own", "ybc_all", "ydt_own", "ydt_all", "zg_own", "zg_all",
    "half_own", "half_in", "part_own", "part_in", "part_own_f", "pre", "values", "weighted",
    "weight_u", "growth_u", "cumt", "stept", "kern", "zmask", "intra", "grad",
    "gbf", "ggrown", "iprod", "colt", "fromintra", "dec", "w_s", "w_r",
    "grp_s", "grp_r", "core_s", "core_r", "z_s", "z_r", "y_s", "y_r",
    "x_s", "x_r", "loc_s", "far", "x_turned",
]


def far_first(n):
    return sorted(range(1, n), key=lambda d: -min(d, n - d))


def layer_kernel(nx, ny, nz, straight, *refs):
    R = types.SimpleNamespace(**dict(zip(NAMES, refs, strict=True)))
    q, depth = R.x_in.shape
    rows, units = R.win.shape
    heads = nz
    width = units // heads
    nstate = R.wbc_in.shape[1]
    tile = min(256, units)
    ntile = units // tile
    hpt = tile // width
    ix = lax.axis_index("dp")
    ic = lax.axis_index("ctx")
    it = lax.axis_index("tensor")
    iz = lax.rem(ic, nz)
    iy = ic // nz
    other = 1 - it

    def dev(x=ix, y=iy, z=iz, t=it):
        return (x, y * nz + z, t)

    def remote(src, dst, ssem, rsem, device):
        return pltpu.make_async_remote_copy(
            src_ref=src,
            dst_ref=dst,
            send_sem=ssem,
            recv_sem=rsem,
            device_id=device,
            device_id_type=MESH,
        )

    def xoff(d):
        return lax.rem(ix + d, nx)

    def yoff(d):
        return lax.rem(iy + d, ny)

    def zoff(d):
        return lax.rem(iz + d, nz)

    barrier = pltpu.get_barrier_semaphore()
    count = 0

    for d in (1, nz - 1):
        pl.semaphore_signal(barrier, inc=1, device_id=dev(z=zoff(d)), device_id_type=MESH)
        count += 1
    for d in range(nx):
        for t in (it, other):
            if d == 0 and t is it:
                continue
            pl.semaphore_signal(barrier, inc=1, device_id=dev(x=xoff(d), t=t), device_id_type=MESH)
            count += 1
    for d in range(1, ny):
        pl.semaphore_signal(barrier, inc=1, device_id=dev(y=yoff(d)), device_id_type=MESH)
        count += 1

    loads = [
        pltpu.make_async_copy(src, dst, R.loc_s.at[k])
        for k, (src, dst) in enumerate(
            (
                (R.win, R.win_all.at[ix]),
                (R.wout, R.wout_all.at[ix]),
                (R.wbc_in, R.wbc),
                (R.wdt_in, R.wdt),
                (R.x_in, R.x),
                (R.bias_in, R.bias),
                (R.rate_in, R.rate),
                (R.gain_in, R.gain),
                (R.skip_in, R.skip),
                (R.g_in, R.g),
            )
        )
    ]
    for c in loads:
        c.start()

    def magnitude(ref):
        def one(i, acc):
            piece = jnp.abs(ref[ix, pl.ds(pl.multiple_of(i * 16, 16), 16), :].astype(F32))
            return acc + piece

        total = lax.fori_loop(0, rows // 16, one, jnp.zeros((16, units), F32))
        out = total[:8, :128] + total[8:, :128]
        for c in range(1, units // 128):
            out = out + total[:8, c * 128 : (c + 1) * 128] + total[8:, c * 128 : (c + 1) * 128]
        return out

    for k in range(nx):
        R.wdt_all[k, heads:, :] = jnp.zeros((128 - heads, rows), BF16)
    for c in loads:
        c.wait()
    pl.semaphore_wait(barrier, count)

    links = [0]
    every = []

    def link(src, dst, device):
        k = links[0]
        links[0] += 1
        c = remote(src, dst, R.w_s.at[k], R.w_r.at[k], device)
        every.append(c)
        return c

    class Ring:
        def __init__(self, n, own, place, before, after, right, left):
            self.relay = []
            if n == 2:
                self.first = [link(own(c), place(c), right) for c in range(2)]
                return
            self.first = [
                link(own(0), place(0), right),
                link(own(1), place(1), left),
                link(own(1), place(1), right),
                link(own(0), place(0), left),
            ]
            self.relay = [
                link(before(0), before(0), right),
                link(after(1), after(1), left),
            ]

        def start(self):
            for c in self.first:
                c.start()

        def forward(self):
            for k, c in enumerate(self.relay):
                self.first[k].wait_recv()
                c.start()

        def neighbours(self):
            for c in self.first[2:] if self.relay else self.first:
                c.wait_recv()

        def opposite(self):
            for c in self.relay:
                c.wait_recv()

    def x_ring(view, dst):
        return Ring(
            nx,
            lambda c: view(None, c),
            lambda c: view(dst.at[ix], c),
            lambda c: view(dst.at[xoff(nx - 1)], c),
            lambda c: view(dst.at[xoff(1)], c),
            dev(x=xoff(1)),
            dev(x=xoff(nx - 1)),
        )

    half_units = units // 2

    class Gather:
        def __init__(self, dst, straight):
            share = (rows - straight) // ny

            def part(first, count):
                def view(ref, c):
                    ref = dst.at[ix] if ref is None else ref
                    return ref.at[pl.ds(first, count), pl.ds(c * half_units, half_units)]

                return view

            def quarter(y):
                return part(pl.multiple_of(straight + y * share, 8), share)

            self.xb = x_ring(quarter(iy), dst)
            self.xa = x_ring(part(0, straight), dst)
            self.y = []
            for slot in (xoff(nx - 1), xoff(1), xoff(2)):
                at = dst.at[slot]
                mine = quarter(iy)
                self.y.append(
                    Ring(
                        ny,
                        lambda c, at=at: mine(at, c),
                        lambda c, at=at: mine(at, c),
                        lambda c, at=at: quarter(yoff(ny - 1))(at, c),
                        lambda c, at=at: quarter(yoff(1))(at, c),
                        dev(y=yoff(1)),
                        dev(y=yoff(ny - 1)),
                    )
                )

        def finish(self):
            self.xa.neighbours()
            self.xa.opposite()
            for ring in self.y:
                ring.neighbours()
                ring.opposite()

    by_rows = rows // 2
    ring_bc = x_ring(
        lambda ref, c: (R.wbc if ref is None else ref).at[pl.ds(c * by_rows, by_rows), :], R.wbc_all
    )
    ring_dt = x_ring(
        lambda ref, c: (
            R.wdt.at[:, pl.ds(c * by_rows, by_rows)]
            if ref is None
            else ref.at[pl.ds(0, heads), pl.ds(c * by_rows, by_rows)]
        ),
        R.wdt_all,
    )
    into = Gather(R.win_all, straight[0])
    outof = Gather(R.wout_all, straight[1])

    group = []
    for d in range(nx):
        for k, t in enumerate((it, other)):
            if d == 0 and k == 0:
                continue
            group.append(
                remote(
                    R.sums_own,
                    R.sums_all.at[2 * ix + it],
                    R.grp_s.at[2 * d + k],
                    R.grp_r.at[2 * d + k],
                    dev(x=xoff(d), t=t),
                )
            )

    into.xb.start()
    ring_bc.start()
    ring_dt.start()
    R.sums_own[0:8, :] = magnitude(R.win_all)
    R.sums_own[8:16, :] = magnitude(R.wout_all)
    for c in group:
        c.start()
    R.sums_all[2 * ix + it] = R.sums_own[...]
    R.wbc_all[ix] = R.wbc[...]
    R.wdt_all[ix, 0:heads, :] = R.wdt[...]
    into.xb.forward()
    into.xa.start()
    into.xb.neighbours()
    into.y[0].start()
    into.y[1].start()
    ring_bc.forward()
    ring_dt.forward()
    into.xb.opposite()
    into.y[2].start()
    def farther(r, carry):
        for k, d in enumerate((1, nz - 1)):
            pl.semaphore_signal(R.far.at[k], inc=1, device_id=dev(z=zoff(d)), device_id_type=MESH)
        for k in range(2):
            pl.semaphore_wait(R.far.at[k], 1)
        return carry

    lax.fori_loop(1, nz // 2, farther, 0)
    into.y[0].forward()
    into.xa.forward()
    into.y[1].forward()

    for ring in (ring_bc, ring_dt):
        ring.neighbours()
        ring.opposite()
    half_bc = jnp.zeros((q, nstate), F32)
    raw_step = jnp.zeros((q, 128), F32)
    for k in range(nx):
        piece = R.x[:, k * rows : (k + 1) * rows]
        half_bc = half_bc + dot(piece, R.wbc_all[k])
        raw_step = raw_step + dot(piece, R.wdt_all[k], 1, 1)
    R.bc_own[...] = half_bc.astype(BF16)
    share_bc = remote(R.bc_own, R.bc.at[it], R.core_s.at[0], R.core_r.at[0], dev(t=other))
    share_bc.start()
    R.bc[it] = R.bc_own[...]

    def lane_pad(v):
        return jnp.concatenate([v, jnp.zeros((1, 128 - heads), F32)], axis=1)

    raw_step = raw_step + lane_pad(R.bias[...])
    rate = -jnp.exp(lane_pad(R.rate[...]))
    step = jnp.maximum(raw_step, 0.0) + jnp.log1p(jnp.exp(-jnp.abs(raw_step)))
    ri = lax.broadcasted_iota(jnp.int32, (q, q), 0)
    ci = lax.broadcasted_iota(jnp.int32, (q, q), 1)
    causal = ri >= ci
    lower = jnp.where(causal, 1.0, 0.0).astype(F32)
    upper = jnp.where(ci >= ri, 1.0, 0.0).astype(F32)
    cum = dot(lower, step * rate, precision=EXACT)
    block_log = cum[q - 1 : q, :]
    R.log_own[...] = block_log

    def log_copy(d):
        return remote(
            R.log_own,
            R.logs.at[iz],
            R.z_s.at[4 * CHUNKS * nz + d],
            R.z_r.at[4 * CHUNKS * nz + d],
            dev(z=zoff(d)),
        )

    def log_start(d, carry):
        log_copy(d).start()
        return carry

    def log_wait(d, carry):
        log_copy(d).wait_recv()
        return carry

    def log_drain(d, carry):
        log_copy(d).wait_send()
        return carry

    lax.fori_loop(1, nz, log_start, 0)
    R.logs[iz] = R.log_own[...]
    into.y[2].forward()
    outof.xb.start()
    outof.xa.start()
    fade = jnp.exp(block_log - cum)
    weight = fade * step
    growth = jnp.exp(cum)
    R.cumt[...] = cum.T
    R.stept[...] = step.T
    eh = lax.broadcasted_iota(jnp.int32, (128, units), 0)
    eu = lax.broadcasted_iota(jnp.int32, (128, units), 1)
    expand = jnp.where(eu // width == eh, 1.0, 0.0).astype(BF16)

    def split(v):
        high = v.astype(BF16)
        return high, (v - high.astype(F32)).astype(BF16)

    def widen(v):
        high, rest = split(v)
        return dot(high, expand) + dot(rest, expand)

    R.weight_u[...] = widen(weight)
    R.growth_u[...] = widen(growth)
    R.skip_u[...] = dot(
        jnp.broadcast_to(lane_pad(R.skip[...]), (8, 128)), expand.astype(F32), precision=EXACT
    )

    for c in group:
        c.wait_recv()
    total = R.sums_all[0]
    for k in range(1, 2 * nx):
        total = total + R.sums_all[k]
    entries = 2.0 * nx * rows * units
    scale_in = jnp.sum(total[0:8, :]) / entries
    scale_out = jnp.sum(total[8:16, :]) / entries

    def ternary(w, scale):
        w = w.astype(F32)
        sign = jnp.where(w > 0.0, 1.0, -1.0)
        return jnp.where(jnp.abs(w) > 0.5 * scale, sign, 0.0).astype(BF16)

    share_bc.wait_recv()
    b_proj, c_proj = R.bc[0], R.bc[1]

    chunk = width // CHUNKS
    spans = [pl.ds(c * chunk, chunk) for c in range(CHUNKS)]

    def z_copy(pair, base, source, to, cell=None):
        own, all_ = pair
        src = own.at[to] if cell is None else own.at[to, spans[cell]]
        dst = all_.at[source] if cell is None else all_.at[source, spans[cell]]
        at = (base + (cell or 0)) * nz + lax.rem(to - source + nz, nz)
        return remote(src, dst, R.z_s.at[at], R.z_r.at[at], dev(z=to))

    def z_send(pair, base, to, near, cell):
        if not near:
            z_copy(pair, base, iz, to, cell).start()
            return

        @pl.when(to != iz)
        def _():
            z_copy(pair, base, iz, to, cell).start()

        @pl.when(to == iz)
        def _():
            pair[1][iz, spans[cell]] = pair[0][iz, spans[cell]]

    def z_wait_from(pair, base, source, near, cell):
        own, all_ = pair
        at = (base + cell) * nz + lax.rem(iz - source + nz, nz)
        copy = remote(
            own.at[source, spans[cell]],
            all_.at[source, spans[cell]],
            R.z_s.at[at],
            R.z_r.at[at],
            dev(z=source),
        )
        if not near:
            copy.wait_recv()
            return

        @pl.when(source != iz)
        def _():
            copy.wait_recv()

    def z_wait(pair, base, cell=None):
        def one(d, carry):
            z_copy(pair, base, iz, zoff(d), cell).wait_recv()
            return carry

        lax.fori_loop(1, nz, one, 0)

    def z_drain(pair, base, cell=None):
        def one(d, carry):
            z_copy(pair, base, iz, zoff(d), cell).wait_send()
            return carry

        lax.fori_loop(1, nz, one, 0)

    locs = (R.loc_own, R.loc_all)
    ents = (R.ent_own, R.held)
    terms = (R.term_own, R.term_all)
    leas = (R.lea_own, R.leav)
    at_loc, at_ent, at_term, at_lea = (CHUNKS * e for e in range(4))
    at_log, at_zg = 4 * CHUNKS, 4 * CHUNKS + 1

    offs = sorted(range(ntile), key=lambda d: -min(d, ntile - d))
    own_tile = iz // hpt

    def tiles():
        for off in offs:
            t = lax.rem(own_tile + off, ntile)
            yield t, pl.ds(pl.multiple_of(t * tile, tile), tile), off == 0

    into.finish()
    for t, cols, near in tiles():
        acc = jnp.zeros((q, tile), F32)
        for k in range(nx):
            code = ternary(R.win_all[k, :, cols], scale_in)
            R.codes[k, :, cols] = code
            acc = acc + dot(R.x[:, k * rows : (k + 1) * rows], code)
        v = scale_in * acc
        R.pre[:, cols] = v
        val = (v * lax.logistic(v)).astype(BF16)
        R.values[:, cols] = val
        wv = (val.astype(F32) * R.weight_u[:, cols]).astype(BF16)
        R.weighted[:, cols] = wv
        R.loc_own[pl.ds(t * hpt, hpt)] = (
            dot(wv, b_proj, 0, 0).astype(BF16).reshape(hpt, width, nstate)
        )
        for i in range(hpt):
            z_send(locs, at_loc, t * hpt + i, near, 0)
    outof.xb.forward()
    outof.xb.neighbours()
    outof.y[0].start()
    outof.y[1].start()
    for cell in range(1, CHUNKS):
        for t, cols, near in tiles():
            for i in range(hpt):
                z_send(locs, at_loc, t * hpt + i, near, cell)

    gram = dot(c_proj, b_proj, 1, 1)
    lane = ci
    left_half = lax.broadcasted_iota(jnp.int32, (q, 2 * width), 1) < width
    zero_pair = jnp.zeros((q, 2 * width), BF16)

    def pick(s, pair):
        return jnp.where(left_half, pair, zero_pair) if s == 0 else jnp.where(left_half, zero_pair, pair)

    def inside(p, carry):
        cols = pl.ds(pl.multiple_of(p * 2 * width, 2 * width), 2 * width)
        pair = R.values[:, cols]
        acc = jnp.zeros((q, 2 * width), F32)
        for s in range(2):
            h = 2 * p + s
            col = jnp.sum(jnp.where(lane == h, cum, 0.0), axis=1, keepdims=True)
            row = R.cumt[pl.ds(h, 1), :]
            mask = jnp.exp(jnp.where(causal, col - row, -jnp.inf)) * R.stept[pl.ds(h, 1), :]
            R.zmask[h] = mask
            kb = (gram * mask).astype(BF16)
            R.kern[h] = kb
            acc = acc + dot(kb, pick(s, pair))
        R.intra[:, cols] = acc
        return carry

    lax.fori_loop(0, heads // 2, inside, 0)
    outof.xb.opposite()
    outof.y[2].start()
    outof.xa.forward()
    for ring in outof.y:
        ring.forward()

    lax.fori_loop(1, nz, log_wait, 0)
    log_rows = R.logs[...].reshape(nz, 128)
    lane_z = lax.broadcasted_iota(jnp.int32, (nz, 128), 1)
    log_col = jnp.sum(jnp.where(lane_z == iz, log_rows, 0.0), axis=1, keepdims=True)
    R.dec[...] = jnp.broadcast_to(jnp.exp(log_col), (nz, 128))
    row_decay = jnp.broadcast_to(jnp.exp(jnp.sum(log_col)), (16, nstate))
    high, rest = split(row_decay)
    decay_rows = jnp.where(
        lax.broadcasted_iota(jnp.int32, (16, nstate), 0) < 8, high.astype(F32), rest.astype(F32)
    ).astype(BF16)

    def scan(arrived, own, total, totals, at, forward):
        copies = []
        for cell in range(CHUNKS):
            rows_of = spans[cell]

            def step_of(i, state):
                k = i if forward else nz - 1 - i
                return R.dec[pl.ds(k, 1), :] * state + arrived[1][k, rows_of].astype(F32)

            empty = jnp.zeros((chunk, nstate), F32)
            z_wait(arrived, at[0], cell)
            total[cell, 0:chunk, :] = lax.fori_loop(0, nz, step_of, empty).astype(BF16)
            total[cell, chunk:, :] = decay_rows
            mine = []
            for d in far_first(ny):
                sem = (at[1] + cell) * ny + d
                mine.append(
                    remote(
                        total.at[cell],
                        totals.at[cell, iy],
                        R.y_s.at[sem],
                        R.y_r.at[sem],
                        dev(y=yoff(d)),
                    )
                )
            for c in mine:
                c.start()
            totals[cell, iy] = total[cell]
            for c in mine:
                c.wait_recv()
            copies += mine
            state = empty
            for k in range(ny) if forward else range(ny - 1, -1, -1):
                tail = totals[cell, k, chunk:, :].astype(F32)
                factor = tail[0:1, :] + tail[8:9, :]
                grown = factor * state + totals[cell, k, 0:chunk, :].astype(F32)
                state = jnp.where(k < iy if forward else k > iy, grown, state)

            def emit(i, state):
                k = i if forward else nz - 1 - i
                own[0][k, rows_of] = state.astype(BF16)
                return step_of(i, state)

            lax.fori_loop(0, nz, emit, state)
            for off in offs:
                t = lax.rem(own_tile - off + ntile, ntile)
                for i in range(hpt):
                    z_send(own, at[2], t * hpt + i, off == 0, cell)
        return copies

    y_fwd = scan(locs, ents, R.fwd_own, R.fwd_all, (at_loc, 0, at_ent), True)

    x_copies = [
        remote(
            R.x.at[:, pl.ds(pl.multiple_of(xoff(d) * rows, rows), rows)],
            R.x_all.at[ix],
            R.x_s.at[d],
            R.x_r.at[d],
            dev(x=xoff(d)),
        )
        for d in range(1, nx)
    ]
    for c in x_copies:
        c.start()
    R.x_all[ix] = R.x[:, pl.ds(pl.multiple_of(ix * rows, rows), rows)]
    outof.finish()

    def project_out(j, carry):
        cols = pl.ds(pl.multiple_of(j * tile, tile), tile)
        acc = jnp.zeros((q, tile), F32)
        for k in range(nx):
            acc = acc + dot(
                R.g[:, k * rows : (k + 1) * rows], ternary(R.wout_all[k, :, cols], scale_out)
            )
        R.grad[:, cols] = scale_out * acc * R.gain[:, cols]
        return carry

    lax.fori_loop(0, ntile, project_out, 0)

    for t, cols, near in tiles():
        for i in range(hpt):
            for cell in range(CHUNKS):
                z_wait_from(ents, at_ent, t * hpt + i, near, cell)
        hb = R.held[pl.ds(t * hpt, hpt)].reshape(tile, nstate)
        grow = R.growth_u[:, cols]
        inter = grow * dot(c_proj, hb, 1, 1)
        output = R.intra[:, cols] + inter + R.skip_u[0:1, cols] * R.values[:, cols].astype(F32)
        scaled = R.grad[:, cols]
        pieces = []
        for g in range(tile // GROUP):
            sl = slice(g * GROUP, (g + 1) * GROUP)
            o, s = output[:, sl], scaled[:, sl]
            inverse = lax.rsqrt(jnp.mean(o * o, axis=1, keepdims=True) + 1e-05)
            mixed = jnp.mean(s * o, axis=1, keepdims=True)
            pieces.append(inverse * (s - o * (inverse * inverse) * mixed))
        grad_y = jnp.concatenate(pieces, axis=1) if len(pieces) > 1 else pieces[0]
        grown = (grad_y * grow).astype(BF16)
        R.term_own[pl.ds(t * hpt, hpt)] = (
            dot(grown, c_proj, 0, 0).astype(BF16).reshape(hpt, width, nstate)
        )
        for i in range(hpt):
            z_send(terms, at_term, t * hpt + i, near, 0)
        R.grad[:, cols] = grad_y
        R.gbf[:, cols] = grad_y.astype(BF16)
        R.ggrown[:, cols] = grown
        R.iprod[:, cols] = grad_y * inter

    for cell in range(1, CHUNKS):
        for t, cols, near in tiles():
            for i in range(hpt):
                z_send(terms, at_term, t * hpt + i, near, cell)

    def head_sum(v, e=expand):
        high, rest = split(v)
        return dot(high, e, 1, 1) + dot(rest, e, 1, 1)

    R.colt[...] = jnp.zeros((128, q), F32)

    def inside_back(p, carry):
        zsum, rsum = carry
        cols = pl.ds(pl.multiple_of(p * 2 * width, 2 * width), 2 * width)
        pair = R.values[:, cols]
        gpair = R.gbf[:, cols]
        acc = jnp.zeros((q, 2 * width), F32)
        for s in range(2):
            h = 2 * p + s
            picked = pick(s, gpair)
            z = dot(picked, pair, 1, 1) * R.zmask[h]
            zsum = zsum + z
            product = z * gram
            rs = jnp.sum(product, axis=1, keepdims=True)
            rsum = jnp.where(lane == h, rs, rsum)
            R.colt[pl.ds(h, 1), :] = jnp.sum(product, axis=0, keepdims=True)
            acc = acc + dot(R.kern[h], picked, 0, 0)
        R.fromintra[:, cols] = acc + R.skip_u[0:1, cols] * R.grad[:, cols]
        return (zsum, rsum)

    zero_q = jnp.zeros((q, q), F32)
    zsum, row_sums = lax.fori_loop(0, heads // 2, inside_back, (zero_q, zero_q))
    inter_sum = head_sum(R.iprod[...])
    col_sums = R.colt[...].T
    zsum = zsum.astype(BF16)
    grad_c = dot(zsum, b_proj) + dot(R.ggrown[...], R.held[...].reshape(units, nstate))
    grad_b = dot(zsum, c_proj, 0, 0)

    y_bwd = scan(terms, leas, R.bwd_own, R.bwd_all, (at_term, CHUNKS, at_lea), False)

    for c in x_copies:
        c.wait_recv()
    for k in range(nx):
        R.x_turned[k] = R.x_all[k].astype(F32).T.astype(BF16)

    grad_weight = jnp.zeros((q, 128), F32)
    state_dot = jnp.zeros((8, 128), F32)
    ones = jnp.ones((8, nstate), BF16)
    tile_head = lax.broadcasted_iota(jnp.int32, (128, tile), 0)
    tile_unit = lax.broadcasted_iota(jnp.int32, (128, tile), 1)
    for t, cols, near in tiles():
        for i in range(hpt):
            for cell in range(CHUNKS):
                z_wait_from(leas, at_lea, t * hpt + i, near, cell)
        lb = R.leav[pl.ds(t * hpt, hpt)].reshape(tile, nstate)
        hb = R.held[pl.ds(t * hpt, hpt)].reshape(tile, nstate)
        e = jnp.where(tile_unit // width + t * hpt == tile_head, 1.0, 0.0).astype(BF16)
        grad_b = grad_b + dot(R.weighted[:, cols], lb)
        gw = dot(b_proj, lb, 1, 1)
        grad_weight = grad_weight + head_sum(gw * R.values[:, cols].astype(F32), e)
        high, rest = split(lb.astype(F32) * hb.astype(F32))
        state_dot = state_dot + head_sum(dot(ones, high, 1, 1) + dot(ones, rest, 1, 1), e)
        R.iprod[:, cols] = gw

    R.half_own[...] = jnp.where(it == 0, grad_c, grad_b).astype(BF16)
    share_half = remote(R.half_own, R.half_in, R.core_s.at[1], R.core_r.at[1], dev(t=other))
    share_half.start()
    mine = jnp.where(it == 0, grad_b, grad_c)

    gw_w = grad_weight * weight
    grad_log = jnp.sum(gw_w, axis=0, keepdims=True) + jnp.exp(block_log) * state_dot[0:1, :]
    grad_cum = inter_sum + row_sums - col_sums - gw_w
    grad_cum = grad_cum + jnp.where(ri == q - 1, grad_log, 0.0)
    grad_rate = dot(upper, grad_cum, precision=EXACT)
    grad_step = col_sums / step + grad_weight * fade + rate * grad_rate
    grad_raw = jnp.where(lane < heads, grad_step * lax.logistic(raw_step), 0.0)
    R.sdt_own[...] = grad_raw.T[0:heads, :].astype(BF16)
    send_dt = grad_raw.astype(BF16)

    share_half.wait_recv()
    R.sbc_own[...] = (mine + R.half_in[...].astype(F32)).astype(BF16)
    s_copies = []
    for d in far_first(nx):
        for k, (own, all_) in enumerate(((R.sbc_own, R.sbc_all), (R.sdt_own, R.sdt_all))):
            at = nx * (k + 1) + d
            s_copies.append(
                remote(own, all_.at[ix], R.x_s.at[at], R.x_r.at[at], dev(x=xoff(d)))
            )
    for c in s_copies:
        c.start()
    R.sbc_all[ix] = R.sbc_own[...]
    R.sdt_all[ix] = R.sdt_own[...]

    def silu_back(j, carry):
        cols = pl.ds(pl.multiple_of(j * tile, tile), tile)
        grad_values = R.fromintra[:, cols] + R.iprod[:, cols] * R.weight_u[:, cols]
        v = R.pre[:, cols]
        sg = lax.logistic(v)
        R.gbf[:, cols] = (scale_in * (grad_values * sg * (1.0 + v * (1.0 - sg)))).astype(BF16)
        return carry

    lax.fori_loop(0, ntile, silu_back, 0)
    per = nx // 2

    def partial_in(side, j):
        k = side * per + j
        return (
            dot(R.gbf[...], R.codes[k], 1, 1)
            + dot(R.sbc_own[...], R.wbc_all[k], 1, 1)
            + dot(send_dt, R.wdt_all[k])
        )

    for j in range(per):
        R.part_own[:, j * rows : (j + 1) * rows] = partial_in(other, j).astype(BF16)
    share_part = remote(R.part_own, R.part_in, R.core_s.at[2], R.core_r.at[2], dev(t=other))
    share_part.start()

    for c in s_copies:
        c.wait_recv()
    grad_w = jnp.zeros((rows, nstate), F32)
    grad_t = jnp.zeros((heads, rows), F32)
    for k in range(nx):
        grad_w = grad_w + dot(R.x_turned[k], R.sbc_all[k])
        grad_t = grad_t + dot(R.sdt_all[k], R.x_all[k])
    yrows = rows // ny
    R.ybc_own[...] = grad_w.astype(BF16).reshape(ny, yrows, nstate)
    for k in range(ny):
        R.ydt_own[k] = grad_t[:, k * yrows : (k + 1) * yrows].astype(BF16)
    yg_copies = []
    for d in far_first(ny):
        for k, (own, all_) in enumerate(((R.ybc_own, R.ybc_all), (R.ydt_own, R.ydt_all))):
            at = ny * (k + 2 * CHUNKS) + d
            yg_copies.append(
                remote(own.at[yoff(d)], all_.at[iy], R.y_s.at[at], R.y_r.at[at], dev(y=yoff(d)))
            )
    for c in yg_copies:
        c.start()
    R.ybc_all[iy] = R.ybc_own[iy]
    R.ydt_all[iy] = R.ydt_own[iy]

    for j in range(per):
        R.part_own_f[:, j * rows : (j + 1) * rows] = partial_in(it, j)

    for c in yg_copies:
        c.wait_recv()
    ysum = R.ybc_all[0].astype(F32)
    tsum = R.ydt_all[0].astype(F32)
    for k in range(1, ny):
        ysum = ysum + R.ybc_all[k].astype(F32)
        tsum = tsum + R.ydt_all[k].astype(F32)
    tsum = jnp.concatenate([tsum, jnp.zeros((128 - heads, yrows), F32)], axis=0).T
    few = yrows // nz
    for k in range(nz):
        sl = slice(k * few, (k + 1) * few)
        R.zg_own[k] = jnp.concatenate([ysum[sl], tsum[sl]], axis=0).astype(BF16)
    for d in far_first(nz):
        z_copy((R.zg_own, R.zg_all), at_zg, iz, zoff(d)).start()
    R.zg_all[iz] = R.zg_own[iz]

    share_part.wait_recv()
    R.gin[...] = (R.part_own_f[...] + R.part_in[...].astype(F32)).astype(BF16)

    z_wait((R.zg_own, R.zg_all), at_zg)
    gsum = R.zg_all[0].astype(F32)
    for k in range(1, nz):
        gsum = gsum + R.zg_all[k].astype(F32)
    norm = (q * nx * ny * nz) ** -0.5
    R.gbc[...] = gsum[:few, :] * norm
    R.gdt[...] = gsum[few:, :heads] * norm

    for c in every + group + [share_bc, share_half, share_part]:
        c.wait_send()
    for c in y_fwd + y_bwd + yg_copies + x_copies + s_copies:
        c.wait_send()
    for cell in range(CHUNKS):
        z_drain(locs, at_loc, cell)
        z_drain(ents, at_ent, cell)
        z_drain(terms, at_term, cell)
        z_drain(leas, at_lea, cell)
    z_drain((R.zg_own, R.zg_all), at_zg)
    lax.fori_loop(1, nz, log_drain, 0)


def shards(mesh_shape, layer_in, out_grad, w_in, w_out, w_bc, w_dt, dt_bias, a_log, d_skip, norm_gain):
    nx, nc = mesh_shape
    heads = a_log.shape[0]
    nz = heads
    ny = nc // nz
    q, depth = layer_in.shape[1:]
    rows, units = w_in.shape
    nstate = w_bc.shape[1]
    width = units // heads
    yrows = rows // ny
    few = yrows // nz
    straight = [part * rows // 8 // (8 * ny) * 8 * ny for part in (3, 5)]
    V = pltpu.VMEM
    dma = pltpu.SemaphoreType.DMA
    state = V((nz, width, nstate), BF16)
    full = V((q, units), F32)
    half = V((q, units), BF16)
    total = V((CHUNKS, width // CHUNKS + 16, nstate), BF16)
    totals = V((CHUNKS, ny, width // CHUNKS + 16, nstate), BF16)
    scratch = dict(
        x=V((q, depth), BF16),
        g=V((q, depth), BF16),
        wbc=V((rows, nstate), BF16),
        wdt=V((heads, rows), BF16),
        gain=V((1, units), F32),
        skip=V((1, heads), F32),
        bias=V((1, heads), F32),
        rate=V((1, heads), F32),
        skip_u=V((8, units), F32),
        win_all=V((nx, rows, units), BF16),
        wout_all=V((nx, rows, units), BF16),
        wbc_all=V((nx, rows, nstate), BF16),
        wdt_all=V((nx, 128, rows), BF16),
        codes=V((nx, rows, units), BF16),
        sums_own=V((16, 128), F32),
        sums_all=V((2 * nx, 16, 128), F32),
        bc_own=V((q, nstate), BF16),
        bc=V((2, q, nstate), BF16),
        log_own=V((1, 128), F32),
        logs=V((nz, 1, 128), F32),
        loc_own=state,
        loc_all=state,
        ent_own=state,
        held=state,
        term_own=state,
        term_all=state,
        lea_own=state,
        leav=state,
        fwd_own=total,
        fwd_all=totals,
        bwd_own=total,
        bwd_all=totals,
        x_all=V((nx, q, rows), BF16),
        x_turned=V((nx, rows, q), BF16),
        sbc_own=V((q, nstate), BF16),
        sbc_all=V((nx, q, nstate), BF16),
        sdt_own=V((heads, q), BF16),
        sdt_all=V((nx, heads, q), BF16),
        ybc_own=V((ny, yrows, nstate), BF16),
        ybc_all=V((ny, yrows, nstate), BF16),
        ydt_own=V((ny, heads, yrows), BF16),
        ydt_all=V((ny, heads, yrows), BF16),
        zg_own=V((nz, 2 * few, nstate), BF16),
        zg_all=V((nz, 2 * few, nstate), BF16),
        half_own=V((q, nstate), BF16),
        half_in=V((q, nstate), BF16),
        part_own=V((q, depth // 2), BF16),
        part_in=V((q, depth // 2), BF16),
        part_own_f=V((q, depth // 2), F32),
        pre=full,
        values=half,
        weighted=half,
        weight_u=full,
        growth_u=full,
        cumt=V((128, q), F32),
        stept=V((128, q), F32),
        kern=V((heads, q, q), BF16),
        zmask=V((heads, q, q), F32),
        intra=full,
        grad=full,
        gbf=half,
        ggrown=half,
        iprod=full,
        colt=V((128, q), F32),
        fromintra=full,
        dec=V((nz, 128), F32),
        w_s=dma((72,)),
        w_r=dma((72,)),
        grp_s=dma((2 * nx,)),
        grp_r=dma((2 * nx,)),
        core_s=dma((3,)),
        core_r=dma((3,)),
        z_s=dma(((4 * CHUNKS + 2) * nz,)),
        z_r=dma(((4 * CHUNKS + 2) * nz,)),
        y_s=dma(((2 * CHUNKS + 2) * ny,)),
        y_r=dma(((2 * CHUNKS + 2) * ny,)),
        x_s=dma((3 * nx,)),
        x_r=dma((3 * nx,)),
        loc_s=dma((10,)),
        far=pltpu.SemaphoreType.REGULAR((2,)),
    )
    names = NAMES[13:]
    vm = pl.BlockSpec(memory_space=pltpu.VMEM)
    grad_in, grad_bc, grad_dt = pl.pallas_call(
        functools.partial(layer_kernel, nx, ny, nz, straight),
        out_shape=(
            jax.ShapeDtypeStruct((q, depth // 2), BF16),
            jax.ShapeDtypeStruct((few, nstate), F32),
            jax.ShapeDtypeStruct((few, heads), F32),
        ),
        in_specs=[pl.BlockSpec(memory_space=pltpu.HBM)] * 10,
        out_specs=(vm, vm, vm),
        scratch_shapes=[scratch[n] for n in names],
        compiler_params=pltpu.CompilerParams(
            collective_id=0, has_side_effects=True, vmem_limit_bytes=60 * 1024 * 1024
        ),
        name="ternary_layer",
    )(
        layer_in[0],
        out_grad[0],
        w_in,
        w_out,
        w_bc,
        w_dt.T,
        norm_gain[None],
        d_skip[None],
        dt_bias[None],
        a_log[None],
    )
    return (grad_in[None], grad_bc, grad_dt)


def solution(mesh):
    in_specs = (
        P("dp", "ctx", None),
        P("dp", "ctx", None),
        P("dp", "tensor"),
        P("dp", "tensor"),
        P("dp", "tensor"),
        P("dp", "tensor"),
        P("tensor"),
        P("tensor"),
        P("tensor"),
        P("tensor"),
    )
    out_specs = (P("dp", "ctx", "tensor"), P(("dp", "ctx"), "tensor"), P(("dp", "ctx"), "tensor"))
    body = functools.partial(shards, (mesh.shape["dp"], mesh.shape["ctx"]))
    return jax.shard_map(body, mesh=mesh, in_specs=in_specs, out_specs=out_specs, check_vma=False)
```

```python
import functools
import types

import jax
import jax.numpy as jnp
from jax import lax
from jax.experimental import pallas as pl
from jax.experimental.pallas import tpu as pltpu
from jax.sharding import PartitionSpec as P

GROUP = 256
CHUNKS = 1
MESH = pl.DeviceIdType.MESH
F32 = jnp.float32
BF16 = jnp.bfloat16
EXACT = lax.Precision.HIGHEST


def dot(a, b, ca=1, cb=0, precision=None):
    return lax.dot_general(
        a, b, (((ca,), (cb,)), ((), ())), precision=precision, preferred_element_type=F32
    )


NAMES = [
    "x_in", "g_in", "win", "wout", "wbc_in", "wdt_in", "gain_in", "skip_in",
    "bias_in", "rate_in", "gin", "gbc", "gdt", "x", "g", "wbc",
    "wdt", "gain", "skip", "bias", "rate", "skip_u", "win_all", "wout_all",
    "wbc_all", "wdt_all", "codes", "sums_own", "sums_all", "bc_own", "bc", "log_own",
    "logs", "loc_own", "loc_all", "ent_own", "held", "term_own", "term_all", "lea_own",
    "leav", "fwd_own", "fwd_all", "bwd_own", "bwd_all", "x_all", "sbc_own", "sbc_all",
    "sdt_own", "sdt_all", "ybc_own", "ybc_all", "ydt_own", "ydt_all", "zg_own", "zg_all",
    "half_own", "half_in", "part_own", "part_in", "part_own_f", "pre", "values", "weighted",
    "weight_u", "growth_u", "cumt", "stept", "kern", "zmask", "intra", "grad",
    "gbf", "ggrown", "iprod", "colt", "fromintra", "dec", "w_s", "w_r",
    "grp_s", "grp_r", "core_s", "core_r", "z_s", "z_r", "y_s", "y_r",
    "x_s", "x_r", "loc_s", "far", "x_turned",
]


def far_first(n):
    return sorted(range(1, n), key=lambda d: -min(d, n - d))


def layer_kernel(nx, ny, nz, straight, *refs):
    R = types.SimpleNamespace(**dict(zip(NAMES, refs, strict=True)))
    q, depth = R.x_in.shape
    rows, units = R.win.shape
    heads = nz
    width = units // heads
    nstate = R.wbc_in.shape[1]
    tile = min(256, units)
    ntile = units // tile
    hpt = tile // width
    ix = lax.axis_index("dp")
    ic = lax.axis_index("ctx")
    it = lax.axis_index("tensor")
    iz = lax.rem(ic, nz)
    iy = ic // nz
    other = 1 - it

    def dev(x=ix, y=iy, z=iz, t=it):
        return (x, y * nz + z, t)

    def remote(src, dst, ssem, rsem, device):
        return pltpu.make_async_remote_copy(
            src_ref=src,
            dst_ref=dst,
            send_sem=ssem,
            recv_sem=rsem,
            device_id=device,
            device_id_type=MESH,
        )

    def xoff(d):
        return lax.rem(ix + d, nx)

    def yoff(d):
        return lax.rem(iy + d, ny)

    def zoff(d):
        return lax.rem(iz + d, nz)

    barrier = pltpu.get_barrier_semaphore()
    count = 0

    for d in (1, nz - 1):
        pl.semaphore_signal(barrier, inc=1, device_id=dev(z=zoff(d)), device_id_type=MESH)
        count += 1
    for d in range(nx):
        for t in (it, other):
            if d == 0 and t is it:
                continue
            pl.semaphore_signal(barrier, inc=1, device_id=dev(x=xoff(d), t=t), device_id_type=MESH)
            count += 1
    for d in range(1, ny):
        pl.semaphore_signal(barrier, inc=1, device_id=dev(y=yoff(d)), device_id_type=MESH)
        count += 1

    loads = [
        pltpu.make_async_copy(src, dst, R.loc_s.at[k])
        for k, (src, dst) in enumerate(
            (
                (R.win, R.win_all.at[ix]),
                (R.wout, R.wout_all.at[ix]),
                (R.wbc_in, R.wbc),
                (R.wdt_in, R.wdt),
                (R.x_in, R.x),
                (R.bias_in, R.bias),
                (R.rate_in, R.rate),
                (R.gain_in, R.gain),
                (R.skip_in, R.skip),
                (R.g_in, R.g),
            )
        )
    ]
    for c in loads:
        c.start()

    def magnitude(ref):
        def one(i, acc):
            piece = jnp.abs(ref[ix, pl.ds(pl.multiple_of(i * 16, 16), 16), :].astype(F32))
            return acc + piece

        total = lax.fori_loop(0, rows // 16, one, jnp.zeros((16, units), F32))
        out = total[:8, :128] + total[8:, :128]
        for c in range(1, units // 128):
            out = out + total[:8, c * 128 : (c + 1) * 128] + total[8:, c * 128 : (c + 1) * 128]
        return out

    for k in range(nx):
        R.wdt_all[k, heads:, :] = jnp.zeros((128 - heads, rows), BF16)
    for c in loads:
        c.wait()
    pl.semaphore_wait(barrier, count)

    links = [0]
    every = []

    def link(src, dst, device):
        k = links[0]
        links[0] += 1
        c = remote(src, dst, R.w_s.at[k], R.w_r.at[k], device)
        every.append(c)
        return c

    class Ring:
        def __init__(self, n, own, place, before, after, right, left):
            self.relay = []
            if n == 2:
                self.first = [link(own(c), place(c), right) for c in range(2)]
                return
            self.first = [
                link(own(0), place(0), right),
                link(own(1), place(1), left),
                link(own(1), place(1), right),
                link(own(0), place(0), left),
            ]
            self.relay = [
                link(before(0), before(0), right),
                link(after(1), after(1), left),
            ]

        def start(self):
            for c in self.first:
                c.start()

        def forward(self):
            for k, c in enumerate(self.relay):
                self.first[k].wait_recv()
                c.start()

        def neighbours(self):
            for c in self.first[2:] if self.relay else self.first:
                c.wait_recv()

        def opposite(self):
            for c in self.relay:
                c.wait_recv()

    def x_ring(view, dst):
        return Ring(
            nx,
            lambda c: view(None, c),
            lambda c: view(dst.at[ix], c),
            lambda c: view(dst.at[xoff(nx - 1)], c),
            lambda c: view(dst.at[xoff(1)], c),
            dev(x=xoff(1)),
            dev(x=xoff(nx - 1)),
        )

    half_units = units // 2

    class Gather:
        def __init__(self, dst, straight):
            share = (rows - straight) // ny

            def part(first, count):
                def view(ref, c):
                    ref = dst.at[ix] if ref is None else ref
                    return ref.at[pl.ds(first, count), pl.ds(c * half_units, half_units)]

                return view

            def quarter(y):
                return part(pl.multiple_of(straight + y * share, 8), share)

            self.xb = x_ring(quarter(iy), dst)
            self.xa = x_ring(part(0, straight), dst)
            self.y = []
            for slot in (xoff(nx - 1), xoff(1), xoff(2)):
                at = dst.at[slot]
                mine = quarter(iy)
                self.y.append(
                    Ring(
                        ny,
                        lambda c, at=at: mine(at, c),
                        lambda c, at=at: mine(at, c),
                        lambda c, at=at: quarter(yoff(ny - 1))(at, c),
                        lambda c, at=at: quarter(yoff(1))(at, c),
                        dev(y=yoff(1)),
                        dev(y=yoff(ny - 1)),
                    )
                )

        def finish(self):
            self.xa.neighbours()
            self.xa.opposite()
            for ring in self.y:
                ring.neighbours()
                ring.opposite()

    by_rows = rows // 2
    ring_bc = x_ring(
        lambda ref, c: (R.wbc if ref is None else ref).at[pl.ds(c * by_rows, by_rows), :], R.wbc_all
    )
    ring_dt = x_ring(
        lambda ref, c: (
            R.wdt.at[:, pl.ds(c * by_rows, by_rows)]
            if ref is None
            else ref.at[pl.ds(0, heads), pl.ds(c * by_rows, by_rows)]
        ),
        R.wdt_all,
    )
    into = Gather(R.win_all, straight[0])
    outof = Gather(R.wout_all, straight[1])

    group = []
    for d in range(nx):
        for k, t in enumerate((it, other)):
            if d == 0 and k == 0:
                continue
            group.append(
                remote(
                    R.sums_own,
                    R.sums_all.at[2 * ix + it],
                    R.grp_s.at[2 * d + k],
                    R.grp_r.at[2 * d + k],
                    dev(x=xoff(d), t=t),
                )
            )

    into.xb.start()
    ring_bc.start()
    ring_dt.start()
    R.sums_own[0:8, :] = magnitude(R.win_all)
    R.sums_own[8:16, :] = magnitude(R.wout_all)
    for c in group:
        c.start()
    R.sums_all[2 * ix + it] = R.sums_own[...]
    R.wbc_all[ix] = R.wbc[...]
    R.wdt_all[ix, 0:heads, :] = R.wdt[...]
    into.xb.forward()
    into.xa.start()
    into.xb.neighbours()
    into.y[0].start()
    into.y[1].start()
    ring_bc.forward()
    ring_dt.forward()
    into.xb.opposite()
    into.y[2].start()
    def farther(r, carry):
        for k, d in enumerate((1, nz - 1)):
            pl.semaphore_signal(R.far.at[k], inc=1, device_id=dev(z=zoff(d)), device_id_type=MESH)
        for k in range(2):
            pl.semaphore_wait(R.far.at[k], 1)
        return carry

    lax.fori_loop(1, nz // 2, farther, 0)
    into.y[0].forward()
    into.xa.forward()
    outof.xb.start()
    outof.xa.start()
    into.y[1].forward()

    for ring in (ring_bc, ring_dt):
        ring.neighbours()
        ring.opposite()
    half_bc = jnp.zeros((q, nstate), F32)
    raw_step = jnp.zeros((q, 128), F32)
    for k in range(nx):
        piece = R.x[:, k * rows : (k + 1) * rows]
        half_bc = half_bc + dot(piece, R.wbc_all[k])
        raw_step = raw_step + dot(piece, R.wdt_all[k], 1, 1)
    R.bc_own[...] = half_bc.astype(BF16)
    share_bc = remote(R.bc_own, R.bc.at[it], R.core_s.at[0], R.core_r.at[0], dev(t=other))
    share_bc.start()
    R.bc[it] = R.bc_own[...]

    def lane_pad(v):
        return jnp.concatenate([v, jnp.zeros((1, 128 - heads), F32)], axis=1)

    raw_step = raw_step + lane_pad(R.bias[...])
    rate = -jnp.exp(lane_pad(R.rate[...]))
    step = jnp.maximum(raw_step, 0.0) + jnp.log1p(jnp.exp(-jnp.abs(raw_step)))
    ri = lax.broadcasted_iota(jnp.int32, (q, q), 0)
    ci = lax.broadcasted_iota(jnp.int32, (q, q), 1)
    causal = ri >= ci
    lower = jnp.where(causal, 1.0, 0.0).astype(F32)
    upper = jnp.where(ci >= ri, 1.0, 0.0).astype(F32)
    cum = dot(lower, step * rate, precision=EXACT)
    block_log = cum[q - 1 : q, :]
    R.log_own[...] = block_log

    def log_copy(d):
        return remote(
            R.log_own,
            R.logs.at[iz],
            R.z_s.at[4 * CHUNKS * nz + d],
            R.z_r.at[4 * CHUNKS * nz + d],
            dev(z=zoff(d)),
        )

    def log_start(d, carry):
        log_copy(d).start()
        return carry

    def log_wait(d, carry):
        log_copy(d).wait_recv()
        return carry

    def log_drain(d, carry):
        log_copy(d).wait_send()
        return carry

    lax.fori_loop(1, nz, log_start, 0)
    R.logs[iz] = R.log_own[...]
    into.y[2].forward()
    fade = jnp.exp(block_log - cum)
    weight = fade * step
    growth = jnp.exp(cum)
    R.cumt[...] = cum.T
    R.stept[...] = step.T
    eh = lax.broadcasted_iota(jnp.int32, (128, units), 0)
    eu = lax.broadcasted_iota(jnp.int32, (128, units), 1)
    expand = jnp.where(eu // width == eh, 1.0, 0.0).astype(BF16)

    def split(v):
        high = v.astype(BF16)
        return high, (v - high.astype(F32)).astype(BF16)

    def widen(v):
        high, rest = split(v)
        return dot(high, expand) + dot(rest, expand)

    R.weight_u[...] = widen(weight)
    R.growth_u[...] = widen(growth)
    R.skip_u[...] = dot(
        jnp.broadcast_to(lane_pad(R.skip[...]), (8, 128)), expand.astype(F32), precision=EXACT
    )

    for c in group:
        c.wait_recv()
    total = R.sums_all[0]
    for k in range(1, 2 * nx):
        total = total + R.sums_all[k]
    entries = 2.0 * nx * rows * units
    scale_in = jnp.sum(total[0:8, :]) / entries
    scale_out = jnp.sum(total[8:16, :]) / entries

    def ternary(w, scale):
        w = w.astype(F32)
        sign = jnp.where(w > 0.0, 1.0, -1.0)
        return jnp.where(jnp.abs(w) > 0.5 * scale, sign, 0.0).astype(BF16)

    share_bc.wait_recv()
    b_proj, c_proj = R.bc[0], R.bc[1]

    chunk = width // CHUNKS
    spans = [pl.ds(c * chunk, chunk) for c in range(CHUNKS)]

    def z_copy(pair, base, source, to, cell=None):
        own, all_ = pair
        src = own.at[to] if cell is None else own.at[to, spans[cell]]
        dst = all_.at[source] if cell is None else all_.at[source, spans[cell]]
        at = (base + (cell or 0)) * nz + lax.rem(to - source + nz, nz)
        return remote(src, dst, R.z_s.at[at], R.z_r.at[at], dev(z=to))

    def z_send(pair, base, to, near, cell):
        if not near:
            z_copy(pair, base, iz, to, cell).start()
            return

        @pl.when(to != iz)
        def _():
            z_copy(pair, base, iz, to, cell).start()

        @pl.when(to == iz)
        def _():
            pair[1][iz, spans[cell]] = pair[0][iz, spans[cell]]

    def z_wait_from(pair, base, source, near, cell):
        own, all_ = pair
        at = (base + cell) * nz + lax.rem(iz - source + nz, nz)
        copy = remote(
            own.at[source, spans[cell]],
            all_.at[source, spans[cell]],
            R.z_s.at[at],
            R.z_r.at[at],
            dev(z=source),
        )
        if not near:
            copy.wait_recv()
            return

        @pl.when(source != iz)
        def _():
            copy.wait_recv()

    def z_wait(pair, base, cell=None):
        def one(d, carry):
            z_copy(pair, base, iz, zoff(d), cell).wait_recv()
            return carry

        lax.fori_loop(1, nz, one, 0)

    def z_drain(pair, base, cell=None):
        def one(d, carry):
            z_copy(pair, base, iz, zoff(d), cell).wait_send()
            return carry

        lax.fori_loop(1, nz, one, 0)

    locs = (R.loc_own, R.loc_all)
    ents = (R.ent_own, R.held)
    terms = (R.term_own, R.term_all)
    leas = (R.lea_own, R.leav)
    at_loc, at_ent, at_term, at_lea = (CHUNKS * e for e in range(4))
    at_log, at_zg = 4 * CHUNKS, 4 * CHUNKS + 1

    offs = sorted(range(ntile), key=lambda d: -min(d, ntile - d))
    own_tile = iz // hpt

    def tiles():
        for off in offs:
            t = lax.rem(own_tile + off, ntile)
            yield t, pl.ds(pl.multiple_of(t * tile, tile), tile), off == 0

    outof.xb.forward()
    outof.xb.neighbours()
    outof.y[0].start()
    outof.y[1].start()
    into.finish()
    for t, cols, near in tiles():
        acc = jnp.zeros((q, tile), F32)
        for k in range(nx):
            code = ternary(R.win_all[k, :, cols], scale_in)
            R.codes[k, :, cols] = code
            acc = acc + dot(R.x[:, k * rows : (k + 1) * rows], code)
        v = scale_in * acc
        R.pre[:, cols] = v
        val = (v * lax.logistic(v)).astype(BF16)
        R.values[:, cols] = val
        wv = (val.astype(F32) * R.weight_u[:, cols]).astype(BF16)
        R.weighted[:, cols] = wv
        R.loc_own[pl.ds(t * hpt, hpt)] = (
            dot(wv, b_proj, 0, 0).astype(BF16).reshape(hpt, width, nstate)
        )
        for i in range(hpt):
            z_send(locs, at_loc, t * hpt + i, near, 0)
    for cell in range(1, CHUNKS):
        for t, cols, near in tiles():
            for i in range(hpt):
                z_send(locs, at_loc, t * hpt + i, near, cell)

    gram = dot(c_proj, b_proj, 1, 1)
    lane = ci
    left_half = lax.broadcasted_iota(jnp.int32, (q, 2 * width), 1) < width
    zero_pair = jnp.zeros((q, 2 * width), BF16)

    def pick(s, pair):
        return jnp.where(left_half, pair, zero_pair) if s == 0 else jnp.where(left_half, zero_pair, pair)

    def inside(p, carry):
        cols = pl.ds(pl.multiple_of(p * 2 * width, 2 * width), 2 * width)
        pair = R.values[:, cols]
        acc = jnp.zeros((q, 2 * width), F32)
        for s in range(2):
            h = 2 * p + s
            col = jnp.sum(jnp.where(lane == h, cum, 0.0), axis=1, keepdims=True)
            row = R.cumt[pl.ds(h, 1), :]
            mask = jnp.exp(jnp.where(causal, col - row, -jnp.inf)) * R.stept[pl.ds(h, 1), :]
            R.zmask[h] = mask
            kb = (gram * mask).astype(BF16)
            R.kern[h] = kb
            acc = acc + dot(kb, pick(s, pair))
        R.intra[:, cols] = acc
        return carry

    lax.fori_loop(0, heads // 2, inside, 0)
    outof.xb.opposite()
    outof.y[2].start()
    outof.xa.forward()
    for ring in outof.y:
        ring.forward()

    lax.fori_loop(1, nz, log_wait, 0)
    log_rows = R.logs[...].reshape(nz, 128)
    lane_z = lax.broadcasted_iota(jnp.int32, (nz, 128), 1)
    log_col = jnp.sum(jnp.where(lane_z == iz, log_rows, 0.0), axis=1, keepdims=True)
    R.dec[...] = jnp.broadcast_to(jnp.exp(log_col), (nz, 128))
    row_decay = jnp.broadcast_to(jnp.exp(jnp.sum(log_col)), (16, nstate))
    high, rest = split(row_decay)
    decay_rows = jnp.where(
        lax.broadcasted_iota(jnp.int32, (16, nstate), 0) < 8, high.astype(F32), rest.astype(F32)
    ).astype(BF16)

    def scan(arrived, own, total, totals, at, forward):
        copies = []
        for cell in range(CHUNKS):
            rows_of = spans[cell]

            def step_of(i, state):
                k = i if forward else nz - 1 - i
                return R.dec[pl.ds(k, 1), :] * state + arrived[1][k, rows_of].astype(F32)

            empty = jnp.zeros((chunk, nstate), F32)
            z_wait(arrived, at[0], cell)
            total[cell, 0:chunk, :] = lax.fori_loop(0, nz, step_of, empty, unroll=True).astype(BF16)
            total[cell, chunk:, :] = decay_rows
            mine = []
            for d in far_first(ny):
                sem = (at[1] + cell) * ny + d
                mine.append(
                    remote(
                        total.at[cell],
                        totals.at[cell, iy],
                        R.y_s.at[sem],
                        R.y_r.at[sem],
                        dev(y=yoff(d)),
                    )
                )
            for c in mine:
                c.start()
            totals[cell, iy] = total[cell]
            for c in mine:
                c.wait_recv()
            copies += mine
            state = empty
            for k in range(ny) if forward else range(ny - 1, -1, -1):
                tail = totals[cell, k, chunk:, :].astype(F32)
                factor = tail[0:1, :] + tail[8:9, :]
                grown = factor * state + totals[cell, k, 0:chunk, :].astype(F32)
                state = jnp.where(k < iy if forward else k > iy, grown, state)

            def emit(i, state):
                k = i if forward else nz - 1 - i
                own[0][k, rows_of] = state.astype(BF16)
                return step_of(i, state)

            lax.fori_loop(0, nz, emit, state, unroll=True)
            for off in offs:
                t = lax.rem(own_tile - off + ntile, ntile)
                for i in range(hpt):
                    z_send(own, at[2], t * hpt + i, off == 0, cell)
        return copies

    y_fwd = scan(locs, ents, R.fwd_own, R.fwd_all, (at_loc, 0, at_ent), True)

    x_copies = [
        remote(
            R.x.at[:, pl.ds(pl.multiple_of(xoff(d) * rows, rows), rows)],
            R.x_all.at[ix],
            R.x_s.at[d],
            R.x_r.at[d],
            dev(x=xoff(d)),
        )
        for d in range(1, nx)
    ]
    for c in x_copies:
        c.start()
    R.x_all[ix] = R.x[:, pl.ds(pl.multiple_of(ix * rows, rows), rows)]
    outof.finish()

    def project_out(j, carry):
        cols = pl.ds(pl.multiple_of(j * tile, tile), tile)
        acc = jnp.zeros((q, tile), F32)
        for k in range(nx):
            acc = acc + dot(
                R.g[:, k * rows : (k + 1) * rows], ternary(R.wout_all[k, :, cols], scale_out)
            )
        R.grad[:, cols] = scale_out * acc * R.gain[:, cols]
        return carry

    lax.fori_loop(0, ntile, project_out, 0)

    for t, cols, near in tiles():
        for i in range(hpt):
            for cell in range(CHUNKS):
                z_wait_from(ents, at_ent, t * hpt + i, near, cell)
        hb = R.held[pl.ds(t * hpt, hpt)].reshape(tile, nstate)
        grow = R.growth_u[:, cols]
        inter = grow * dot(c_proj, hb, 1, 1)
        output = R.intra[:, cols] + inter + R.skip_u[0:1, cols] * R.values[:, cols].astype(F32)
        scaled = R.grad[:, cols]
        pieces = []
        for g in range(tile // GROUP):
            sl = slice(g * GROUP, (g + 1) * GROUP)
            o, s = output[:, sl], scaled[:, sl]
            inverse = lax.rsqrt(jnp.mean(o * o, axis=1, keepdims=True) + 1e-05)
            mixed = jnp.mean(s * o, axis=1, keepdims=True)
            pieces.append(inverse * (s - o * (inverse * inverse) * mixed))
        grad_y = jnp.concatenate(pieces, axis=1) if len(pieces) > 1 else pieces[0]
        grown = (grad_y * grow).astype(BF16)
        R.term_own[pl.ds(t * hpt, hpt)] = (
            dot(grown, c_proj, 0, 0).astype(BF16).reshape(hpt, width, nstate)
        )
        for i in range(hpt):
            z_send(terms, at_term, t * hpt + i, near, 0)
        R.grad[:, cols] = grad_y
        R.gbf[:, cols] = grad_y.astype(BF16)
        R.ggrown[:, cols] = grown
        R.iprod[:, cols] = grad_y * inter

    for cell in range(1, CHUNKS):
        for t, cols, near in tiles():
            for i in range(hpt):
                z_send(terms, at_term, t * hpt + i, near, cell)

    def head_sum(v, e=expand):
        high, rest = split(v)
        return dot(high, e, 1, 1) + dot(rest, e, 1, 1)

    R.colt[...] = jnp.zeros((128, q), F32)

    def inside_back(p, carry):
        zsum, rsum = carry
        cols = pl.ds(pl.multiple_of(p * 2 * width, 2 * width), 2 * width)
        pair = R.values[:, cols]
        gpair = R.gbf[:, cols]
        acc = jnp.zeros((q, 2 * width), F32)
        for s in range(2):
            h = 2 * p + s
            picked = pick(s, gpair)
            z = dot(picked, pair, 1, 1) * R.zmask[h]
            zsum = zsum + z
            product = z * gram
            rs = jnp.sum(product, axis=1, keepdims=True)
            rsum = jnp.where(lane == h, rs, rsum)
            R.colt[pl.ds(h, 1), :] = jnp.sum(product, axis=0, keepdims=True)
            acc = acc + dot(R.kern[h], picked, 0, 0)
        R.fromintra[:, cols] = acc + R.skip_u[0:1, cols] * R.grad[:, cols]
        return (zsum, rsum)

    zero_q = jnp.zeros((q, q), F32)
    zsum, row_sums = lax.fori_loop(0, heads // 2, inside_back, (zero_q, zero_q))
    inter_sum = head_sum(R.iprod[...])
    col_sums = R.colt[...].T
    zsum = zsum.astype(BF16)
    grad_c = dot(zsum, b_proj) + dot(R.ggrown[...], R.held[...].reshape(units, nstate))
    grad_b = dot(zsum, c_proj, 0, 0)

    y_bwd = scan(terms, leas, R.bwd_own, R.bwd_all, (at_term, CHUNKS, at_lea), False)

    for c in x_copies:
        c.wait_recv()
    for k in range(nx):
        R.x_turned[k] = R.x_all[k].astype(F32).T.astype(BF16)

    grad_weight = jnp.zeros((q, 128), F32)
    state_dot = jnp.zeros((8, 128), F32)
    ones = jnp.ones((8, nstate), BF16)
    tile_head = lax.broadcasted_iota(jnp.int32, (128, tile), 0)
    tile_unit = lax.broadcasted_iota(jnp.int32, (128, tile), 1)
    for t, cols, near in tiles():
        for i in range(hpt):
            for cell in range(CHUNKS):
                z_wait_from(leas, at_lea, t * hpt + i, near, cell)
        lb = R.leav[pl.ds(t * hpt, hpt)].reshape(tile, nstate)
        hb = R.held[pl.ds(t * hpt, hpt)].reshape(tile, nstate)
        e = jnp.where(tile_unit // width + t * hpt == tile_head, 1.0, 0.0).astype(BF16)
        grad_b = grad_b + dot(R.weighted[:, cols], lb)
        gw = dot(b_proj, lb, 1, 1)
        grad_weight = grad_weight + head_sum(gw * R.values[:, cols].astype(F32), e)
        high, rest = split(lb.astype(F32) * hb.astype(F32))
        state_dot = state_dot + head_sum(dot(ones, high, 1, 1) + dot(ones, rest, 1, 1), e)
        R.iprod[:, cols] = gw

    R.half_own[...] = jnp.where(it == 0, grad_c, grad_b).astype(BF16)
    share_half = remote(R.half_own, R.half_in, R.core_s.at[1], R.core_r.at[1], dev(t=other))
    share_half.start()
    mine = jnp.where(it == 0, grad_b, grad_c)

    gw_w = grad_weight * weight
    grad_log = jnp.sum(gw_w, axis=0, keepdims=True) + jnp.exp(block_log) * state_dot[0:1, :]
    grad_cum = inter_sum + row_sums - col_sums - gw_w
    grad_cum = grad_cum + jnp.where(ri == q - 1, grad_log, 0.0)
    grad_rate = dot(upper, grad_cum, precision=EXACT)
    grad_step = col_sums / step + grad_weight * fade + rate * grad_rate
    grad_raw = jnp.where(lane < heads, grad_step * lax.logistic(raw_step), 0.0)
    R.sdt_own[...] = grad_raw.T[0:heads, :].astype(BF16)
    send_dt = grad_raw.astype(BF16)

    share_half.wait_recv()
    R.sbc_own[...] = (mine + R.half_in[...].astype(F32)).astype(BF16)
    s_copies = []
    for d in far_first(nx):
        for k, (own, all_) in enumerate(((R.sbc_own, R.sbc_all), (R.sdt_own, R.sdt_all))):
            at = nx * (k + 1) + d
            s_copies.append(
                remote(own, all_.at[ix], R.x_s.at[at], R.x_r.at[at], dev(x=xoff(d)))
            )
    for c in s_copies:
        c.start()
    R.sbc_all[ix] = R.sbc_own[...]
    R.sdt_all[ix] = R.sdt_own[...]

    def silu_back(j, carry):
        cols = pl.ds(pl.multiple_of(j * tile, tile), tile)
        grad_values = R.fromintra[:, cols] + R.iprod[:, cols] * R.weight_u[:, cols]
        v = R.pre[:, cols]
        sg = lax.logistic(v)
        R.gbf[:, cols] = (scale_in * (grad_values * sg * (1.0 + v * (1.0 - sg)))).astype(BF16)
        return carry

    lax.fori_loop(0, ntile, silu_back, 0)
    per = nx // 2

    def partial_in(side, j):
        k = side * per + j
        return (
            dot(R.gbf[...], R.codes[k], 1, 1)
            + dot(R.sbc_own[...], R.wbc_all[k], 1, 1)
            + dot(send_dt, R.wdt_all[k])
        )

    for j in range(per):
        R.part_own[:, j * rows : (j + 1) * rows] = partial_in(other, j).astype(BF16)
    share_part = remote(R.part_own, R.part_in, R.core_s.at[2], R.core_r.at[2], dev(t=other))
    share_part.start()

    for c in s_copies:
        c.wait_recv()
    grad_w = jnp.zeros((rows, nstate), F32)
    grad_t = jnp.zeros((heads, rows), F32)
    for k in range(nx):
        grad_w = grad_w + dot(R.x_turned[k], R.sbc_all[k])
        grad_t = grad_t + dot(R.sdt_all[k], R.x_all[k])
    yrows = rows // ny
    R.ybc_own[...] = grad_w.astype(BF16).reshape(ny, yrows, nstate)
    for k in range(ny):
        R.ydt_own[k] = grad_t[:, k * yrows : (k + 1) * yrows].astype(BF16)
    yg_copies = []
    for d in far_first(ny):
        for k, (own, all_) in enumerate(((R.ybc_own, R.ybc_all), (R.ydt_own, R.ydt_all))):
            at = ny * (k + 2 * CHUNKS) + d
            yg_copies.append(
                remote(own.at[yoff(d)], all_.at[iy], R.y_s.at[at], R.y_r.at[at], dev(y=yoff(d)))
            )
    for c in yg_copies:
        c.start()
    R.ybc_all[iy] = R.ybc_own[iy]
    R.ydt_all[iy] = R.ydt_own[iy]

    for j in range(per):
        R.part_own_f[:, j * rows : (j + 1) * rows] = partial_in(it, j)

    for c in yg_copies:
        c.wait_recv()
    ysum = R.ybc_all[0].astype(F32)
    tsum = R.ydt_all[0].astype(F32)
    for k in range(1, ny):
        ysum = ysum + R.ybc_all[k].astype(F32)
        tsum = tsum + R.ydt_all[k].astype(F32)
    tsum = jnp.concatenate([tsum, jnp.zeros((128 - heads, yrows), F32)], axis=0).T
    few = yrows // nz
    for k in range(nz):
        sl = slice(k * few, (k + 1) * few)
        R.zg_own[k] = jnp.concatenate([ysum[sl], tsum[sl]], axis=0).astype(BF16)
    for d in far_first(nz):
        z_copy((R.zg_own, R.zg_all), at_zg, iz, zoff(d)).start()
    R.zg_all[iz] = R.zg_own[iz]

    share_part.wait_recv()
    R.gin[...] = (R.part_own_f[...] + R.part_in[...].astype(F32)).astype(BF16)

    for c in every + group + [share_bc, share_half, share_part]:
        c.wait_send()
    for c in y_fwd + y_bwd + yg_copies + x_copies + s_copies:
        c.wait_send()
    for cell in range(CHUNKS):
        z_drain(locs, at_loc, cell)
        z_drain(ents, at_ent, cell)
        z_drain(terms, at_term, cell)
        z_drain(leas, at_lea, cell)
    lax.fori_loop(1, nz, log_drain, 0)

    z_wait((R.zg_own, R.zg_all), at_zg)
    gsum = R.zg_all[0].astype(F32)
    for k in range(1, nz):
        gsum = gsum + R.zg_all[k].astype(F32)
    norm = (q * nx * ny * nz) ** -0.5
    R.gbc[...] = gsum[:few, :] * norm
    R.gdt[...] = gsum[few:, :heads] * norm

    z_drain((R.zg_own, R.zg_all), at_zg)


def place_kernel(a, b, c, a_out, b_out, c_out):
    a_out[...] = a[...]
    b_out[...] = b[...]
    c_out[...] = c[...]


def shards(mesh_shape, layer_in, out_grad, w_in, w_out, w_bc, w_dt, dt_bias, a_log, d_skip, norm_gain):
    nx, nc = mesh_shape
    heads = a_log.shape[0]
    nz = heads
    ny = nc // nz
    q, depth = layer_in.shape[1:]
    rows, units = w_in.shape
    nstate = w_bc.shape[1]
    width = units // heads
    yrows = rows // ny
    few = yrows // nz
    straight = [part * rows // 16 // (8 * ny) * 8 * ny for part in (6, 6)]
    V = pltpu.VMEM
    dma = pltpu.SemaphoreType.DMA
    state = V((nz, width, nstate), BF16)
    full = V((q, units), F32)
    half = V((q, units), BF16)
    total = V((CHUNKS, width // CHUNKS + 16, nstate), BF16)
    totals = V((CHUNKS, ny, width // CHUNKS + 16, nstate), BF16)
    scratch = dict(
        x=V((q, depth), BF16),
        g=V((q, depth), BF16),
        wbc=V((rows, nstate), BF16),
        wdt=V((heads, rows), BF16),
        gain=V((1, units), F32),
        skip=V((1, heads), F32),
        bias=V((1, heads), F32),
        rate=V((1, heads), F32),
        skip_u=V((8, units), F32),
        win_all=V((nx, rows, units), BF16),
        wout_all=V((nx, rows, units), BF16),
        wbc_all=V((nx, rows, nstate), BF16),
        wdt_all=V((nx, 128, rows), BF16),
        codes=V((nx, rows, units), BF16),
        sums_own=V((16, 128), F32),
        sums_all=V((2 * nx, 16, 128), F32),
        bc_own=V((q, nstate), BF16),
        bc=V((2, q, nstate), BF16),
        log_own=V((1, 128), F32),
        logs=V((nz, 1, 128), F32),
        loc_own=state,
        loc_all=state,
        ent_own=state,
        held=state,
        term_own=state,
        term_all=state,
        lea_own=state,
        leav=state,
        fwd_own=total,
        fwd_all=totals,
        bwd_own=total,
        bwd_all=totals,
        x_all=V((nx, q, rows), BF16),
        x_turned=V((nx, rows, q), BF16),
        sbc_own=V((q, nstate), BF16),
        sbc_all=V((nx, q, nstate), BF16),
        sdt_own=V((heads, q), BF16),
        sdt_all=V((nx, heads, q), BF16),
        ybc_own=V((ny, yrows, nstate), BF16),
        ybc_all=V((ny, yrows, nstate), BF16),
        ydt_own=V((ny, heads, yrows), BF16),
        ydt_all=V((ny, heads, yrows), BF16),
        zg_own=V((nz, 2 * few, nstate), BF16),
        zg_all=V((nz, 2 * few, nstate), BF16),
        half_own=V((q, nstate), BF16),
        half_in=V((q, nstate), BF16),
        part_own=V((q, depth // 2), BF16),
        part_in=V((q, depth // 2), BF16),
        part_own_f=V((q, depth // 2), F32),
        pre=full,
        values=half,
        weighted=half,
        weight_u=full,
        growth_u=full,
        cumt=V((128, q), F32),
        stept=V((128, q), F32),
        kern=V((heads, q, q), BF16),
        zmask=V((heads, q, q), F32),
        intra=full,
        grad=full,
        gbf=half,
        ggrown=half,
        iprod=full,
        colt=V((128, q), F32),
        fromintra=full,
        dec=V((nz, 128), F32),
        w_s=dma((72,)),
        w_r=dma((72,)),
        grp_s=dma((2 * nx,)),
        grp_r=dma((2 * nx,)),
        core_s=dma((3,)),
        core_r=dma((3,)),
        z_s=dma(((4 * CHUNKS + 2) * nz,)),
        z_r=dma(((4 * CHUNKS + 2) * nz,)),
        y_s=dma(((2 * CHUNKS + 2) * ny,)),
        y_r=dma(((2 * CHUNKS + 2) * ny,)),
        x_s=dma((3 * nx,)),
        x_r=dma((3 * nx,)),
        loc_s=dma((10,)),
        far=pltpu.SemaphoreType.REGULAR((2,)),
    )
    names = NAMES[13:]
    vm = pl.BlockSpec(memory_space=pltpu.VMEM)
    grad_in, grad_bc, grad_dt = pl.pallas_call(
        functools.partial(layer_kernel, nx, ny, nz, straight),
        out_shape=(
            jax.ShapeDtypeStruct((q, depth // 2), BF16),
            jax.ShapeDtypeStruct((few, nstate), F32),
            jax.ShapeDtypeStruct((few, heads), F32),
        ),
        in_specs=[pl.BlockSpec(memory_space=pltpu.HBM)] * 10,
        out_specs=(vm, vm, vm),
        scratch_shapes=[scratch[n] for n in names],
        compiler_params=pltpu.CompilerParams(
            collective_id=0, has_side_effects=True, vmem_limit_bytes=60 * 1024 * 1024
        ),
        name="ternary_layer",
    )(
        layer_in[0],
        out_grad[0],
        w_in,
        w_out,
        w_bc,
        w_dt.T,
        norm_gain[None],
        d_skip[None],
        dt_bias[None],
        a_log[None],
    )
    outs = (grad_in, grad_bc, grad_dt)
    grad_in, grad_bc, grad_dt = pl.pallas_call(
        place_kernel,
        out_shape=tuple(jax.ShapeDtypeStruct(o.shape, o.dtype) for o in outs),
        in_specs=[vm] * 3,
        out_specs=(vm, vm, vm),
        name="place_outputs",
    )(*outs)
    return (grad_in[None], grad_bc, grad_dt)


def solution(mesh):
    in_specs = (
        P("dp", "ctx", None),
        P("dp", "ctx", None),
        P("dp", "tensor"),
        P("dp", "tensor"),
        P("dp", "tensor"),
        P("dp", "tensor"),
        P("tensor"),
        P("tensor"),
        P("tensor"),
        P("tensor"),
    )
    out_specs = (P("dp", "ctx", "tensor"), P(("dp", "ctx"), "tensor"), P(("dp", "ctx"), "tensor"))
    body = functools.partial(shards, (mesh.shape["dp"], mesh.shape["ctx"]))
    return jax.shard_map(body, mesh=mesh, in_specs=in_specs, out_specs=out_specs, check_vma=False)
```

```python
import functools
import types

import jax
import jax.numpy as jnp
from jax import lax
from jax.experimental import pallas as pl
from jax.experimental.pallas import tpu as pltpu
from jax.sharding import PartitionSpec as P

GROUP = 256
CHUNKS = 1
MESH = pl.DeviceIdType.MESH
F32 = jnp.float32
BF16 = jnp.bfloat16
EXACT = lax.Precision.HIGHEST


def dot(a, b, ca=1, cb=0, precision=None):
    return lax.dot_general(
        a, b, (((ca,), (cb,)), ((), ())), precision=precision, preferred_element_type=F32
    )


NAMES = [
    "x_in", "g_in", "win", "wout", "wbc_in", "wdt_in", "gain_in", "skip_in",
    "bias_in", "rate_in", "gin", "gbc", "gdt", "x", "g", "wbc",
    "wdt", "gain", "skip", "bias", "rate", "skip_u", "win_all", "wout_all",
    "wbc_all", "wdt_all", "codes", "sums_own", "sums_all", "bc_own", "bc", "log_own",
    "logs", "loc_own", "loc_all", "ent_own", "held", "term_own", "term_all", "lea_own",
    "leav", "fwd_own", "fwd_all", "bwd_own", "bwd_all", "x_all", "sbc_own", "sbc_all",
    "sdt_own", "sdt_all", "ybc_own", "ybc_all", "ydt_own", "ydt_all", "zg_own", "zg_all",
    "half_own", "half_in", "part_own", "part_in", "part_own_f", "pre", "values", "weighted",
    "weight_u", "growth_u", "cumt", "stept", "kern", "zmask", "intra", "grad",
    "gbf", "ggrown", "iprod", "colt", "fromintra", "dec", "w_s", "w_r",
    "grp_s", "grp_r", "core_s", "core_r", "z_s", "z_r", "y_s", "y_r",
    "x_s", "x_r", "loc_s", "far", "x_turned",
]


def far_first(n):
    return sorted(range(1, n), key=lambda d: -min(d, n - d))


def layer_kernel(nx, ny, nz, straight, *refs):
    R = types.SimpleNamespace(**dict(zip(NAMES, refs, strict=True)))
    q, depth = R.x_in.shape
    rows, units = R.win.shape
    heads = nz
    width = units // heads
    nstate = R.wbc_in.shape[1]
    tile = min(256, units)
    ntile = units // tile
    hpt = tile // width
    ix = lax.axis_index("dp")
    ic = lax.axis_index("ctx")
    it = lax.axis_index("tensor")
    iz = lax.rem(ic, nz)
    iy = ic // nz
    other = 1 - it

    def dev(x=ix, y=iy, z=iz, t=it):
        return (x, y * nz + z, t)

    def remote(src, dst, ssem, rsem, device):
        return pltpu.make_async_remote_copy(
            src_ref=src,
            dst_ref=dst,
            send_sem=ssem,
            recv_sem=rsem,
            device_id=device,
            device_id_type=MESH,
        )

    def xoff(d):
        return lax.rem(ix + d, nx)

    def yoff(d):
        return lax.rem(iy + d, ny)

    def zoff(d):
        return lax.rem(iz + d, nz)

    barrier = pltpu.get_barrier_semaphore()
    count = 0

    for d in (1, nz - 1):
        pl.semaphore_signal(barrier, inc=1, device_id=dev(z=zoff(d)), device_id_type=MESH)
        count += 1
    for d in range(nx):
        for t in (it, other):
            if d == 0 and t is it:
                continue
            pl.semaphore_signal(barrier, inc=1, device_id=dev(x=xoff(d), t=t), device_id_type=MESH)
            count += 1
    for d in range(1, ny):
        pl.semaphore_signal(barrier, inc=1, device_id=dev(y=yoff(d)), device_id_type=MESH)
        count += 1

    loads = [
        pltpu.make_async_copy(src, dst, R.loc_s.at[k])
        for k, (src, dst) in enumerate(
            (
                (R.win, R.win_all.at[ix]),
                (R.wout, R.wout_all.at[ix]),
                (R.wbc_in, R.wbc),
                (R.wdt_in, R.wdt),
                (R.x_in, R.x),
                (R.bias_in, R.bias),
                (R.rate_in, R.rate),
                (R.gain_in, R.gain),
                (R.skip_in, R.skip),
                (R.g_in, R.g),
            )
        )
    ]
    for c in loads:
        c.start()

    def magnitude(ref):
        def one(i, acc):
            piece = jnp.abs(ref[ix, pl.ds(pl.multiple_of(i * 16, 16), 16), :].astype(F32))
            return acc + piece

        total = lax.fori_loop(0, rows // 16, one, jnp.zeros((16, units), F32))
        out = total[:8, :128] + total[8:, :128]
        for c in range(1, units // 128):
            out = out + total[:8, c * 128 : (c + 1) * 128] + total[8:, c * 128 : (c + 1) * 128]
        return out

    for k in range(nx):
        R.wdt_all[k, heads:, :] = jnp.zeros((128 - heads, rows), BF16)
    for c in loads:
        c.wait()
    pl.semaphore_wait(barrier, count)

    links = [0]
    every = []

    def link(src, dst, device):
        k = links[0]
        links[0] += 1
        c = remote(src, dst, R.w_s.at[k], R.w_r.at[k], device)
        every.append(c)
        return c

    class Ring:
        def __init__(self, n, own, place, before, after, right, left):
            self.relay = []
            if n == 2:
                self.first = [link(own(c), place(c), right) for c in range(2)]
                return
            self.first = [
                link(own(0), place(0), right),
                link(own(1), place(1), left),
                link(own(1), place(1), right),
                link(own(0), place(0), left),
            ]
            self.relay = [
                link(before(0), before(0), right),
                link(after(1), after(1), left),
            ]

        def start(self):
            for c in self.first:
                c.start()

        def forward(self):
            for k, c in enumerate(self.relay):
                self.first[k].wait_recv()
                c.start()

        def neighbours(self):
            for c in self.first[2:] if self.relay else self.first:
                c.wait_recv()

        def opposite(self):
            for c in self.relay:
                c.wait_recv()

    def x_ring(view, dst):
        return Ring(
            nx,
            lambda c: view(None, c),
            lambda c: view(dst.at[ix], c),
            lambda c: view(dst.at[xoff(nx - 1)], c),
            lambda c: view(dst.at[xoff(1)], c),
            dev(x=xoff(1)),
            dev(x=xoff(nx - 1)),
        )

    half_units = units // 2

    class Gather:
        def __init__(self, dst, straight):
            share = (rows - straight) // ny

            def part(first, count):
                def view(ref, c):
                    ref = dst.at[ix] if ref is None else ref
                    return ref.at[pl.ds(first, count), pl.ds(c * half_units, half_units)]

                return view

            def quarter(y):
                return part(pl.multiple_of(straight + y * share, 8), share)

            self.xb = x_ring(quarter(iy), dst)
            self.xa = x_ring(part(0, straight), dst)
            self.y = []
            for slot in (xoff(nx - 1), xoff(1), xoff(2)):
                at = dst.at[slot]
                mine = quarter(iy)
                self.y.append(
                    Ring(
                        ny,
                        lambda c, at=at: mine(at, c),
                        lambda c, at=at: mine(at, c),
                        lambda c, at=at: quarter(yoff(ny - 1))(at, c),
                        lambda c, at=at: quarter(yoff(1))(at, c),
                        dev(y=yoff(1)),
                        dev(y=yoff(ny - 1)),
                    )
                )

        def finish(self):
            self.xa.neighbours()
            self.xa.opposite()
            for ring in self.y:
                ring.neighbours()
                ring.opposite()

    by_rows = rows // 2
    ring_bc = x_ring(
        lambda ref, c: (R.wbc if ref is None else ref).at[pl.ds(c * by_rows, by_rows), :], R.wbc_all
    )
    ring_dt = x_ring(
        lambda ref, c: (
            R.wdt.at[:, pl.ds(c * by_rows, by_rows)]
            if ref is None
            else ref.at[pl.ds(0, heads), pl.ds(c * by_rows, by_rows)]
        ),
        R.wdt_all,
    )
    into = Gather(R.win_all, straight[0])
    outof = Gather(R.wout_all, straight[1])

    group = []
    for d in range(nx):
        for k, t in enumerate((it, other)):
            if d == 0 and k == 0:
                continue
            group.append(
                remote(
                    R.sums_own,
                    R.sums_all.at[2 * ix + it],
                    R.grp_s.at[2 * d + k],
                    R.grp_r.at[2 * d + k],
                    dev(x=xoff(d), t=t),
                )
            )

    into.xb.start()
    ring_bc.start()
    ring_dt.start()
    R.sums_own[0:8, :] = magnitude(R.win_all)
    R.sums_own[8:16, :] = magnitude(R.wout_all)
    for c in group:
        c.start()
    R.sums_all[2 * ix + it] = R.sums_own[...]
    R.wbc_all[ix] = R.wbc[...]
    R.wdt_all[ix, 0:heads, :] = R.wdt[...]
    into.xb.forward()
    into.xa.start()
    into.xb.neighbours()
    into.y[0].start()
    into.y[1].start()
    ring_bc.forward()
    ring_dt.forward()
    into.xb.opposite()
    into.y[2].start()
    def farther(r, carry):
        for k, d in enumerate((1, nz - 1)):
            pl.semaphore_signal(R.far.at[k], inc=1, device_id=dev(z=zoff(d)), device_id_type=MESH)
        for k in range(2):
            pl.semaphore_wait(R.far.at[k], 1)
        return carry

    lax.fori_loop(1, nz // 2, farther, 0)
    into.y[0].forward()
    into.xa.forward()
    outof.xb.start()
    outof.xa.start()
    into.y[1].forward()

    for ring in (ring_bc, ring_dt):
        ring.neighbours()
        ring.opposite()
    half_bc = jnp.zeros((q, nstate), F32)
    raw_step = jnp.zeros((q, 128), F32)
    for k in range(nx):
        piece = R.x[:, k * rows : (k + 1) * rows]
        half_bc = half_bc + dot(piece, R.wbc_all[k])
        raw_step = raw_step + dot(piece, R.wdt_all[k], 1, 1)
    R.bc_own[...] = half_bc.astype(BF16)
    share_bc = remote(R.bc_own, R.bc.at[it], R.core_s.at[0], R.core_r.at[0], dev(t=other))
    share_bc.start()
    R.bc[it] = R.bc_own[...]

    def lane_pad(v):
        return jnp.concatenate([v, jnp.zeros((1, 128 - heads), F32)], axis=1)

    raw_step = raw_step + lane_pad(R.bias[...])
    rate = -jnp.exp(lane_pad(R.rate[...]))
    step = jnp.maximum(raw_step, 0.0) + jnp.log1p(jnp.exp(-jnp.abs(raw_step)))
    ri = lax.broadcasted_iota(jnp.int32, (q, q), 0)
    ci = lax.broadcasted_iota(jnp.int32, (q, q), 1)
    causal = ri >= ci
    lower = jnp.where(causal, 1.0, 0.0).astype(F32)
    upper = jnp.where(ci >= ri, 1.0, 0.0).astype(F32)
    cum = dot(lower, step * rate, precision=EXACT)
    block_log = cum[q - 1 : q, :]
    R.log_own[...] = block_log

    def log_copy(d):
        return remote(
            R.log_own,
            R.logs.at[iz],
            R.z_s.at[4 * CHUNKS * nz + d],
            R.z_r.at[4 * CHUNKS * nz + d],
            dev(z=zoff(d)),
        )

    def log_start(d, carry):
        log_copy(d).start()
        return carry

    def log_wait(d, carry):
        log_copy(d).wait_recv()
        return carry

    def log_drain(d, carry):
        log_copy(d).wait_send()
        return carry

    lax.fori_loop(1, nz, log_start, 0)
    R.logs[iz] = R.log_own[...]
    into.y[2].forward()
    fade = jnp.exp(block_log - cum)
    weight = fade * step
    growth = jnp.exp(cum)
    R.cumt[...] = cum.T
    R.stept[...] = step.T
    eh = lax.broadcasted_iota(jnp.int32, (128, units), 0)
    eu = lax.broadcasted_iota(jnp.int32, (128, units), 1)
    expand = jnp.where(eu // width == eh, 1.0, 0.0).astype(BF16)

    def split(v):
        high = v.astype(BF16)
        return high, (v - high.astype(F32)).astype(BF16)

    def widen(v):
        high, rest = split(v)
        return dot(high, expand) + dot(rest, expand)

    R.weight_u[...] = widen(weight)
    R.growth_u[...] = widen(growth)
    R.skip_u[...] = dot(
        jnp.broadcast_to(lane_pad(R.skip[...]), (8, 128)), expand.astype(F32), precision=EXACT
    )

    for c in group:
        c.wait_recv()
    total = R.sums_all[0]
    for k in range(1, 2 * nx):
        total = total + R.sums_all[k]
    entries = 2.0 * nx * rows * units
    scale_in = jnp.sum(total[0:8, :]) / entries
    scale_out = jnp.sum(total[8:16, :]) / entries

    def ternary(w, scale):
        w = w.astype(F32)
        sign = jnp.where(w > 0.0, 1.0, -1.0)
        return jnp.where(jnp.abs(w) > 0.5 * scale, sign, 0.0).astype(BF16)

    share_bc.wait_recv()
    b_proj, c_proj = R.bc[0], R.bc[1]

    chunk = width // CHUNKS
    spans = [pl.ds(c * chunk, chunk) for c in range(CHUNKS)]

    def z_copy(pair, base, source, to, cell=None):
        own, all_ = pair
        src = own.at[to] if cell is None else own.at[to, spans[cell]]
        dst = all_.at[source] if cell is None else all_.at[source, spans[cell]]
        at = (base + (cell or 0)) * nz + lax.rem(to - source + nz, nz)
        return remote(src, dst, R.z_s.at[at], R.z_r.at[at], dev(z=to))

    def z_send(pair, base, to, near, cell):
        if not near:
            z_copy(pair, base, iz, to, cell).start()
            return

        @pl.when(to != iz)
        def _():
            z_copy(pair, base, iz, to, cell).start()

        @pl.when(to == iz)
        def _():
            pair[1][iz, spans[cell]] = pair[0][iz, spans[cell]]

    def z_wait_from(pair, base, source, near, cell):
        own, all_ = pair
        at = (base + cell) * nz + lax.rem(iz - source + nz, nz)
        copy = remote(
            own.at[source, spans[cell]],
            all_.at[source, spans[cell]],
            R.z_s.at[at],
            R.z_r.at[at],
            dev(z=source),
        )
        if not near:
            copy.wait_recv()
            return

        @pl.when(source != iz)
        def _():
            copy.wait_recv()

    def z_wait(pair, base, cell=None):
        def one(d, carry):
            z_copy(pair, base, iz, zoff(d), cell).wait_recv()
            return carry

        lax.fori_loop(1, nz, one, 0, unroll=True)

    def z_drain(pair, base, cell=None):
        def one(d, carry):
            z_copy(pair, base, iz, zoff(d), cell).wait_send()
            return carry

        lax.fori_loop(1, nz, one, 0)

    locs = (R.loc_own, R.loc_all)
    ents = (R.ent_own, R.held)
    terms = (R.term_own, R.term_all)
    leas = (R.lea_own, R.leav)
    at_loc, at_ent, at_term, at_lea = (CHUNKS * e for e in range(4))
    at_log, at_zg = 4 * CHUNKS, 4 * CHUNKS + 1

    offs = sorted(range(ntile), key=lambda d: -min(d, ntile - d))
    own_tile = iz // hpt

    def tiles():
        for off in offs:
            t = lax.rem(own_tile + off, ntile)
            yield t, pl.ds(pl.multiple_of(t * tile, tile), tile), off == 0

    outof.xb.forward()
    outof.xb.neighbours()
    outof.y[0].start()
    outof.y[1].start()
    into.finish()
    for t, cols, near in tiles():
        acc = jnp.zeros((q, tile), F32)
        for k in range(nx):
            code = ternary(R.win_all[k, :, cols], scale_in)
            R.codes[k, :, cols] = code
            acc = acc + dot(R.x[:, k * rows : (k + 1) * rows], code)
        v = scale_in * acc
        R.pre[:, cols] = v
        val = (v * lax.logistic(v)).astype(BF16)
        R.values[:, cols] = val
        wv = (val.astype(F32) * R.weight_u[:, cols]).astype(BF16)
        R.weighted[:, cols] = wv
        R.loc_own[pl.ds(t * hpt, hpt)] = (
            dot(wv, b_proj, 0, 0).astype(BF16).reshape(hpt, width, nstate)
        )
        for i in range(hpt):
            z_send(locs, at_loc, t * hpt + lax.rem(iz + i, hpt), near, 0)
    for cell in range(1, CHUNKS):
        for t, cols, near in tiles():
            for i in range(hpt):
                z_send(locs, at_loc, t * hpt + lax.rem(iz + i, hpt), near, cell)

    gram = dot(c_proj, b_proj, 1, 1)
    lane = ci
    left_half = lax.broadcasted_iota(jnp.int32, (q, 2 * width), 1) < width
    zero_pair = jnp.zeros((q, 2 * width), BF16)

    def pick(s, pair):
        return jnp.where(left_half, pair, zero_pair) if s == 0 else jnp.where(left_half, zero_pair, pair)

    def inside(p, carry):
        cols = pl.ds(pl.multiple_of(p * 2 * width, 2 * width), 2 * width)
        pair = R.values[:, cols]
        acc = jnp.zeros((q, 2 * width), F32)
        for s in range(2):
            h = 2 * p + s
            col = jnp.sum(jnp.where(lane == h, cum, 0.0), axis=1, keepdims=True)
            row = R.cumt[pl.ds(h, 1), :]
            mask = jnp.exp(jnp.where(causal, col - row, -jnp.inf)) * R.stept[pl.ds(h, 1), :]
            R.zmask[h] = mask
            kb = (gram * mask).astype(BF16)
            R.kern[h] = kb
            acc = acc + dot(kb, pick(s, pair))
        R.intra[:, cols] = acc
        return carry

    outof.xb.opposite()
    outof.y[2].start()
    outof.y[0].forward()
    outof.y[1].forward()
    lax.fori_loop(0, heads // 2, inside, 0)
    outof.xa.forward()
    outof.y[2].forward()

    lax.fori_loop(1, nz, log_wait, 0, unroll=True)
    log_rows = R.logs[...].reshape(nz, 128)
    lane_z = lax.broadcasted_iota(jnp.int32, (nz, 128), 1)
    log_col = jnp.sum(jnp.where(lane_z == iz, log_rows, 0.0), axis=1, keepdims=True)
    R.dec[...] = jnp.broadcast_to(jnp.exp(log_col), (nz, 128))
    row_decay = jnp.broadcast_to(jnp.exp(jnp.sum(log_col)), (16, nstate))
    high, rest = split(row_decay)
    decay_rows = jnp.where(
        lax.broadcasted_iota(jnp.int32, (16, nstate), 0) < 8, high.astype(F32), rest.astype(F32)
    ).astype(BF16)

    def scan(arrived, own, total, totals, at, forward):
        copies = []
        for cell in range(CHUNKS):
            rows_of = spans[cell]

            def step_of(i, state):
                k = i if forward else nz - 1 - i
                return R.dec[pl.ds(k, 1), :] * state + arrived[1][k, rows_of].astype(F32)

            empty = jnp.zeros((chunk, nstate), F32)
            z_wait(arrived, at[0], cell)
            total[cell, 0:chunk, :] = lax.fori_loop(0, nz, step_of, empty, unroll=True).astype(BF16)
            total[cell, chunk:, :] = decay_rows
            mine = []
            for d in far_first(ny):
                sem = (at[1] + cell) * ny + d
                mine.append(
                    remote(
                        total.at[cell],
                        totals.at[cell, iy],
                        R.y_s.at[sem],
                        R.y_r.at[sem],
                        dev(y=yoff(d)),
                    )
                )
            for c in mine:
                c.start()
            totals[cell, iy] = total[cell]
            for c in mine:
                c.wait_recv()
            copies += mine
            state = empty
            for k in range(ny) if forward else range(ny - 1, -1, -1):
                tail = totals[cell, k, chunk:, :].astype(F32)
                factor = tail[0:1, :] + tail[8:9, :]
                grown = factor * state + totals[cell, k, 0:chunk, :].astype(F32)
                state = jnp.where(k < iy if forward else k > iy, grown, state)

            def emit(i, state):
                k = i if forward else nz - 1 - i
                own[0][k, rows_of] = state.astype(BF16)
                return step_of(i, state)

            lax.fori_loop(0, nz, emit, state, unroll=True)
            for off in offs:
                t = lax.rem(own_tile - off + ntile, ntile)
                for i in range(hpt):
                    z_send(own, at[2], t * hpt + lax.rem(iz + i, hpt), off == 0, cell)
        return copies

    y_fwd = scan(locs, ents, R.fwd_own, R.fwd_all, (at_loc, 0, at_ent), True)

    x_copies = [
        remote(
            R.x.at[:, pl.ds(pl.multiple_of(xoff(d) * rows, rows), rows)],
            R.x_all.at[ix],
            R.x_s.at[d],
            R.x_r.at[d],
            dev(x=xoff(d)),
        )
        for d in range(1, nx)
    ]
    for c in x_copies:
        c.start()
    R.x_all[ix] = R.x[:, pl.ds(pl.multiple_of(ix * rows, rows), rows)]
    outof.finish()

    def project_out(j, carry):
        cols = pl.ds(pl.multiple_of(j * tile, tile), tile)
        acc = jnp.zeros((q, tile), F32)
        for k in range(nx):
            acc = acc + dot(
                R.g[:, k * rows : (k + 1) * rows], ternary(R.wout_all[k, :, cols], scale_out)
            )
        R.grad[:, cols] = scale_out * acc * R.gain[:, cols]
        return carry

    lax.fori_loop(0, ntile, project_out, 0)

    for t, cols, near in tiles():
        for i in range(hpt):
            for cell in range(CHUNKS):
                z_wait_from(ents, at_ent, t * hpt + i, near, cell)
        hb = R.held[pl.ds(t * hpt, hpt)].reshape(tile, nstate)
        grow = R.growth_u[:, cols]
        inter = grow * dot(c_proj, hb, 1, 1)
        output = R.intra[:, cols] + inter + R.skip_u[0:1, cols] * R.values[:, cols].astype(F32)
        scaled = R.grad[:, cols]
        pieces = []
        for g in range(tile // GROUP):
            sl = slice(g * GROUP, (g + 1) * GROUP)
            o, s = output[:, sl], scaled[:, sl]
            inverse = lax.rsqrt(jnp.mean(o * o, axis=1, keepdims=True) + 1e-05)
            mixed = jnp.mean(s * o, axis=1, keepdims=True)
            pieces.append(inverse * (s - o * (inverse * inverse) * mixed))
        grad_y = jnp.concatenate(pieces, axis=1) if len(pieces) > 1 else pieces[0]
        grown = (grad_y * grow).astype(BF16)
        R.term_own[pl.ds(t * hpt, hpt)] = (
            dot(grown, c_proj, 0, 0).astype(BF16).reshape(hpt, width, nstate)
        )
        for i in range(hpt):
            z_send(terms, at_term, t * hpt + lax.rem(iz + i, hpt), near, 0)
        R.grad[:, cols] = grad_y
        R.gbf[:, cols] = grad_y.astype(BF16)
        R.ggrown[:, cols] = grown
        R.iprod[:, cols] = grad_y * inter

    for cell in range(1, CHUNKS):
        for t, cols, near in tiles():
            for i in range(hpt):
                z_send(terms, at_term, t * hpt + lax.rem(iz + i, hpt), near, cell)

    def head_sum(v, e=expand):
        high, rest = split(v)
        return dot(high, e, 1, 1) + dot(rest, e, 1, 1)

    R.colt[...] = jnp.zeros((128, q), F32)

    def inside_back(p, carry):
        zsum, rsum = carry
        cols = pl.ds(pl.multiple_of(p * 2 * width, 2 * width), 2 * width)
        pair = R.values[:, cols]
        gpair = R.gbf[:, cols]
        acc = jnp.zeros((q, 2 * width), F32)
        for s in range(2):
            h = 2 * p + s
            picked = pick(s, gpair)
            z = dot(picked, pair, 1, 1) * R.zmask[h]
            zsum = zsum + z
            product = z * gram
            rs = jnp.sum(product, axis=1, keepdims=True)
            rsum = jnp.where(lane == h, rs, rsum)
            R.colt[pl.ds(h, 1), :] = jnp.sum(product, axis=0, keepdims=True)
            acc = acc + dot(R.kern[h], picked, 0, 0)
        R.fromintra[:, cols] = acc + R.skip_u[0:1, cols] * R.grad[:, cols]
        return (zsum, rsum)

    zero_q = jnp.zeros((q, q), F32)
    zsum, row_sums = lax.fori_loop(0, heads // 2, inside_back, (zero_q, zero_q))
    inter_sum = head_sum(R.iprod[...])
    col_sums = R.colt[...].T
    zsum = zsum.astype(BF16)
    grad_c = dot(zsum, b_proj) + dot(R.ggrown[...], R.held[...].reshape(units, nstate))
    grad_b = dot(zsum, c_proj, 0, 0)

    y_bwd = scan(terms, leas, R.bwd_own, R.bwd_all, (at_term, CHUNKS, at_lea), False)

    for c in x_copies:
        c.wait_recv()
    for k in range(nx):
        R.x_turned[k] = R.x_all[k].astype(F32).T.astype(BF16)

    grad_weight = jnp.zeros((q, 128), F32)
    state_dot = jnp.zeros((8, 128), F32)
    ones = jnp.ones((8, nstate), BF16)
    tile_head = lax.broadcasted_iota(jnp.int32, (128, tile), 0)
    tile_unit = lax.broadcasted_iota(jnp.int32, (128, tile), 1)
    for t, cols, near in tiles():
        for i in range(hpt):
            for cell in range(CHUNKS):
                z_wait_from(leas, at_lea, t * hpt + i, near, cell)
        lb = R.leav[pl.ds(t * hpt, hpt)].reshape(tile, nstate)
        hb = R.held[pl.ds(t * hpt, hpt)].reshape(tile, nstate)
        e = jnp.where(tile_unit // width + t * hpt == tile_head, 1.0, 0.0).astype(BF16)
        grad_b = grad_b + dot(R.weighted[:, cols], lb)
        gw = dot(b_proj, lb, 1, 1)
        grad_weight = grad_weight + head_sum(gw * R.values[:, cols].astype(F32), e)
        high, rest = split(lb.astype(F32) * hb.astype(F32))
        state_dot = state_dot + head_sum(dot(ones, high, 1, 1) + dot(ones, rest, 1, 1), e)
        R.iprod[:, cols] = gw

    R.half_own[...] = jnp.where(it == 0, grad_c, grad_b).astype(BF16)
    share_half = remote(R.half_own, R.half_in, R.core_s.at[1], R.core_r.at[1], dev(t=other))
    share_half.start()
    mine = jnp.where(it == 0, grad_b, grad_c)

    gw_w = grad_weight * weight
    grad_log = jnp.sum(gw_w, axis=0, keepdims=True) + jnp.exp(block_log) * state_dot[0:1, :]
    grad_cum = inter_sum + row_sums - col_sums - gw_w
    grad_cum = grad_cum + jnp.where(ri == q - 1, grad_log, 0.0)
    grad_rate = dot(upper, grad_cum, precision=EXACT)
    grad_step = col_sums / step + grad_weight * fade + rate * grad_rate
    grad_raw = jnp.where(lane < heads, grad_step * lax.logistic(raw_step), 0.0)
    R.sdt_own[...] = grad_raw.T[0:heads, :].astype(BF16)
    send_dt = grad_raw.astype(BF16)

    share_half.wait_recv()
    R.sbc_own[...] = (mine + R.half_in[...].astype(F32)).astype(BF16)
    s_copies = []
    for d in far_first(nx):
        for k, (own, all_) in enumerate(((R.sbc_own, R.sbc_all), (R.sdt_own, R.sdt_all))):
            at = nx * (k + 1) + d
            s_copies.append(
                remote(own, all_.at[ix], R.x_s.at[at], R.x_r.at[at], dev(x=xoff(d)))
            )
    for c in s_copies:
        c.start()
    R.sbc_all[ix] = R.sbc_own[...]
    R.sdt_all[ix] = R.sdt_own[...]

    def silu_back(j, carry):
        cols = pl.ds(pl.multiple_of(j * tile, tile), tile)
        grad_values = R.fromintra[:, cols] + R.iprod[:, cols] * R.weight_u[:, cols]
        v = R.pre[:, cols]
        sg = lax.logistic(v)
        R.gbf[:, cols] = (scale_in * (grad_values * sg * (1.0 + v * (1.0 - sg)))).astype(BF16)
        return carry

    lax.fori_loop(0, ntile, silu_back, 0)
    per = nx // 2

    def partial_in(side, j):
        k = side * per + j
        return (
            dot(R.gbf[...], R.codes[k], 1, 1)
            + dot(R.sbc_own[...], R.wbc_all[k], 1, 1)
            + dot(send_dt, R.wdt_all[k])
        )

    for j in range(per):
        R.part_own[:, j * rows : (j + 1) * rows] = partial_in(other, j).astype(BF16)
    share_part = remote(R.part_own, R.part_in, R.core_s.at[2], R.core_r.at[2], dev(t=other))
    share_part.start()

    for c in s_copies:
        c.wait_recv()
    grad_w = jnp.zeros((rows, nstate), F32)
    grad_t = jnp.zeros((heads, rows), F32)
    for k in range(nx):
        grad_w = grad_w + dot(R.x_turned[k], R.sbc_all[k])
        grad_t = grad_t + dot(R.sdt_all[k], R.x_all[k])
    yrows = rows // ny
    R.ybc_own[...] = grad_w.astype(BF16).reshape(ny, yrows, nstate)
    for k in range(ny):
        R.ydt_own[k] = grad_t[:, k * yrows : (k + 1) * yrows].astype(BF16)
    yg_copies = []
    for d in far_first(ny):
        for k, (own, all_) in enumerate(((R.ybc_own, R.ybc_all), (R.ydt_own, R.ydt_all))):
            at = ny * (k + 2 * CHUNKS) + d
            yg_copies.append(
                remote(own.at[yoff(d)], all_.at[iy], R.y_s.at[at], R.y_r.at[at], dev(y=yoff(d)))
            )
    for c in yg_copies:
        c.start()
    R.ybc_all[iy] = R.ybc_own[iy]
    R.ydt_all[iy] = R.ydt_own[iy]

    for j in range(per):
        R.part_own_f[:, j * rows : (j + 1) * rows] = partial_in(it, j)

    for c in yg_copies:
        c.wait_recv()
    ysum = R.ybc_all[0].astype(F32)
    tsum = R.ydt_all[0].astype(F32)
    for k in range(1, ny):
        ysum = ysum + R.ybc_all[k].astype(F32)
        tsum = tsum + R.ydt_all[k].astype(F32)
    tsum = jnp.concatenate([tsum, jnp.zeros((128 - heads, yrows), F32)], axis=0).T
    few = yrows // nz
    for k in range(nz):
        sl = slice(k * few, (k + 1) * few)
        R.zg_own[k] = jnp.concatenate([ysum[sl], tsum[sl]], axis=0).astype(BF16)
    for d in far_first(nz):
        z_copy((R.zg_own, R.zg_all), at_zg, iz, zoff(d)).start()
    R.zg_all[iz] = R.zg_own[iz]

    share_part.wait_recv()
    R.gin[...] = (R.part_own_f[...] + R.part_in[...].astype(F32)).astype(BF16)

    for c in every + group + [share_bc, share_half, share_part]:
        c.wait_send()
    for c in y_fwd + y_bwd + yg_copies + x_copies + s_copies:
        c.wait_send()
    for cell in range(CHUNKS):
        z_drain(locs, at_loc, cell)
        z_drain(ents, at_ent, cell)
        z_drain(terms, at_term, cell)
        z_drain(leas, at_lea, cell)
    lax.fori_loop(1, nz, log_drain, 0)

    z_wait((R.zg_own, R.zg_all), at_zg)
    gsum = R.zg_all[0].astype(F32)
    for k in range(1, nz):
        gsum = gsum + R.zg_all[k].astype(F32)
    norm = (q * nx * ny * nz) ** -0.5
    R.gbc[...] = gsum[:few, :] * norm
    R.gdt[...] = gsum[few:, :heads] * norm

    z_drain((R.zg_own, R.zg_all), at_zg)


def place_kernel(a, b, c, a_out, b_out, c_out):
    a_out[...] = a[...]
    b_out[...] = b[...]
    c_out[...] = c[...]


def shards(mesh_shape, layer_in, out_grad, w_in, w_out, w_bc, w_dt, dt_bias, a_log, d_skip, norm_gain):
    nx, nc = mesh_shape
    heads = a_log.shape[0]
    nz = heads
    ny = nc // nz
    q, depth = layer_in.shape[1:]
    rows, units = w_in.shape
    nstate = w_bc.shape[1]
    width = units // heads
    yrows = rows // ny
    few = yrows // nz
    straight = [part * rows // 16 // (8 * ny) * 8 * ny for part in (6, 6)]
    V = pltpu.VMEM
    dma = pltpu.SemaphoreType.DMA
    state = V((nz, width, nstate), BF16)
    full = V((q, units), F32)
    half = V((q, units), BF16)
    total = V((CHUNKS, width // CHUNKS + 16, nstate), BF16)
    totals = V((CHUNKS, ny, width // CHUNKS + 16, nstate), BF16)
    scratch = dict(
        x=V((q, depth), BF16),
        g=V((q, depth), BF16),
        wbc=V((rows, nstate), BF16),
        wdt=V((heads, rows), BF16),
        gain=V((1, units), F32),
        skip=V((1, heads), F32),
        bias=V((1, heads), F32),
        rate=V((1, heads), F32),
        skip_u=V((8, units), F32),
        win_all=V((nx, rows, units), BF16),
        wout_all=V((nx, rows, units), BF16),
        wbc_all=V((nx, rows, nstate), BF16),
        wdt_all=V((nx, 128, rows), BF16),
        codes=V((nx, rows, units), BF16),
        sums_own=V((16, 128), F32),
        sums_all=V((2 * nx, 16, 128), F32),
        bc_own=V((q, nstate), BF16),
        bc=V((2, q, nstate), BF16),
        log_own=V((1, 128), F32),
        logs=V((nz, 1, 128), F32),
        loc_own=state,
        loc_all=state,
        ent_own=state,
        held=state,
        term_own=state,
        term_all=state,
        lea_own=state,
        leav=state,
        fwd_own=total,
        fwd_all=totals,
        bwd_own=total,
        bwd_all=totals,
        x_all=V((nx, q, rows), BF16),
        x_turned=V((nx, rows, q), BF16),
        sbc_own=V((q, nstate), BF16),
        sbc_all=V((nx, q, nstate), BF16),
        sdt_own=V((heads, q), BF16),
        sdt_all=V((nx, heads, q), BF16),
        ybc_own=V((ny, yrows, nstate), BF16),
        ybc_all=V((ny, yrows, nstate), BF16),
        ydt_own=V((ny, heads, yrows), BF16),
        ydt_all=V((ny, heads, yrows), BF16),
        zg_own=V((nz, 2 * few, nstate), BF16),
        zg_all=V((nz, 2 * few, nstate), BF16),
        half_own=V((q, nstate), BF16),
        half_in=V((q, nstate), BF16),
        part_own=V((q, depth // 2), BF16),
        part_in=V((q, depth // 2), BF16),
        part_own_f=V((q, depth // 2), F32),
        pre=full,
        values=half,
        weighted=half,
        weight_u=full,
        growth_u=full,
        cumt=V((128, q), F32),
        stept=V((128, q), F32),
        kern=V((heads, q, q), BF16),
        zmask=V((heads, q, q), F32),
        intra=full,
        grad=full,
        gbf=half,
        ggrown=half,
        iprod=full,
        colt=V((128, q), F32),
        fromintra=full,
        dec=V((nz, 128), F32),
        w_s=dma((72,)),
        w_r=dma((72,)),
        grp_s=dma((2 * nx,)),
        grp_r=dma((2 * nx,)),
        core_s=dma((3,)),
        core_r=dma((3,)),
        z_s=dma(((4 * CHUNKS + 2) * nz,)),
        z_r=dma(((4 * CHUNKS + 2) * nz,)),
        y_s=dma(((2 * CHUNKS + 2) * ny,)),
        y_r=dma(((2 * CHUNKS + 2) * ny,)),
        x_s=dma((3 * nx,)),
        x_r=dma((3 * nx,)),
        loc_s=dma((10,)),
        far=pltpu.SemaphoreType.REGULAR((2,)),
    )
    names = NAMES[13:]
    vm = pl.BlockSpec(memory_space=pltpu.VMEM)
    grad_in, grad_bc, grad_dt = pl.pallas_call(
        functools.partial(layer_kernel, nx, ny, nz, straight),
        out_shape=(
            jax.ShapeDtypeStruct((q, depth // 2), BF16),
            jax.ShapeDtypeStruct((few, nstate), F32),
            jax.ShapeDtypeStruct((few, heads), F32),
        ),
        in_specs=[pl.BlockSpec(memory_space=pltpu.HBM)] * 10,
        out_specs=(vm, vm, vm),
        scratch_shapes=[scratch[n] for n in names],
        compiler_params=pltpu.CompilerParams(
            collective_id=0, has_side_effects=True, vmem_limit_bytes=60 * 1024 * 1024
        ),
        name="ternary_layer",
    )(
        layer_in[0],
        out_grad[0],
        w_in,
        w_out,
        w_bc,
        w_dt.T,
        norm_gain[None],
        d_skip[None],
        dt_bias[None],
        a_log[None],
    )
    outs = (grad_in, grad_bc, grad_dt)
    grad_in, grad_bc, grad_dt = pl.pallas_call(
        place_kernel,
        out_shape=tuple(jax.ShapeDtypeStruct(o.shape, o.dtype) for o in outs),
        in_specs=[vm] * 3,
        out_specs=(vm, vm, vm),
        name="place_outputs",
    )(*outs)
    return (grad_in[None], grad_bc, grad_dt)


def solution(mesh):
    in_specs = (
        P("dp", "ctx", None),
        P("dp", "ctx", None),
        P("dp", "tensor"),
        P("dp", "tensor"),
        P("dp", "tensor"),
        P("dp", "tensor"),
        P("tensor"),
        P("tensor"),
        P("tensor"),
        P("tensor"),
    )
    out_specs = (P("dp", "ctx", "tensor"), P(("dp", "ctx"), "tensor"), P(("dp", "ctx"), "tensor"))
    body = functools.partial(shards, (mesh.shape["dp"], mesh.shape["ctx"]))
    return jax.shard_map(body, mesh=mesh, in_specs=in_specs, out_specs=out_specs, check_vma=False)
```

```python
import functools
import types

import jax
import jax.numpy as jnp
from jax import lax
from jax.experimental import pallas as pl
from jax.experimental.pallas import tpu as pltpu
from jax.sharding import PartitionSpec as P

GROUP = 256
CHUNKS = 1
MESH = pl.DeviceIdType.MESH
F32 = jnp.float32
BF16 = jnp.bfloat16
EXACT = lax.Precision.HIGHEST


def dot(a, b, ca=1, cb=0, precision=None):
    return lax.dot_general(
        a, b, (((ca,), (cb,)), ((), ())), precision=precision, preferred_element_type=F32
    )


NAMES = [
    "x_in", "g_in", "win", "wout", "wbc_in", "wdt_in", "gain_in", "skip_in",
    "bias_in", "rate_in", "gin", "gbc", "gdt", "x", "g", "wbc",
    "wdt", "gain", "skip", "bias", "rate", "skip_u", "win_all", "wout_all",
    "wbc_all", "wdt_all", "codes", "sums_own", "sums_all", "bc_own", "bc", "log_own",
    "logs", "loc_own", "loc_all", "ent_own", "held", "term_own", "term_all", "lea_own",
    "leav", "fwd_own", "fwd_all", "bwd_own", "bwd_all", "x_all", "sbc_own", "sbc_all",
    "sdt_own", "sdt_all", "ybc_own", "ybc_all", "ydt_own", "ydt_all", "zg_own", "zg_all",
    "half_own", "half_in", "part_own", "part_in", "part_own_f", "pre", "values", "weighted",
    "weight_u", "growth_u", "cumt", "stept", "kern", "zmask", "intra", "grad",
    "gbf", "ggrown", "iprod", "colt", "fromintra", "dec", "w_s", "w_r",
    "grp_s", "grp_r", "core_s", "core_r", "z_s", "z_r", "y_s", "y_r",
    "x_s", "x_r", "loc_s", "far", "x_turned",
]


def far_first(n):
    return sorted(range(1, n), key=lambda d: -min(d, n - d))


def layer_kernel(nx, ny, nz, straight, *refs):
    R = types.SimpleNamespace(**dict(zip(NAMES, refs, strict=True)))
    q, depth = R.x_in.shape
    rows, units = R.win.shape
    heads = nz
    width = units // heads
    nstate = R.wbc_in.shape[1]
    tile = min(256, units)
    ntile = units // tile
    hpt = tile // width
    ix = lax.axis_index("dp")
    ic = lax.axis_index("ctx")
    it = lax.axis_index("tensor")
    iz = lax.rem(ic, nz)
    iy = ic // nz
    other = 1 - it

    def dev(x=ix, y=iy, z=iz, t=it):
        return (x, y * nz + z, t)

    def remote(src, dst, ssem, rsem, device):
        return pltpu.make_async_remote_copy(
            src_ref=src,
            dst_ref=dst,
            send_sem=ssem,
            recv_sem=rsem,
            device_id=device,
            device_id_type=MESH,
        )

    def xoff(d):
        return lax.rem(ix + d, nx)

    def yoff(d):
        return lax.rem(iy + d, ny)

    def zoff(d):
        return lax.rem(iz + d, nz)

    barrier = pltpu.get_barrier_semaphore()
    count = 0

    for d in (1, nz - 1):
        pl.semaphore_signal(barrier, inc=1, device_id=dev(z=zoff(d)), device_id_type=MESH)
        count += 1
    for d in range(nx):
        for t in (it, other):
            if d == 0 and t is it:
                continue
            pl.semaphore_signal(barrier, inc=1, device_id=dev(x=xoff(d), t=t), device_id_type=MESH)
            count += 1
    for d in range(1, ny):
        pl.semaphore_signal(barrier, inc=1, device_id=dev(y=yoff(d)), device_id_type=MESH)
        count += 1

    loads = [
        pltpu.make_async_copy(src, dst, R.loc_s.at[k])
        for k, (src, dst) in enumerate(
            (
                (R.win, R.win_all.at[ix]),
                (R.wout, R.wout_all.at[ix]),
                (R.wbc_in, R.wbc),
                (R.wdt_in, R.wdt),
                (R.x_in, R.x),
                (R.bias_in, R.bias),
                (R.rate_in, R.rate),
                (R.gain_in, R.gain),
                (R.skip_in, R.skip),
                (R.g_in, R.g),
            )
        )
    ]
    for c in loads:
        c.start()

    def magnitude(ref):
        def one(i, acc):
            piece = jnp.abs(ref[ix, pl.ds(pl.multiple_of(i * 16, 16), 16), :].astype(F32))
            return acc + piece

        total = lax.fori_loop(0, rows // 16, one, jnp.zeros((16, units), F32))
        out = total[:8, :128] + total[8:, :128]
        for c in range(1, units // 128):
            out = out + total[:8, c * 128 : (c + 1) * 128] + total[8:, c * 128 : (c + 1) * 128]
        return out

    for k in range(nx):
        R.wdt_all[k, heads:, :] = jnp.zeros((128 - heads, rows), BF16)
    for c in loads:
        c.wait()
    pl.semaphore_wait(barrier, count)

    links = [0]
    every = []

    def link(src, dst, device):
        k = links[0]
        links[0] += 1
        c = remote(src, dst, R.w_s.at[k], R.w_r.at[k], device)
        every.append(c)
        return c

    class Ring:
        def __init__(self, n, own, place, before, after, right, left):
            self.relay = []
            if n == 2:
                self.first = [link(own(c), place(c), right) for c in range(2)]
                return
            self.first = [
                link(own(0), place(0), right),
                link(own(1), place(1), left),
                link(own(1), place(1), right),
                link(own(0), place(0), left),
            ]
            self.relay = [
                link(before(0), before(0), right),
                link(after(1), after(1), left),
            ]

        def start(self):
            for c in self.first:
                c.start()

        def forward(self):
            for k, c in enumerate(self.relay):
                self.first[k].wait_recv()
                c.start()

        def neighbours(self):
            for c in self.first[2:] if self.relay else self.first:
                c.wait_recv()

        def opposite(self):
            for c in self.relay:
                c.wait_recv()

    def x_ring(view, dst):
        return Ring(
            nx,
            lambda c: view(None, c),
            lambda c: view(dst.at[ix], c),
            lambda c: view(dst.at[xoff(nx - 1)], c),
            lambda c: view(dst.at[xoff(1)], c),
            dev(x=xoff(1)),
            dev(x=xoff(nx - 1)),
        )

    half_units = units // 2

    class Gather:
        def __init__(self, dst, straight):
            share = (rows - straight) // ny

            def part(first, count):
                def view(ref, c):
                    ref = dst.at[ix] if ref is None else ref
                    return ref.at[pl.ds(first, count), pl.ds(c * half_units, half_units)]

                return view

            def quarter(y):
                return part(pl.multiple_of(straight + y * share, 8), share)

            self.xb = x_ring(quarter(iy), dst)
            self.xa = x_ring(part(0, straight), dst)
            self.y = []
            for slot in (xoff(nx - 1), xoff(1), xoff(2)):
                at = dst.at[slot]
                mine = quarter(iy)
                self.y.append(
                    Ring(
                        ny,
                        lambda c, at=at: mine(at, c),
                        lambda c, at=at: mine(at, c),
                        lambda c, at=at: quarter(yoff(ny - 1))(at, c),
                        lambda c, at=at: quarter(yoff(1))(at, c),
                        dev(y=yoff(1)),
                        dev(y=yoff(ny - 1)),
                    )
                )

        def finish(self):
            self.xa.neighbours()
            self.xa.opposite()
            for ring in self.y:
                ring.neighbours()
                ring.opposite()

    by_rows = rows // 2
    ring_bc = x_ring(
        lambda ref, c: (R.wbc if ref is None else ref).at[pl.ds(c * by_rows, by_rows), :], R.wbc_all
    )
    ring_dt = x_ring(
        lambda ref, c: (
            R.wdt.at[:, pl.ds(c * by_rows, by_rows)]
            if ref is None
            else ref.at[pl.ds(0, heads), pl.ds(c * by_rows, by_rows)]
        ),
        R.wdt_all,
    )
    into = Gather(R.win_all, straight[0])
    outof = Gather(R.wout_all, straight[1])

    group = []
    for d in range(nx):
        for k, t in enumerate((it, other)):
            if d == 0 and k == 0:
                continue
            group.append(
                remote(
                    R.sums_own,
                    R.sums_all.at[2 * ix + it],
                    R.grp_s.at[2 * d + k],
                    R.grp_r.at[2 * d + k],
                    dev(x=xoff(d), t=t),
                )
            )

    into.xb.start()
    ring_bc.start()
    ring_dt.start()
    R.sums_own[0:8, :] = magnitude(R.win_all)
    R.sums_own[8:16, :] = magnitude(R.wout_all)
    for c in group:
        c.start()
    R.sums_all[2 * ix + it] = R.sums_own[...]
    R.wbc_all[ix] = R.wbc[...]
    R.wdt_all[ix, 0:heads, :] = R.wdt[...]
    into.xb.forward()
    into.xa.start()
    into.xb.neighbours()
    into.y[0].start()
    into.y[1].start()
    ring_bc.forward()
    ring_dt.forward()
    into.xb.opposite()
    into.y[2].start()
    def farther(r, carry):
        for k, d in enumerate((1, nz - 1)):
            pl.semaphore_signal(R.far.at[k], inc=1, device_id=dev(z=zoff(d)), device_id_type=MESH)
        for k in range(2):
            pl.semaphore_wait(R.far.at[k], 1)
        return carry

    lax.fori_loop(1, nz // 2, farther, 0)
    into.y[0].forward()
    into.xa.forward()
    outof.xb.start()
    outof.xa.start()
    into.y[1].forward()

    for ring in (ring_bc, ring_dt):
        ring.neighbours()
        ring.opposite()
    half_bc = jnp.zeros((q, nstate), F32)
    raw_step = jnp.zeros((q, 128), F32)
    for k in range(nx):
        piece = R.x[:, k * rows : (k + 1) * rows]
        half_bc = half_bc + dot(piece, R.wbc_all[k])
        raw_step = raw_step + dot(piece, R.wdt_all[k], 1, 1)
    R.bc_own[...] = half_bc.astype(BF16)
    share_bc = remote(R.bc_own, R.bc.at[it], R.core_s.at[0], R.core_r.at[0], dev(t=other))
    share_bc.start()
    R.bc[it] = R.bc_own[...]

    def lane_pad(v):
        return jnp.concatenate([v, jnp.zeros((1, 128 - heads), F32)], axis=1)

    raw_step = raw_step + lane_pad(R.bias[...])
    rate = -jnp.exp(lane_pad(R.rate[...]))
    step = jnp.maximum(raw_step, 0.0) + jnp.log1p(jnp.exp(-jnp.abs(raw_step)))
    ri = lax.broadcasted_iota(jnp.int32, (q, q), 0)
    ci = lax.broadcasted_iota(jnp.int32, (q, q), 1)
    causal = ri >= ci
    lower = jnp.where(causal, 1.0, 0.0).astype(F32)
    upper = jnp.where(ci >= ri, 1.0, 0.0).astype(F32)
    cum = dot(lower, step * rate, precision=EXACT)
    block_log = cum[q - 1 : q, :]
    R.log_own[...] = block_log

    def log_copy(d):
        return remote(
            R.log_own,
            R.logs.at[iz],
            R.z_s.at[4 * CHUNKS * nz + d],
            R.z_r.at[4 * CHUNKS * nz + d],
            dev(z=zoff(d)),
        )

    def log_start(d, carry):
        log_copy(d).start()
        return carry

    def log_wait(d, carry):
        log_copy(d).wait_recv()
        return carry

    def log_drain(d, carry):
        log_copy(d).wait_send()
        return carry

    lax.fori_loop(1, nz, log_start, 0)
    R.logs[iz] = R.log_own[...]
    into.y[2].forward()
    fade = jnp.exp(block_log - cum)
    weight = fade * step
    growth = jnp.exp(cum)
    R.cumt[...] = cum.T
    R.stept[...] = step.T
    eh = lax.broadcasted_iota(jnp.int32, (128, units), 0)
    eu = lax.broadcasted_iota(jnp.int32, (128, units), 1)
    expand = jnp.where(eu // width == eh, 1.0, 0.0).astype(BF16)

    def split(v):
        high = v.astype(BF16)
        return high, (v - high.astype(F32)).astype(BF16)

    def widen(v):
        high, rest = split(v)
        return dot(high, expand) + dot(rest, expand)

    R.weight_u[...] = widen(weight)
    R.growth_u[...] = widen(growth)
    R.skip_u[...] = dot(
        jnp.broadcast_to(lane_pad(R.skip[...]), (8, 128)), expand.astype(F32), precision=EXACT
    )

    for c in group:
        c.wait_recv()
    total = R.sums_all[0]
    for k in range(1, 2 * nx):
        total = total + R.sums_all[k]
    entries = 2.0 * nx * rows * units
    scale_in = jnp.sum(total[0:8, :]) / entries
    scale_out = jnp.sum(total[8:16, :]) / entries

    def ternary(w, scale):
        w = w.astype(F32)
        sign = jnp.where(w > 0.0, 1.0, -1.0)
        return jnp.where(jnp.abs(w) > 0.5 * scale, sign, 0.0).astype(BF16)

    share_bc.wait_recv()
    b_proj, c_proj = R.bc[0], R.bc[1]

    chunk = width // CHUNKS
    spans = [pl.ds(c * chunk, chunk) for c in range(CHUNKS)]

    def z_copy(pair, base, source, to, cell=None):
        own, all_ = pair
        src = own.at[to] if cell is None else own.at[to, spans[cell]]
        dst = all_.at[source] if cell is None else all_.at[source, spans[cell]]
        at = (base + (cell or 0)) * nz + lax.rem(to - source + nz, nz)
        return remote(src, dst, R.z_s.at[at], R.z_r.at[at], dev(z=to))

    def z_send(pair, base, to, near, cell):
        if not near:
            z_copy(pair, base, iz, to, cell).start()
            return

        @pl.when(to != iz)
        def _():
            z_copy(pair, base, iz, to, cell).start()

        @pl.when(to == iz)
        def _():
            pair[1][iz, spans[cell]] = pair[0][iz, spans[cell]]

    def z_wait_from(pair, base, source, near, cell):
        own, all_ = pair
        at = (base + cell) * nz + lax.rem(iz - source + nz, nz)
        copy = remote(
            own.at[source, spans[cell]],
            all_.at[source, spans[cell]],
            R.z_s.at[at],
            R.z_r.at[at],
            dev(z=source),
        )
        if not near:
            copy.wait_recv()
            return

        @pl.when(source != iz)
        def _():
            copy.wait_recv()

    def z_wait(pair, base, cell=None):
        def one(d, carry):
            z_copy(pair, base, iz, zoff(d), cell).wait_recv()
            return carry

        lax.fori_loop(1, nz, one, 0, unroll=True)

    def z_drain(pair, base, cell=None):
        def one(d, carry):
            z_copy(pair, base, iz, zoff(d), cell).wait_send()
            return carry

        lax.fori_loop(1, nz, one, 0)

    locs = (R.loc_own, R.loc_all)
    ents = (R.ent_own, R.held)
    terms = (R.term_own, R.term_all)
    leas = (R.lea_own, R.leav)
    at_loc, at_ent, at_term, at_lea = (CHUNKS * e for e in range(4))
    at_log, at_zg = 4 * CHUNKS, 4 * CHUNKS + 1

    offs = sorted(range(ntile), key=lambda d: -min(d, ntile - d))
    own_tile = iz // hpt

    def tiles():
        for off in offs:
            t = lax.rem(own_tile + off, ntile)
            yield t, pl.ds(pl.multiple_of(t * tile, tile), tile), off == 0

    outof.xb.forward()
    outof.xb.neighbours()
    outof.y[0].start()
    outof.y[1].start()
    into.finish()
    for t, cols, near in tiles():
        acc = jnp.zeros((q, tile), F32)
        for k in range(nx):
            code = ternary(R.win_all[k, :, cols], scale_in)
            R.codes[k, :, cols] = code
            acc = acc + dot(R.x[:, k * rows : (k + 1) * rows], code)
        v = scale_in * acc
        R.pre[:, cols] = v
        val = (v * lax.logistic(v)).astype(BF16)
        R.values[:, cols] = val
        wv = (val.astype(F32) * R.weight_u[:, cols]).astype(BF16)
        R.weighted[:, cols] = wv
        R.loc_own[pl.ds(t * hpt, hpt)] = (
            dot(wv, b_proj, 0, 0).astype(BF16).reshape(hpt, width, nstate)
        )
        for i in range(hpt):
            z_send(locs, at_loc, t * hpt + lax.rem(iz + i, hpt), near, 0)
    for cell in range(1, CHUNKS):
        for t, cols, near in tiles():
            for i in range(hpt):
                z_send(locs, at_loc, t * hpt + lax.rem(iz + i, hpt), near, cell)

    gram = dot(c_proj, b_proj, 1, 1)
    lane = ci
    left_half = lax.broadcasted_iota(jnp.int32, (q, 2 * width), 1) < width
    zero_pair = jnp.zeros((q, 2 * width), BF16)

    def pick(s, pair):
        return jnp.where(left_half, pair, zero_pair) if s == 0 else jnp.where(left_half, zero_pair, pair)

    def inside(p, carry):
        cols = pl.ds(pl.multiple_of(p * 2 * width, 2 * width), 2 * width)
        pair = R.values[:, cols]
        acc = jnp.zeros((q, 2 * width), F32)
        for s in range(2):
            h = 2 * p + s
            col = jnp.sum(jnp.where(lane == h, cum, 0.0), axis=1, keepdims=True)
            row = R.cumt[pl.ds(h, 1), :]
            mask = jnp.exp(jnp.where(causal, col - row, -jnp.inf)) * R.stept[pl.ds(h, 1), :]
            R.zmask[h] = mask
            kb = (gram * mask).astype(BF16)
            R.kern[h] = kb
            acc = acc + dot(kb, pick(s, pair))
        R.intra[:, cols] = acc
        return carry

    outof.xb.opposite()
    outof.y[2].start()
    outof.y[0].forward()
    outof.y[1].forward()
    lax.fori_loop(0, heads // 2, inside, 0)
    outof.xa.forward()
    outof.y[2].forward()

    lax.fori_loop(1, nz, log_wait, 0, unroll=True)
    log_rows = R.logs[...].reshape(nz, 128)
    lane_z = lax.broadcasted_iota(jnp.int32, (nz, 128), 1)
    log_col = jnp.sum(jnp.where(lane_z == iz, log_rows, 0.0), axis=1, keepdims=True)
    R.dec[...] = jnp.broadcast_to(jnp.exp(log_col), (nz, 128))
    row_decay = jnp.broadcast_to(jnp.exp(jnp.sum(log_col)), (16, nstate))
    high, rest = split(row_decay)
    decay_rows = jnp.where(
        lax.broadcasted_iota(jnp.int32, (16, nstate), 0) < 8, high.astype(F32), rest.astype(F32)
    ).astype(BF16)

    def scan(arrived, own, total, totals, at, forward):
        copies = []
        for cell in range(CHUNKS):
            rows_of = spans[cell]

            def step_of(i, state):
                k = i if forward else nz - 1 - i
                return R.dec[pl.ds(k, 1), :] * state + arrived[1][k, rows_of].astype(F32)

            empty = jnp.zeros((chunk, nstate), F32)
            z_wait(arrived, at[0], cell)
            total[cell, 0:chunk, :] = lax.fori_loop(0, nz, step_of, empty, unroll=True).astype(BF16)
            total[cell, chunk:, :] = decay_rows
            mine = []
            for d in far_first(ny):
                sem = (at[1] + cell) * ny + d
                mine.append(
                    remote(
                        total.at[cell],
                        totals.at[cell, iy],
                        R.y_s.at[sem],
                        R.y_r.at[sem],
                        dev(y=yoff(d)),
                    )
                )
            for c in mine:
                c.start()
            totals[cell, iy] = total[cell]
            for c in mine:
                c.wait_recv()
            copies += mine
            state = empty
            for k in range(ny) if forward else range(ny - 1, -1, -1):
                tail = totals[cell, k, chunk:, :].astype(F32)
                factor = tail[0:1, :] + tail[8:9, :]
                grown = factor * state + totals[cell, k, 0:chunk, :].astype(F32)
                state = jnp.where(k < iy if forward else k > iy, grown, state)

            def emit(i, state):
                k = i if forward else nz - 1 - i
                own[0][k, rows_of] = state.astype(BF16)
                return step_of(i, state)

            lax.fori_loop(0, nz, emit, state, unroll=True)
            for off in offs:
                t = lax.rem(own_tile - off + ntile, ntile)
                for i in range(hpt):
                    z_send(own, at[2], t * hpt + lax.rem(iz + i, hpt), off == 0, cell)
        return copies

    y_fwd = scan(locs, ents, R.fwd_own, R.fwd_all, (at_loc, 0, at_ent), True)

    outof.finish()

    def project_out(j, carry):
        cols = pl.ds(pl.multiple_of(j * tile, tile), tile)
        acc = jnp.zeros((q, tile), F32)
        for k in range(nx):
            acc = acc + dot(
                R.g[:, k * rows : (k + 1) * rows], ternary(R.wout_all[k, :, cols], scale_out)
            )
        R.grad[:, cols] = scale_out * acc * R.gain[:, cols]
        return carry

    lax.fori_loop(0, ntile, project_out, 0)

    for t, cols, near in tiles():
        for i in range(hpt):
            for cell in range(CHUNKS):
                z_wait_from(ents, at_ent, t * hpt + i, near, cell)
        hb = R.held[pl.ds(t * hpt, hpt)].reshape(tile, nstate)
        grow = R.growth_u[:, cols]
        inter = grow * dot(c_proj, hb, 1, 1)
        output = R.intra[:, cols] + inter + R.skip_u[0:1, cols] * R.values[:, cols].astype(F32)
        scaled = R.grad[:, cols]
        pieces = []
        for g in range(tile // GROUP):
            sl = slice(g * GROUP, (g + 1) * GROUP)
            o, s = output[:, sl], scaled[:, sl]
            inverse = lax.rsqrt(jnp.mean(o * o, axis=1, keepdims=True) + 1e-05)
            mixed = jnp.mean(s * o, axis=1, keepdims=True)
            pieces.append(inverse * (s - o * (inverse * inverse) * mixed))
        grad_y = jnp.concatenate(pieces, axis=1) if len(pieces) > 1 else pieces[0]
        grown = (grad_y * grow).astype(BF16)
        R.term_own[pl.ds(t * hpt, hpt)] = (
            dot(grown, c_proj, 0, 0).astype(BF16).reshape(hpt, width, nstate)
        )
        for i in range(hpt):
            z_send(terms, at_term, t * hpt + lax.rem(iz + i, hpt), near, 0)
        R.grad[:, cols] = grad_y
        R.gbf[:, cols] = grad_y.astype(BF16)
        R.ggrown[:, cols] = grown
        R.iprod[:, cols] = grad_y * inter

    for cell in range(1, CHUNKS):
        for t, cols, near in tiles():
            for i in range(hpt):
                z_send(terms, at_term, t * hpt + lax.rem(iz + i, hpt), near, cell)

    x_copies = [
        remote(
            R.x.at[:, pl.ds(pl.multiple_of(xoff(d) * rows, rows), rows)],
            R.x_all.at[ix],
            R.x_s.at[d],
            R.x_r.at[d],
            dev(x=xoff(d)),
        )
        for d in range(1, nx)
    ]
    for c in x_copies:
        c.start()
    R.x_all[ix] = R.x[:, pl.ds(pl.multiple_of(ix * rows, rows), rows)]

    def head_sum(v, e=expand):
        high, rest = split(v)
        return dot(high, e, 1, 1) + dot(rest, e, 1, 1)

    R.colt[...] = jnp.zeros((128, q), F32)

    def inside_back(p, carry):
        zsum, rsum = carry
        cols = pl.ds(pl.multiple_of(p * 2 * width, 2 * width), 2 * width)
        pair = R.values[:, cols]
        gpair = R.gbf[:, cols]
        acc = jnp.zeros((q, 2 * width), F32)
        for s in range(2):
            h = 2 * p + s
            picked = pick(s, gpair)
            z = dot(picked, pair, 1, 1) * R.zmask[h]
            zsum = zsum + z
            product = z * gram
            rs = jnp.sum(product, axis=1, keepdims=True)
            rsum = jnp.where(lane == h, rs, rsum)
            R.colt[pl.ds(h, 1), :] = jnp.sum(product, axis=0, keepdims=True)
            acc = acc + dot(R.kern[h], picked, 0, 0)
        R.fromintra[:, cols] = acc + R.skip_u[0:1, cols] * R.grad[:, cols]
        return (zsum, rsum)

    zero_q = jnp.zeros((q, q), F32)
    zsum, row_sums = lax.fori_loop(0, heads // 2, inside_back, (zero_q, zero_q))
    inter_sum = head_sum(R.iprod[...])
    col_sums = R.colt[...].T
    zsum = zsum.astype(BF16)
    grad_c = dot(zsum, b_proj) + dot(R.ggrown[...], R.held[...].reshape(units, nstate))
    grad_b = dot(zsum, c_proj, 0, 0)

    y_bwd = scan(terms, leas, R.bwd_own, R.bwd_all, (at_term, CHUNKS, at_lea), False)

    for c in x_copies:
        c.wait_recv()
    for k in range(nx):
        R.x_turned[k] = R.x_all[k].astype(F32).T.astype(BF16)

    grad_weight = jnp.zeros((q, 128), F32)
    state_dot = jnp.zeros((8, 128), F32)
    ones = jnp.ones((8, nstate), BF16)
    tile_head = lax.broadcasted_iota(jnp.int32, (128, tile), 0)
    tile_unit = lax.broadcasted_iota(jnp.int32, (128, tile), 1)
    for t, cols, near in tiles():
        for i in range(hpt):
            for cell in range(CHUNKS):
                z_wait_from(leas, at_lea, t * hpt + i, near, cell)
        lb = R.leav[pl.ds(t * hpt, hpt)].reshape(tile, nstate)
        hb = R.held[pl.ds(t * hpt, hpt)].reshape(tile, nstate)
        e = jnp.where(tile_unit // width + t * hpt == tile_head, 1.0, 0.0).astype(BF16)
        grad_b = grad_b + dot(R.weighted[:, cols], lb)
        gw = dot(b_proj, lb, 1, 1)
        grad_weight = grad_weight + head_sum(gw * R.values[:, cols].astype(F32), e)
        high, rest = split(lb.astype(F32) * hb.astype(F32))
        state_dot = state_dot + head_sum(dot(ones, high, 1, 1) + dot(ones, rest, 1, 1), e)
        R.iprod[:, cols] = gw

    R.half_own[...] = jnp.where(it == 0, grad_c, grad_b).astype(BF16)
    share_half = remote(R.half_own, R.half_in, R.core_s.at[1], R.core_r.at[1], dev(t=other))
    share_half.start()
    mine = jnp.where(it == 0, grad_b, grad_c)

    gw_w = grad_weight * weight
    grad_log = jnp.sum(gw_w, axis=0, keepdims=True) + jnp.exp(block_log) * state_dot[0:1, :]
    grad_cum = inter_sum + row_sums - col_sums - gw_w
    grad_cum = grad_cum + jnp.where(ri == q - 1, grad_log, 0.0)
    grad_rate = dot(upper, grad_cum, precision=EXACT)
    grad_step = col_sums / step + grad_weight * fade + rate * grad_rate
    grad_raw = jnp.where(lane < heads, grad_step * lax.logistic(raw_step), 0.0)
    R.sdt_own[...] = grad_raw.T[0:heads, :].astype(BF16)
    send_dt = grad_raw.astype(BF16)

    share_half.wait_recv()
    R.sbc_own[...] = (mine + R.half_in[...].astype(F32)).astype(BF16)
    s_copies = []
    for d in far_first(nx):
        for k, (own, all_) in enumerate(((R.sbc_own, R.sbc_all), (R.sdt_own, R.sdt_all))):
            at = nx * (k + 1) + d
            s_copies.append(
                remote(own, all_.at[ix], R.x_s.at[at], R.x_r.at[at], dev(x=xoff(d)))
            )
    for c in s_copies:
        c.start()
    R.sbc_all[ix] = R.sbc_own[...]
    R.sdt_all[ix] = R.sdt_own[...]

    def silu_back(j, carry):
        cols = pl.ds(pl.multiple_of(j * tile, tile), tile)
        grad_values = R.fromintra[:, cols] + R.iprod[:, cols] * R.weight_u[:, cols]
        v = R.pre[:, cols]
        sg = lax.logistic(v)
        R.gbf[:, cols] = (scale_in * (grad_values * sg * (1.0 + v * (1.0 - sg)))).astype(BF16)
        return carry

    lax.fori_loop(0, ntile, silu_back, 0)
    per = nx // 2

    def partial_in(side, j):
        k = side * per + j
        return (
            dot(R.gbf[...], R.codes[k], 1, 1)
            + dot(R.sbc_own[...], R.wbc_all[k], 1, 1)
            + dot(send_dt, R.wdt_all[k])
        )

    for j in range(per):
        R.part_own[:, j * rows : (j + 1) * rows] = partial_in(other, j).astype(BF16)
    share_part = remote(R.part_own, R.part_in, R.core_s.at[2], R.core_r.at[2], dev(t=other))
    share_part.start()

    for c in s_copies:
        c.wait_recv()
    grad_w = jnp.zeros((rows, nstate), F32)
    grad_t = jnp.zeros((heads, rows), F32)
    for k in range(nx):
        grad_w = grad_w + dot(R.x_turned[k], R.sbc_all[k])
        grad_t = grad_t + dot(R.sdt_all[k], R.x_all[k])
    yrows = rows // ny
    R.ybc_own[...] = grad_w.astype(BF16).reshape(ny, yrows, nstate)
    for k in range(ny):
        R.ydt_own[k] = grad_t[:, k * yrows : (k + 1) * yrows].astype(BF16)
    yg_copies = []
    for d in far_first(ny):
        for k, (own, all_) in enumerate(((R.ybc_own, R.ybc_all), (R.ydt_own, R.ydt_all))):
            at = ny * (k + 2 * CHUNKS) + d
            yg_copies.append(
                remote(own.at[yoff(d)], all_.at[iy], R.y_s.at[at], R.y_r.at[at], dev(y=yoff(d)))
            )
    for c in yg_copies:
        c.start()
    R.ybc_all[iy] = R.ybc_own[iy]
    R.ydt_all[iy] = R.ydt_own[iy]

    for j in range(per):
        R.part_own_f[:, j * rows : (j + 1) * rows] = partial_in(it, j)

    for c in yg_copies:
        c.wait_recv()
    ysum = R.ybc_all[0].astype(F32)
    tsum = R.ydt_all[0].astype(F32)
    for k in range(1, ny):
        ysum = ysum + R.ybc_all[k].astype(F32)
        tsum = tsum + R.ydt_all[k].astype(F32)
    tsum = jnp.concatenate([tsum, jnp.zeros((128 - heads, yrows), F32)], axis=0).T
    few = yrows // nz
    for k in range(nz):
        sl = slice(k * few, (k + 1) * few)
        R.zg_own[k] = jnp.concatenate([ysum[sl], tsum[sl]], axis=0).astype(BF16)
    for d in far_first(nz):
        z_copy((R.zg_own, R.zg_all), at_zg, iz, zoff(d)).start()
    R.zg_all[iz] = R.zg_own[iz]

    share_part.wait_recv()
    R.gin[...] = (R.part_own_f[...] + R.part_in[...].astype(F32)).astype(BF16)

    for c in every + group + [share_bc, share_half, share_part]:
        c.wait_send()
    for c in y_fwd + y_bwd + yg_copies + x_copies + s_copies:
        c.wait_send()
    for cell in range(CHUNKS):
        z_drain(locs, at_loc, cell)
        z_drain(ents, at_ent, cell)
        z_drain(terms, at_term, cell)
        z_drain(leas, at_lea, cell)
    lax.fori_loop(1, nz, log_drain, 0)

    z_wait((R.zg_own, R.zg_all), at_zg)
    gsum = R.zg_all[0].astype(F32)
    for k in range(1, nz):
        gsum = gsum + R.zg_all[k].astype(F32)
    norm = (q * nx * ny * nz) ** -0.5
    R.gbc[...] = gsum[:few, :] * norm
    R.gdt[...] = gsum[few:, :heads] * norm

    z_drain((R.zg_own, R.zg_all), at_zg)


def place_kernel(a, b, c, a_out, b_out, c_out):
    a_out[...] = a[...]
    b_out[...] = b[...]
    c_out[...] = c[...]


def shards(mesh_shape, layer_in, out_grad, w_in, w_out, w_bc, w_dt, dt_bias, a_log, d_skip, norm_gain):
    nx, nc = mesh_shape
    heads = a_log.shape[0]
    nz = heads
    ny = nc // nz
    q, depth = layer_in.shape[1:]
    rows, units = w_in.shape
    nstate = w_bc.shape[1]
    width = units // heads
    yrows = rows // ny
    few = yrows // nz
    straight = [part * rows // 16 // (8 * ny) * 8 * ny for part in (6, 6)]
    V = pltpu.VMEM
    dma = pltpu.SemaphoreType.DMA
    state = V((nz, width, nstate), BF16)
    full = V((q, units), F32)
    half = V((q, units), BF16)
    total = V((CHUNKS, width // CHUNKS + 16, nstate), BF16)
    totals = V((CHUNKS, ny, width // CHUNKS + 16, nstate), BF16)
    scratch = dict(
        x=V((q, depth), BF16),
        g=V((q, depth), BF16),
        wbc=V((rows, nstate), BF16),
        wdt=V((heads, rows), BF16),
        gain=V((1, units), F32),
        skip=V((1, heads), F32),
        bias=V((1, heads), F32),
        rate=V((1, heads), F32),
        skip_u=V((8, units), F32),
        win_all=V((nx, rows, units), BF16),
        wout_all=V((nx, rows, units), BF16),
        wbc_all=V((nx, rows, nstate), BF16),
        wdt_all=V((nx, 128, rows), BF16),
        codes=V((nx, rows, units), BF16),
        sums_own=V((16, 128), F32),
        sums_all=V((2 * nx, 16, 128), F32),
        bc_own=V((q, nstate), BF16),
        bc=V((2, q, nstate), BF16),
        log_own=V((1, 128), F32),
        logs=V((nz, 1, 128), F32),
        loc_own=state,
        loc_all=state,
        ent_own=state,
        held=state,
        term_own=state,
        term_all=state,
        lea_own=state,
        leav=state,
        fwd_own=total,
        fwd_all=totals,
        bwd_own=total,
        bwd_all=totals,
        x_all=V((nx, q, rows), BF16),
        x_turned=V((nx, rows, q), BF16),
        sbc_own=V((q, nstate), BF16),
        sbc_all=V((nx, q, nstate), BF16),
        sdt_own=V((heads, q), BF16),
        sdt_all=V((nx, heads, q), BF16),
        ybc_own=V((ny, yrows, nstate), BF16),
        ybc_all=V((ny, yrows, nstate), BF16),
        ydt_own=V((ny, heads, yrows), BF16),
        ydt_all=V((ny, heads, yrows), BF16),
        zg_own=V((nz, 2 * few, nstate), BF16),
        zg_all=V((nz, 2 * few, nstate), BF16),
        half_own=V((q, nstate), BF16),
        half_in=V((q, nstate), BF16),
        part_own=V((q, depth // 2), BF16),
        part_in=V((q, depth // 2), BF16),
        part_own_f=V((q, depth // 2), F32),
        pre=full,
        values=half,
        weighted=half,
        weight_u=full,
        growth_u=full,
        cumt=V((128, q), F32),
        stept=V((128, q), F32),
        kern=V((heads, q, q), BF16),
        zmask=V((heads, q, q), F32),
        intra=full,
        grad=full,
        gbf=half,
        ggrown=half,
        iprod=full,
        colt=V((128, q), F32),
        fromintra=full,
        dec=V((nz, 128), F32),
        w_s=dma((72,)),
        w_r=dma((72,)),
        grp_s=dma((2 * nx,)),
        grp_r=dma((2 * nx,)),
        core_s=dma((3,)),
        core_r=dma((3,)),
        z_s=dma(((4 * CHUNKS + 2) * nz,)),
        z_r=dma(((4 * CHUNKS + 2) * nz,)),
        y_s=dma(((2 * CHUNKS + 2) * ny,)),
        y_r=dma(((2 * CHUNKS + 2) * ny,)),
        x_s=dma((3 * nx,)),
        x_r=dma((3 * nx,)),
        loc_s=dma((10,)),
        far=pltpu.SemaphoreType.REGULAR((2,)),
    )
    names = NAMES[13:]
    vm = pl.BlockSpec(memory_space=pltpu.VMEM)
    grad_in, grad_bc, grad_dt = pl.pallas_call(
        functools.partial(layer_kernel, nx, ny, nz, straight),
        out_shape=(
            jax.ShapeDtypeStruct((q, depth // 2), BF16),
            jax.ShapeDtypeStruct((few, nstate), F32),
            jax.ShapeDtypeStruct((few, heads), F32),
        ),
        in_specs=[pl.BlockSpec(memory_space=pltpu.HBM)] * 10,
        out_specs=(vm, vm, vm),
        scratch_shapes=[scratch[n] for n in names],
        compiler_params=pltpu.CompilerParams(
            collective_id=0, has_side_effects=True, vmem_limit_bytes=60 * 1024 * 1024
        ),
        name="ternary_layer",
    )(
        layer_in[0],
        out_grad[0],
        w_in,
        w_out,
        w_bc,
        w_dt.T,
        norm_gain[None],
        d_skip[None],
        dt_bias[None],
        a_log[None],
    )
    outs = (grad_in, grad_bc, grad_dt)
    grad_in, grad_bc, grad_dt = pl.pallas_call(
        place_kernel,
        out_shape=tuple(jax.ShapeDtypeStruct(o.shape, o.dtype) for o in outs),
        in_specs=[vm] * 3,
        out_specs=(vm, vm, vm),
        name="place_outputs",
    )(*outs)
    return (grad_in[None], grad_bc, grad_dt)


def solution(mesh):
    in_specs = (
        P("dp", "ctx", None),
        P("dp", "ctx", None),
        P("dp", "tensor"),
        P("dp", "tensor"),
        P("dp", "tensor"),
        P("dp", "tensor"),
        P("tensor"),
        P("tensor"),
        P("tensor"),
        P("tensor"),
    )
    out_specs = (P("dp", "ctx", "tensor"), P(("dp", "ctx"), "tensor"), P(("dp", "ctx"), "tensor"))
    body = functools.partial(shards, (mesh.shape["dp"], mesh.shape["ctx"]))
    return jax.shard_map(body, mesh=mesh, in_specs=in_specs, out_specs=out_specs, check_vma=False)
```
